512 devices in a mesh: chan: 16 (over y_lo, x, core), space: 32 (over z, y_hi).
Axes of the slice: x: 4, y: 8 (y_hi: 4, y_lo: 2; y = y_hi * 2 + y_lo), z: 8, core: 2. Of those that a mesh axis runs over, the one named last changes fastest.
Arguments:
- fields: bfloat16 [1, 20, 512, 1024], P(None, None, 'chan', 'space'), may hold values from -6 to 6
- stem_weight: bfloat16 [3, 3, 20, 32], replicated, may hold values from -0.4375 to 0.4375
- stem_bias: float32 [32], replicated, may hold values from -3 to 3
- embed_weight: bfloat16 [7, 7, 32, 1024], P(None, None, None, 'chan'), may hold values from -0.4 to 0.4
- embed_bias: float32 [1024], replicated, may hold values from -3 to 3
- norm_gain: float32 [1024], replicated, may hold values from 0.5 to 1.5
- norm_bias: float32 [1024], replicated, may hold values from -3 to 3
- mix_in: bfloat16 [32768, 1024], P('space', 'chan'), may hold values from -0.03125 to 0.03125
- mix_in_bias: float32 [1024], replicated, may hold values from -3 to 3
- mix_out: bfloat16 [1024, 32768], P('chan', 'space'), may hold values from -0.1875 to 0.1875
- mix_out_bias: float32 [32768], P('space'), may hold values from -3 to 3
Outputs:
- mixed: bfloat16 [1, 1024, 32768], P(None, 'chan', 'space')
The draws below stay inside these ranges and needn't reach their ends.
All inputs are finite; a program needn't handle non-finite values.
Results may differ from the reference program's by a relative error of at most 0.013.
Values may be sent and summed in bfloat16 or wider, within the bound.
A program may use at most 64 MiB of HBM per device.

```python
import jax
import jax.numpy as jnp
from jax import lax

SAMPLES = 1
HEIGHT = 512
GRID = 1024
VARS = 20
STEM = 32
D = 1024
HID = 1024
TOKENS = 32768


def draw_embed_weight(key, part):
    base_key, scale_key = jax.random.split(jax.random.fold_in(key, 11), 2)
    position = jnp.arange(D, dtype=jnp.float32) / (D - 1)
    jitter = jax.random.uniform(scale_key, (D,), jnp.float32, 0.8, 1.25)
    column = jnp.exp(jnp.log(3.0) * position) * jitter * (49.0 * STEM) ** (-0.5)
    entries = jnp.clip(jax.random.normal(base_key, (7, 7, STEM, D), jnp.float32), -4.0, 4.0)
    return (entries * column[None, None, None, :]).astype(jnp.bfloat16)


def steps_of(own_key, dims, cuts, smallest, high):
    factor_of, own = 1.0, jax.random.fold_in(own_key, 6)
    for dim, shards_of in cuts:
        steps = jnp.exp(jax.random.uniform(jax.random.fold_in(own, dim), (shards_of,), jnp.float32, smallest / len(cuts), high / len(cuts)))
        factor_of = factor_of * jnp.repeat(steps, dims[dim] // shards_of).reshape([-1 if axis == dim else 1 for axis in range(len(dims))])
    return factor_of


def centred(rng, shape, deviation, reach, cuts=(), held_as=jnp.bfloat16):
    drawn = jax.random.normal(rng, shape, jnp.float32) * deviation
    if len(cuts) > 0:
        drawn = steps_of(rng, shape, cuts, -0.22, 0.18) * drawn
    return jnp.clip(drawn, min=-reach, max=reach).astype(held_as)


def setup_inputs(seed: int = 0) -> dict:
    key_of = jax.random.split(jax.random.key(seed), 12)
    fields = centred(key_of[0], (SAMPLES, VARS, HEIGHT, GRID), 1.0, 6.0, ((2, 16), (3, 32)))
    stem_weight = centred(key_of[1], (3, 3, VARS, STEM), (9 * VARS) ** -0.5, 0.4375)
    stem_bias = centred(key_of[2], (STEM,), 0.5, 3.0, (), jnp.float32)
    embed_weight = draw_embed_weight(jax.random.fold_in(key_of[11], 71), 0)
    embed_bias = centred(key_of[4], (D,), 0.5, 3.0, (), jnp.float32)
    norm_gain = jnp.clip(1.0 + 0.1 * jax.random.normal(key_of[5], (D,), jnp.float32), 0.5, 1.5)
    norm_bias = centred(key_of[6], (D,), 0.5, 3.0, (), jnp.float32)
    mix_in = centred(key_of[7], (TOKENS, HID), TOKENS ** -0.5, 0.03125, ((0, 32), (1, 16)))
    mix_in_bias = centred(key_of[8], (HID,), 0.5, 3.0, (), jnp.float32)
    mix_out = centred(key_of[9], (HID, TOKENS), HID ** -0.5, 0.1875, ((0, 16), (1, 32)))
    mix_out_bias = centred(key_of[10], (TOKENS,), 0.5, 3.0, ((0, 32),), jnp.float32)
    return dict(fields=fields, stem_weight=stem_weight, stem_bias=stem_bias, embed_weight=embed_weight, embed_bias=embed_bias, norm_gain=norm_gain, norm_bias=norm_bias, mix_in=mix_in, mix_in_bias=mix_in_bias, mix_out=mix_out, mix_out_bias=mix_out_bias)


def convolve(inputs, filters, stride, padding):
    return lax.conv_general_dilated(inputs, filters, (stride, stride), padding, dimension_numbers=('NCHW', 'HWIO', 'NCHW'), preferred_element_type=jnp.float32)

def reference(fields, stem_weight, stem_bias, embed_weight, embed_bias, norm_gain, norm_bias, mix_in, mix_in_bias, mix_out, mix_out_bias):
    stem_out = convolve(fields, stem_weight, 1, ((1, 1), (1, 1))) + stem_bias[None, :, None, None]
    stem_out = jax.nn.gelu(stem_out, approximate=False).astype(jnp.bfloat16)
    embedded = convolve(stem_out, embed_weight, 4, ((3, 3), (3, 3))) + embed_bias[None, :, None, None]
    embedded = embedded.astype(jnp.bfloat16)
    values = embedded.astype(jnp.float32)
    average = lax.optimization_barrier(jnp.mean(values, axis=1, keepdims=True))
    variance = lax.optimization_barrier(jnp.mean(values * values, axis=1, keepdims=True)) - average * average
    normed = (values - average) * lax.rsqrt(variance + 1e-05) * norm_gain[None, :, None, None] + norm_bias[None, :, None, None]
    normed = normed.astype(jnp.bfloat16)
    batch = embedded.shape[0]
    width = embedded.shape[1]
    token_rows = jnp.transpose(normed, (0, 1, 3, 2)).reshape(batch * width, -1)
    residual = jnp.transpose(embedded, (0, 1, 3, 2)).reshape(batch * width, -1)
    hidden = jnp.dot(token_rows, mix_in, preferred_element_type=jnp.float32) + mix_in_bias[None, :]
    activated = jax.nn.gelu(hidden, approximate=False).astype(jnp.bfloat16)
    output = jnp.dot(activated, mix_out, preferred_element_type=jnp.float32) + mix_out_bias[None, :]
    output = output + residual.astype(jnp.float32)
    return output.astype(jnp.bfloat16).reshape(batch, width, -1)
```

```python
import functools

import jax
import jax.numpy as jnp
from jax import lax
from jax.experimental import pallas as pl
from jax.experimental.pallas import tpu as pltpu
from jax.sharding import PartitionSpec as P

MESH = pl.DeviceIdType.MESH
CHIPS = 8
SPACE = 32
F32 = jnp.float32
BF16 = jnp.bfloat16


def gelu(x):
    return 0.5 * x * (1.0 + lax.erf(x * 0.7071067811865476))


def kernel(
    t1_ref,
    tw_ref,
    sb_ref,
    w_ref,
    eb_ref,
    gn_ref,
    nb_ref,
    mi_ref,
    mb_ref,
    mo_ref,
    ob_ref,
    out_ref,
    aext,
    gc,
    rv,
    rh,
    rd,
    xall,
    wall,
    eh,
    st,
    mi_all,
    mo_all,
    hs,
    rs,
    act,
    po,
    pr,
    halo_send,
    halo_recv,
    send,
    recv,
    local,
):
    c, s = lax.axis_index("chan"), lax.axis_index("space")
    k, core = c // 2, c % 2
    other = 1 - core
    partner = (2 * k + other, s)
    right, left = (s + 1) % SPACE, (s + SPACE - 1) % SPACE
    side = jnp.where(core == 0, left, right)

    def remote(src, dst, ssem, rsem, to):
        copy = pltpu.make_async_remote_copy(
            src_ref=src, dst_ref=dst, send_sem=ssem, recv_sem=rsem, device_id=to, device_id_type=MESH
        )
        copy.start()

    def wait(ref, sem):
        pltpu.make_async_copy(ref, ref, sem).wait()

    def peer(d):
        return (2 * ((k + d) % CHIPS) + core, s)

    barrier = pltpu.get_barrier_semaphore()

    def greet(to):
        pl.semaphore_signal(barrier, inc=1, device_id=to, device_id_type=MESH)

    @pl.loop(1, 16)
    def _(d):
        greet(((c + d) % 16, s))

    @pl.loop(1, SPACE)
    def _(d):
        greet((c, (s + d) % SPACE))

    greet((2 * k + other, side))
    greet(((2 * k + 15) % 16, side))
    greet(((2 * k + 2) % 16, side))

    for slot in range(10):
        base = slot * 80 // 128 * 128
        window = t1_ref[:, base : base + 256]
        shift = slot * 80 - base
        if shift:
            window = pltpu.roll(window, 256 - shift, axis=1)
        window = window[:, :128]
        for row in range(4):
            aext[row, slot] = window[8 * row : 8 * row + 8]

    pl.semaphore_wait(barrier, 49)

    own_rows = pl.ds(pl.multiple_of(8 * core, 8), 8)
    edge = 3 * core
    below = (k + 2 * core + CHIPS - 1) % CHIPS
    remote(
        aext.at[:, pl.ds(4 * other, 5)], gc.at[:, :, own_rows], halo_send.at[0], halo_recv.at[0], partner
    )
    for to in range(2):
        remote(
            aext.at[edge, pl.ds(4 * to, 5)],
            rv.at[other],
            halo_send.at[1 + to],
            halo_recv.at[1 + other],
            (2 * below + to, s),
        )
        away = right if to == 0 else left
        start = 8 - 8 * to
        remote(
            aext.at[:, start : start + 2],
            rh.at[core],
            halo_send.at[3 + to],
            halo_recv.at[3 + core],
            (2 * k + to, away),
        )
        remote(
            aext.at[edge, start : start + 2],
            rd.at[other],
            halo_send.at[5 + to],
            halo_recv.at[5 + other],
            (2 * below + to, away),
        )
    remote(w_ref, wall.at[core], send.at[0], recv.at[0], partner)
    own_w = pltpu.make_async_copy(w_ref, wall.at[core], local.at[0])
    own_w.start()
    lanes_k = pl.ds(pl.multiple_of(128 * k, 128), 128)
    own_mi = pltpu.make_async_copy(mi_ref, mi_all.at[:, lanes_k], local.at[1])
    own_mi.start()
    rows_k = pl.ds(pl.multiple_of(64 * k, 64), 64)
    own_mo = pltpu.make_async_copy(mo_ref, mo_all.at[rows_k], local.at[2])
    own_mo.start()

    @pl.loop(1, CHIPS)
    def _(d):
        remote(mi_ref, mi_all.at[:, lanes_k], send.at[1], recv.at[1], peer(d))

    gc[:, :, own_rows] = aext[:, pl.ds(4 * core, 5)]
    wait(gc.at[:, :, own_rows], halo_recv.at[0])
    for i in range(2):
        wait(rv.at[i], halo_recv.at[1 + i])
        wait(rh.at[i], halo_recv.at[3 + i])
        wait(rd.at[i], halo_recv.at[5 + i])
    at_left = jnp.logical_and(core == 0, s > 0)
    at_right = jnp.logical_and(core == 1, s < SPACE - 1)
    for half in range(2):
        rows = slice(8 * half, 8 * half + 8)
        for row in range(4):
            for slot, use, column in ((0, at_left, 0), (1, at_left, 1), (4, at_right, 0)):
                gc[row, slot, rows] += jnp.where(use, rh[half, row, column], 0.0)
    beyond = []
    for half, inside in ((0, k > 0), (1, k < CHIPS - 1)):
        slabs = []
        for slot in range(5):
            value = rv[half, slot]
            if slot in (0, 1):
                value = value + jnp.where(at_left, rd[half, slot], 0.0)
            if slot == 4:
                value = value + jnp.where(at_right, rd[half, 0], 0.0)
            value = jnp.where(inside, value, 0.0)
            value = value[7:8] if half == 0 else value[0:1]
            slabs.append(jnp.broadcast_to(value, (16, 128)))
        beyond.append(jnp.concatenate(slabs, axis=0))
    grid = [gc[row].reshape(80, 128) for row in range(4)]
    place = lax.broadcasted_iota(jnp.int32, (80, 128), 0) % 16
    before = jnp.where(place == 0, beyond[0], pltpu.roll(grid[3], 1, axis=0))
    after = jnp.where(place == 15, beyond[1], pltpu.roll(grid[0], 79, axis=0))
    lines = [line.astype(BF16) for line in (before, *grid, after)]
    outside = jnp.logical_and(core == 0, s == 0)
    keep = jnp.logical_or(lax.broadcasted_iota(jnp.int32, (80, 128), 0) >= 16, jnp.logical_not(outside))
    rows16 = pl.ds(pl.multiple_of(16 * k, 16), 16)
    for row in range(4):
        patches = jnp.concatenate(lines[row : row + 3], axis=1)
        stem = jnp.dot(patches, tw_ref[...], preferred_element_type=F32) + sb_ref[...]
        stem = jnp.where(keep, gelu(stem), 0.0)
        xall[:, rows16, 128 * row : 128 * row + 128] = stem.reshape(5, 16, 128).astype(BF16)

    @pl.loop(1, CHIPS)
    def _(d):
        remote(xall.at[:, rows16], xall.at[:, rows16], send.at[2], recv.at[2], peer(d))

    @pl.loop(1, CHIPS)
    def _(d):
        remote(mo_ref, mo_all.at[rows_k], send.at[3], recv.at[3], peer(d))

    own_w.wait()
    wait(w_ref, recv.at[0])
    wait(xall.at[:, :112], recv.at[2])
    tokens = xall[...].reshape(640, 512)
    lane = lax.broadcasted_iota(jnp.int32, (64, 128), 1)
    sums = [[0.0, 0.0] for _ in range(4)]
    for half in range(2):
        terms = jnp.dot(tokens, wall[half], preferred_element_type=F32)
        both = terms[128:640, 128:256] + terms[0:512, 0:128] + eb_ref[pl.ds(2 * k + half, 1), :]
        for column in range(4):
            turned = both[128 * column : 128 * column + 128].T
            shifted = pltpu.roll(turned[0:64], 1, axis=1)
            value = (turned[64:128] + jnp.where(lane > 0, shifted, 0.0)).astype(BF16)
            eh[core, 64 * half : 64 * half + 64, 128 * column : 128 * column + 128] = value
            wide = value.astype(F32)
            sums[column][0] += jnp.sum(wide, axis=0, keepdims=True)
            sums[column][1] += jnp.sum(wide * wide, axis=0, keepdims=True)
    for column in range(4):
        for kind in range(2):
            st[c, kind : kind + 1, 128 * column : 128 * column + 128] = sums[column][kind]

    @pl.loop(1, 16)
    def _(d):
        remote(st.at[c], st.at[c], send.at[4], recv.at[4], ((c + d) % 16, s))

    remote(eh.at[core], eh.at[core], send.at[5], recv.at[5], partner)

    gain = jnp.broadcast_to(gn_ref[pl.ds(k, 1), :], (128, 128)).T
    offset = jnp.broadcast_to(nb_ref[pl.ds(k, 1), :], (128, 128)).T
    gain = jnp.concatenate([gain] * 4, axis=1)
    offset = jnp.concatenate([offset] * 4, axis=1)
    wait(st.at[:15], recv.at[4])
    wait(eh.at[0], recv.at[5])
    normed = []
    for half in range(2):
        total = st[half]
        for chip in range(1, CHIPS):
            total = total + st[2 * chip + half]
        average = total[0:1] * (1.0 / 1024)
        variance = total[1:2] * (1.0 / 1024) - average * average
        scale = lax.rsqrt(variance + 1e-05)
        value = (eh[half].astype(F32) - average) * scale * gain + offset
        normed.append(value.astype(BF16))
    normed = jnp.concatenate(normed, axis=0)

    own_mi.wait()
    wait(mi_all.at[:, :896], recv.at[1])
    low = lax.broadcasted_iota(jnp.int32, (128, 128), 1) < 64
    for block in range(4):
        part = jnp.dot(normed, mi_all[:, 256 * block : 256 * block + 256], preferred_element_type=F32)
        first = part[0:128, 0:128] + pltpu.roll(part[128:256, 0:128], 64, axis=1)
        second = pltpu.roll(part[0:128, 128:256], 64, axis=1) + part[128:256, 128:256]
        summed = jnp.where(low, first, second).astype(BF16)
        for band in range(8):
            hs[4 * band + block] = summed[16 * band : 16 * band + 16]

    @pl.loop(1, SPACE)
    def _(d):
        to = (s + d) % SPACE
        remote(hs.at[to], rs.at[s], send.at[6], recv.at[6], (c, to))

    rs[s] = hs[s]
    wait(rs.at[: SPACE - 1], recv.at[6])
    total = rs[0].astype(F32)
    for source in range(1, SPACE):
        total = total + rs[source].astype(F32)
    total = total + mb_ref[core, pl.ds(s % 4, 1), :]
    act[s] = gelu(total).astype(BF16)

    @pl.loop(1, SPACE)
    def _(d):
        remote(act.at[s], act.at[s], send.at[7], recv.at[7], (c, (s + d) % SPACE))

    own_mo.wait()
    wait(mo_all.at[:448], recv.at[3])
    wait(act.at[: SPACE - 1], recv.at[7])

    def rows_of(which):
        blocks = act[pl.ds(16 * which, 16)]
        lines = [jnp.concatenate([blocks[4 * band + lb] for lb in range(4)], axis=1) for band in range(4)]
        return jnp.concatenate(lines, axis=0)

    po[...] = jnp.dot(rows_of(other), mo_all[...], preferred_element_type=F32)
    remote(po, pr, send.at[8], recv.at[8], partner)
    mine = jnp.dot(rows_of(core), mo_all[...], preferred_element_type=F32) + ob_ref[...]
    residual = [eh[half, pl.ds(pl.multiple_of(64 * core, 64), 64), :].astype(F32) for half in range(2)]
    mine = mine + jnp.concatenate(residual, axis=1)
    wait(pr, recv.at[8])
    out_ref[...] = (mine + pr[...]).astype(BF16)

    wait(gc.at[:, :, own_rows], halo_send.at[0])
    for i in range(2):
        wait(rv.at[i], halo_send.at[1 + i])
        wait(rh.at[i], halo_send.at[3 + i])
        wait(rd.at[i], halo_send.at[5 + i])
    wait(w_ref, send.at[0])
    wait(mi_all.at[:, :896], send.at[1])
    wait(xall.at[:, :112], send.at[2])
    wait(mo_all.at[:448], send.at[3])
    wait(st.at[:15], send.at[4])
    wait(eh.at[0], send.at[5])
    wait(rs.at[: SPACE - 1], send.at[6])
    wait(act.at[: SPACE - 1], send.at[7])
    wait(po, send.at[8])


def shards(
    fields,
    stem_weight,
    stem_bias,
    embed_weight,
    embed_bias,
    norm_gain,
    norm_bias,
    mix_in,
    mix_in_bias,
    mix_out,
    mix_out_bias,
):
    t1 = fields[0].astype(F32).reshape(20, 8, 4, 32).transpose(2, 1, 3, 0).reshape(32, 640)
    t1 = jnp.pad(t1, ((0, 0), (100, 156)))
    tw = jnp.stack([jnp.pad(stem_weight, ((0, 0), (i, 3 - i), (0, 0), (0, 0))) for i in range(4)], axis=3)
    tw = jnp.pad(tw.reshape(3, 120, 128), ((0, 0), (0, 8), (0, 0))).reshape(384, 128)
    sb = jnp.tile(stem_bias, 4)[None]
    w = jnp.pad(embed_weight, ((1, 0), (1, 0), (0, 0), (0, 0))).reshape(2, 4, 2, 4, 32, 64)
    w = w.transpose(1, 3, 4, 2, 0, 5).reshape(512, 256)
    eb = jnp.pad(embed_bias.reshape(16, 64), ((0, 0), (64, 0)))
    mi = jnp.concatenate([mix_in[:512], mix_in[512:]], axis=1)
    mb = mix_in_bias.reshape(8, 2, 64).transpose(1, 0, 2).reshape(2, 4, 128)
    out = pl.pallas_call(
        kernel,
        out_shape=jax.ShapeDtypeStruct((64, 1024), BF16),
        in_specs=[pl.BlockSpec(memory_space=pltpu.VMEM)] * 11,
        out_specs=pl.BlockSpec(memory_space=pltpu.VMEM),
        scratch_shapes=[
            pltpu.VMEM((4, 10, 8, 128), F32),
            pltpu.VMEM((4, 5, 16, 128), F32),
            pltpu.VMEM((2, 5, 8, 128), F32),
            pltpu.VMEM((2, 4, 2, 8, 128), F32),
            pltpu.VMEM((2, 2, 8, 128), F32),
            pltpu.VMEM((5, 128, 512), BF16),
            pltpu.VMEM((2, 512, 256), BF16),
            pltpu.VMEM((2, 128, 512), BF16),
            pltpu.VMEM((16, 2, 512), F32),
            pltpu.VMEM((512, 1024), BF16),
            pltpu.VMEM((512, 1024), BF16),
            pltpu.VMEM((SPACE, 16, 128), BF16),
            pltpu.VMEM((SPACE, 16, 128), BF16),
            pltpu.VMEM((SPACE, 16, 128), BF16),
            pltpu.VMEM((64, 1024), F32),
            pltpu.VMEM((64, 1024), F32),
            pltpu.SemaphoreType.DMA((7,)),
            pltpu.SemaphoreType.DMA((7,)),
            pltpu.SemaphoreType.DMA((9,)),
            pltpu.SemaphoreType.DMA((9,)),
            pltpu.SemaphoreType.DMA((3,)),
        ],
        compiler_params=pltpu.CompilerParams(collective_id=0, has_side_effects=True),
    )(
        t1,
        tw,
        sb,
        w,
        eb,
        norm_gain.reshape(8, 128),
        norm_bias.reshape(8, 128),
        mi,
        mb,
        mix_out,
        mix_out_bias[None],
    )
    return out[None]


def solution(mesh):
    placed = (
        P(None, None, "chan", "space"),
        P(),
        P(),
        P(None, None, None, "chan"),
        P(),
        P(),
        P(),
        P("space", "chan"),
        P(),
        P("chan", "space"),
        P("space"),
    )
    return jax.shard_map(
        shards, mesh=mesh, in_specs=placed, out_specs=P(None, "chan", "space"), check_vma=False
    )
```

```python
import functools

import jax
import jax.numpy as jnp
from jax import lax
from jax.experimental import pallas as pl
from jax.experimental.pallas import tpu as pltpu
from jax.sharding import PartitionSpec as P

MESH = pl.DeviceIdType.MESH
CHIPS = 8
SPACE = 32
F32 = jnp.float32
BF16 = jnp.bfloat16


def gelu(x):
    return 0.5 * x * (1.0 + lax.erf(x * 0.7071067811865476))


def kernel(
    t1_ref,
    tw_ref,
    sb_ref,
    w_ref,
    eb_ref,
    gn_ref,
    nb_ref,
    mi_ref,
    mb_ref,
    mo_ref,
    ob_ref,
    out_ref,
    aext,
    gc,
    rv,
    rh,
    rd,
    xall,
    wall,
    eh,
    st,
    mi_all,
    mo_all,
    hs,
    rs,
    quarter,
    act,
    po,
    pr,
    halo_send,
    halo_recv,
    send,
    recv,
    local,
):
    c, s = lax.axis_index("chan"), lax.axis_index("space")
    k, core = c // 2, c % 2
    other = 1 - core
    partner = (2 * k + other, s)
    z, part = s // 4, s % 4
    right, left = (s + 1) % SPACE, (s + SPACE - 1) % SPACE
    side = jnp.where(core == 0, left, right)

    def remote(src, dst, ssem, rsem, to):
        copy = pltpu.make_async_remote_copy(
            src_ref=src, dst_ref=dst, send_sem=ssem, recv_sem=rsem, device_id=to, device_id_type=MESH
        )
        copy.start()

    def wait(ref, sem):
        pltpu.make_async_copy(ref, ref, sem).wait()

    ring, x = k // 4, k % 4
    ahead, behind = (x + 1) % 4, (x + 3) % 4

    def chip(r, i):
        return (2 * (4 * r + i) + core, s)

    near = [chip(ring, ahead), chip(ring, behind), chip(1 - ring, x), chip(1 - ring, ahead), chip(1 - ring, behind)]

    def spread(src, dst, ssem, rsem):
        for to in near:
            remote(src, dst, ssem, rsem, to)

    def forward(half, ssem, rsem):
        for r in range(2):
            passed = half(4 * r + behind, 0)
            remote(passed, passed, ssem, rsem, chip(ring, ahead))
            passed = half(4 * r + ahead, 1)
            remote(passed, passed, ssem, rsem, chip(ring, behind))

    def mi_half(owner, which):
        return mi_all.at[256 * which : 256 * which + 256, pl.ds(pl.multiple_of(128 * owner, 128), 128)]

    def mo_half(owner, which):
        return mo_all.at[pl.ds(pl.multiple_of(64 * owner + 32 * which, 32), 32)]

    def x_half(owner, which):
        return xall.at[:, pl.ds(pl.multiple_of(16 * owner, 16), 16), 256 * which : 256 * which + 256]

    barrier = pltpu.get_barrier_semaphore()

    def greet(to):
        pl.semaphore_signal(barrier, inc=1, device_id=to, device_id_type=MESH)

    @pl.loop(1, 16)
    def _(d):
        greet(((c + d) % 16, s))

    @pl.loop(1, 8)
    def _(d):
        greet((c, (s + 4 * d) % SPACE))

    for d in range(1, 4):
        greet((c, 4 * z + (part + d) % 4))
    greet((c, side))
    greet((2 * k + other, side))
    greet(((2 * k + 15) % 16, side))
    greet(((2 * k + 2) % 16, side))

    for slot in range(10):
        base = slot * 80 // 128 * 128
        window = t1_ref[:, base : base + 256]
        shift = slot * 80 - base
        if shift:
            window = pltpu.roll(window, 256 - shift, axis=1)
        window = window[:, :128]
        for row in range(4):
            aext[row, slot] = window[8 * row : 8 * row + 8]

    pl.semaphore_wait(barrier, 29)

    own_rows = pl.ds(pl.multiple_of(8 * core, 8), 8)
    edge = 3 * core
    below = (k + 2 * core + CHIPS - 1) % CHIPS
    remote(
        aext.at[:, pl.ds(4 * other, 5)], gc.at[:, :, own_rows], halo_send.at[0], halo_recv.at[0], partner
    )
    for to in range(2):
        remote(
            aext.at[edge, pl.ds(4 * to, 5)],
            rv.at[other],
            halo_send.at[1 + to],
            halo_recv.at[1 + other],
            (2 * below + to, s),
        )
        away = right if to == 0 else left
        start = 8 - 8 * to
        remote(
            aext.at[:, start : start + 2],
            rh.at[core],
            halo_send.at[3 + to],
            halo_recv.at[3 + core],
            (2 * k + to, away),
        )
        remote(
            aext.at[edge, start : start + 2],
            rd.at[other],
            halo_send.at[5 + to],
            halo_recv.at[5 + other],
            (2 * below + to, away),
        )
    remote(w_ref, wall.at[core], send.at[0], recv.at[0], partner)
    own_w = pltpu.make_async_copy(w_ref, wall.at[core], local.at[0])
    own_w.start()
    lanes_k = pl.ds(pl.multiple_of(128 * k, 128), 128)
    own_mi = pltpu.make_async_copy(mi_ref, mi_all.at[:, lanes_k], local.at[1])
    own_mi.start()
    rows_k = pl.ds(pl.multiple_of(64 * k, 64), 64)
    own_mo = pltpu.make_async_copy(mo_ref, mo_all.at[rows_k], local.at[2])
    own_mo.start()

    spread(mi_ref, mi_all.at[:, lanes_k], send.at[1], recv.at[1])

    gc[:, :, own_rows] = aext[:, pl.ds(4 * core, 5)]
    wait(gc.at[:, :, own_rows], halo_recv.at[0])
    for i in range(2):
        wait(rv.at[i], halo_recv.at[1 + i])
        wait(rh.at[i], halo_recv.at[3 + i])
        wait(rd.at[i], halo_recv.at[5 + i])
    at_left = jnp.logical_and(core == 0, s > 0)
    at_right = jnp.logical_and(core == 1, s < SPACE - 1)
    for half in range(2):
        rows = slice(8 * half, 8 * half + 8)
        for row in range(4):
            for slot, use, column in ((0, at_left, 0), (1, at_left, 1), (4, at_right, 0)):
                gc[row, slot, rows] += jnp.where(use, rh[half, row, column], 0.0)
    beyond = []
    for half, inside in ((0, k > 0), (1, k < CHIPS - 1)):
        slabs = []
        for slot in range(5):
            value = rv[half, slot]
            if slot in (0, 1):
                value = value + jnp.where(at_left, rd[half, slot], 0.0)
            if slot == 4:
                value = value + jnp.where(at_right, rd[half, 0], 0.0)
            value = jnp.where(inside, value, 0.0)
            value = value[7:8] if half == 0 else value[0:1]
            slabs.append(jnp.broadcast_to(value, (16, 128)))
        beyond.append(jnp.concatenate(slabs, axis=0))
    grid = [gc[row].reshape(80, 128) for row in range(4)]
    place = lax.broadcasted_iota(jnp.int32, (80, 128), 0) % 16
    before = jnp.where(place == 0, beyond[0], pltpu.roll(grid[3], 1, axis=0))
    after = jnp.where(place == 15, beyond[1], pltpu.roll(grid[0], 79, axis=0))
    lines = [line.astype(BF16) for line in (before, *grid, after)]
    outside = jnp.logical_and(core == 0, s == 0)
    keep = jnp.logical_or(lax.broadcasted_iota(jnp.int32, (80, 128), 0) >= 16, jnp.logical_not(outside))
    rows16 = pl.ds(pl.multiple_of(16 * k, 16), 16)
    for row in range(4):
        patches = jnp.concatenate(lines[row : row + 3], axis=1)
        stem = jnp.dot(patches, tw_ref[...], preferred_element_type=F32) + sb_ref[...]
        stem = jnp.where(keep, gelu(stem), 0.0)
        xall[:, rows16, 128 * row : 128 * row + 128] = stem.reshape(5, 16, 128).astype(BF16)

    spread(xall.at[:, rows16], xall.at[:, rows16], send.at[2], recv.at[2])

    wait(xall.at[:, :80], recv.at[2])
    forward(x_half, send.at[9], recv.at[9])
    wait(mi_all.at[:, :640], recv.at[1])
    forward(mi_half, send.at[10], recv.at[10])

    own_w.wait()
    wait(w_ref, recv.at[0])
    wait(xall.at[:, :32], recv.at[9])
    tokens = xall[...].reshape(640, 512)
    lane = lax.broadcasted_iota(jnp.int32, (64, 128), 1)
    sums = [[0.0, 0.0] for _ in range(4)]
    for half in range(2):
        terms = jnp.dot(tokens, wall[half], preferred_element_type=F32)
        both = terms[128:640, 128:256] + terms[0:512, 0:128] + eb_ref[pl.ds(2 * k + half, 1), :]
        for column in range(4):
            turned = both[128 * column : 128 * column + 128].T
            shifted = pltpu.roll(turned[0:64], 1, axis=1)
            value = (turned[64:128] + jnp.where(lane > 0, shifted, 0.0)).astype(BF16)
            eh[core, 64 * half : 64 * half + 64, 128 * column : 128 * column + 128] = value
            wide = value.astype(F32)
            sums[column][0] += jnp.sum(wide, axis=0, keepdims=True)
            sums[column][1] += jnp.sum(wide * wide, axis=0, keepdims=True)
    for column in range(4):
        for kind in range(2):
            st[c, kind : kind + 1, 128 * column : 128 * column + 128] = sums[column][kind]

    @pl.loop(1, 16)
    def _(d):
        remote(st.at[c], st.at[c], send.at[4], recv.at[4], ((c + d) % 16, s))

    remote(eh.at[core], eh.at[core], send.at[5], recv.at[5], partner)

    gain = jnp.broadcast_to(gn_ref[pl.ds(k, 1), :], (128, 128)).T
    offset = jnp.broadcast_to(nb_ref[pl.ds(k, 1), :], (128, 128)).T
    gain = jnp.concatenate([gain] * 4, axis=1)
    offset = jnp.concatenate([offset] * 4, axis=1)
    wait(st.at[:15], recv.at[4])
    wait(eh.at[0], recv.at[5])
    spread(mo_ref, mo_all.at[rows_k], send.at[3], recv.at[3])
    normed = []
    for half in range(2):
        total = st[half]
        for j in range(1, CHIPS):
            total = total + st[2 * j + half]
        average = total[0:1] * (1.0 / 1024)
        variance = total[1:2] * (1.0 / 1024) - average * average
        scale = lax.rsqrt(variance + 1e-05)
        value = (eh[half].astype(F32) - average) * scale * gain + offset
        normed.append(value.astype(BF16))
    normed = jnp.concatenate(normed, axis=0)

    own_mi.wait()
    wait(mi_all.at[:, :256], recv.at[10])
    low = lax.broadcasted_iota(jnp.int32, (128, 128), 1) < 64
    for block in range(4):
        prod = jnp.dot(normed, mi_all[:, 256 * block : 256 * block + 256], preferred_element_type=F32)
        first = prod[0:128, 0:128] + pltpu.roll(prod[128:256, 0:128], 64, axis=1)
        second = pltpu.roll(prod[0:128, 128:256], 64, axis=1) + prod[128:256, 128:256]
        summed = jnp.where(low, first, second).astype(BF16)
        for band in range(8):
            hs[band, :, 128 * block : 128 * block + 128] = summed[16 * band : 16 * band + 16]

    @pl.loop(1, 8)
    def _(d):
        to = (z + d) % 8
        remote(hs.at[to], rs.at[z], send.at[6], recv.at[6], (c, 4 * to + part))

    rs[z] = hs[z]
    wait(rs.at[:7], recv.at[6])
    total = rs[0].astype(F32)
    for source in range(1, 8):
        total = total + rs[source].astype(F32)
    quarter[part] = total.astype(BF16)
    for d in range(1, 4):
        to = 4 * z + (part + d) % 4
        remote(quarter.at[part], quarter.at[part], send.at[7], recv.at[7], (c, to))
    wait(mo_all.at[:320], recv.at[3])
    forward(mo_half, send.at[11], recv.at[11])
    wait(quarter.at[:3], recv.at[7])
    total = quarter[0].astype(F32)
    for source in range(1, 4):
        total = total + quarter[source].astype(F32)
    total = total + mb_ref[pl.ds(core, 1), :]
    act[z] = gelu(total).astype(BF16)

    @pl.loop(1, 8)
    def _(d):
        remote(act.at[z], act.at[z], send.at[12], recv.at[12], (c, (s + 4 * d) % SPACE))

    own_mo.wait()
    wait(act.at[:7], recv.at[12])
    wait(mo_all.at[:128], recv.at[11])

    def rows_of(which):
        return act[pl.ds(4 * which, 4)].reshape(64, 512)

    po[...] = jnp.dot(rows_of(other), mo_all[...], preferred_element_type=F32)
    remote(po, pr, send.at[8], recv.at[8], partner)
    mine = jnp.dot(rows_of(core), mo_all[...], preferred_element_type=F32) + ob_ref[...]
    residual = [eh[half, pl.ds(pl.multiple_of(64 * core, 64), 64), :].astype(F32) for half in range(2)]
    mine = mine + jnp.concatenate(residual, axis=1)
    wait(pr, recv.at[8])
    out_ref[...] = (mine + pr[...]).astype(BF16)

    wait(gc.at[:, :, own_rows], halo_send.at[0])
    for i in range(2):
        wait(rv.at[i], halo_send.at[1 + i])
        wait(rh.at[i], halo_send.at[3 + i])
        wait(rd.at[i], halo_send.at[5 + i])
    wait(w_ref, send.at[0])
    wait(mi_all.at[:, :640], send.at[1])
    wait(xall.at[:, :80], send.at[2])
    wait(mo_all.at[:320], send.at[3])
    wait(st.at[:15], send.at[4])
    wait(eh.at[0], send.at[5])
    wait(rs.at[:7], send.at[6])
    wait(quarter.at[:3], send.at[7])
    wait(po, send.at[8])
    wait(xall.at[:, :32], send.at[9])
    wait(mi_all.at[:, :256], send.at[10])
    wait(mo_all.at[:128], send.at[11])
    wait(act.at[:7], send.at[12])


def shards(
    fields,
    stem_weight,
    stem_bias,
    embed_weight,
    embed_bias,
    norm_gain,
    norm_bias,
    mix_in,
    mix_in_bias,
    mix_out,
    mix_out_bias,
):
    t1 = fields[0].astype(F32).reshape(20, 8, 4, 32).transpose(2, 1, 3, 0).reshape(32, 640)
    t1 = jnp.pad(t1, ((0, 0), (100, 156)))
    tw = jnp.stack([jnp.pad(stem_weight, ((0, 0), (i, 3 - i), (0, 0), (0, 0))) for i in range(4)], axis=3)
    tw = jnp.pad(tw.reshape(3, 120, 128), ((0, 0), (0, 8), (0, 0))).reshape(384, 128)
    sb = jnp.tile(stem_bias, 4)[None]
    w = jnp.pad(embed_weight, ((1, 0), (1, 0), (0, 0), (0, 0))).reshape(2, 4, 2, 4, 32, 64)
    w = w.transpose(1, 3, 4, 2, 0, 5).reshape(512, 256)
    eb = jnp.pad(embed_bias.reshape(16, 64), ((0, 0), (64, 0)))
    mi = jnp.concatenate([mix_in[:512], mix_in[512:]], axis=1)
    mb = mix_in_bias.reshape(8, 2, 64).transpose(1, 0, 2).reshape(2, 512)
    out = pl.pallas_call(
        kernel,
        out_shape=jax.ShapeDtypeStruct((64, 1024), BF16),
        in_specs=[pl.BlockSpec(memory_space=pltpu.VMEM)] * 11,
        out_specs=pl.BlockSpec(memory_space=pltpu.VMEM),
        scratch_shapes=[
            pltpu.VMEM((4, 10, 8, 128), F32),
            pltpu.VMEM((4, 5, 16, 128), F32),
            pltpu.VMEM((2, 5, 8, 128), F32),
            pltpu.VMEM((2, 4, 2, 8, 128), F32),
            pltpu.VMEM((2, 2, 8, 128), F32),
            pltpu.VMEM((5, 128, 512), BF16),
            pltpu.VMEM((2, 512, 256), BF16),
            pltpu.VMEM((2, 128, 512), BF16),
            pltpu.VMEM((16, 2, 512), F32),
            pltpu.VMEM((512, 1024), BF16),
            pltpu.VMEM((512, 1024), BF16),
            pltpu.VMEM((8, 16, 512), BF16),
            pltpu.VMEM((8, 16, 512), BF16),
            pltpu.VMEM((4, 16, 512), BF16),
            pltpu.VMEM((8, 16, 512), BF16),
            pltpu.VMEM((64, 1024), F32),
            pltpu.VMEM((64, 1024), F32),
            pltpu.SemaphoreType.DMA((7,)),
            pltpu.SemaphoreType.DMA((7,)),
            pltpu.SemaphoreType.DMA((13,)),
            pltpu.SemaphoreType.DMA((13,)),
            pltpu.SemaphoreType.DMA((3,)),
        ],
        compiler_params=pltpu.CompilerParams(collective_id=0, has_side_effects=True),
    )(
        t1,
        tw,
        sb,
        w,
        eb,
        norm_gain.reshape(8, 128),
        norm_bias.reshape(8, 128),
        mi,
        mb,
        mix_out,
        mix_out_bias[None],
    )
    return out[None]


def solution(mesh):
    placed = (
        P(None, None, "chan", "space"),
        P(),
        P(),
        P(None, None, None, "chan"),
        P(),
        P(),
        P(),
        P("space", "chan"),
        P(),
        P("chan", "space"),
        P("space"),
    )
    return jax.shard_map(
        shards, mesh=mesh, in_specs=placed, out_specs=P(None, "chan", "space"), check_vma=False
    )
```

```python
import functools

import jax
import jax.numpy as jnp
from jax import lax
from jax.experimental import pallas as pl
from jax.experimental.pallas import tpu as pltpu
from jax.sharding import PartitionSpec as P

MESH = pl.DeviceIdType.MESH
CHIPS = 8
SPACE = 32
F32 = jnp.float32
BF16 = jnp.bfloat16


def gelu(x):
    return 0.5 * x * (1.0 + lax.erf(x * 0.7071067811865476))


def kernel(
    t1_ref,
    stem_ref,
    sb_ref,
    eb_ref,
    gn_ref,
    nb_ref,
    mb_ref,
    ob_ref,
    embed_ref,
    mi_ref,
    mo_ref,
    out_ref,
    wide,
    aext,
    taps,
    filters,
    gc,
    rv,
    rh,
    rd,
    xall,
    wall,
    eh,
    st,
    mi_all,
    mo_all,
    hs,
    rs,
    quarter,
    act,
    po,
    pr,
    halo_send,
    halo_recv,
    send,
    recv,
    local,
):
    c, s = lax.axis_index("chan"), lax.axis_index("space")
    k, core = c // 2, c % 2
    other = 1 - core
    partner = (2 * k + other, s)
    z, part = s // 4, s % 4
    right, left = (s + 1) % SPACE, (s + SPACE - 1) % SPACE
    side = jnp.where(core == 0, left, right)

    def remote(src, dst, ssem, rsem, to):
        copy = pltpu.make_async_remote_copy(
            src_ref=src, dst_ref=dst, send_sem=ssem, recv_sem=rsem, device_id=to, device_id_type=MESH
        )
        copy.start()

    def wait(ref, sem):
        pltpu.make_async_copy(ref, ref, sem).wait()

    ring, x = k // 4, k % 4
    ahead, behind = (x + 1) % 4, (x + 3) % 4

    def chip(r, i):
        return (2 * (4 * r + i) + core, s)

    near = [chip(ring, ahead), chip(ring, behind), chip(1 - ring, x), chip(1 - ring, ahead), chip(1 - ring, behind)]

    def spread(src, dst, ssem, rsem):
        for to in near:
            remote(src, dst, ssem, rsem, to)

    def forward(half, ssem, rsem):
        for r in range(2):
            passed = half(4 * r + behind, 0)
            remote(passed, passed, ssem, rsem, chip(ring, ahead))
            passed = half(4 * r + ahead, 1)
            remote(passed, passed, ssem, rsem, chip(ring, behind))

    def rows_from(buffer, owner, start, size):
        return buffer.at[pl.ds(pl.multiple_of(64 * owner + start, 16), size)]

    own_rows64 = pl.ds(pl.multiple_of(64 * k, 64), 64)

    def first_round(mine, buffer, ssem, rsem):
        for to in (chip(ring, ahead), chip(ring, behind), chip(1 - ring, x)):
            remote(mine, buffer.at[own_rows64], ssem, rsem, to)

    def second_round(buffer, ssem, rsem):
        across, back, front = 4 * (1 - ring) + x, 4 * ring + behind, 4 * ring + ahead
        for owner, start, to in (
            (back, 0, chip(ring, ahead)),
            (front, 32, chip(ring, behind)),
            (across, 0, chip(ring, ahead)),
            (across, 0, chip(ring, behind)),
            (back, 32, chip(1 - ring, x)),
            (front, 32, chip(1 - ring, x)),
        ):
            passed = rows_from(buffer, owner, start, 32)
            remote(passed, passed, ssem, rsem, to)

    def third_round(buffer, ssem, rsem):
        passed = rows_from(buffer, 4 * ring + (x + 2) % 4, 32, 32)
        remote(passed, passed, ssem, rsem, chip(1 - ring, x))
        passed = rows_from(buffer, 4 * (1 - ring) + behind, 0, 16)
        remote(passed, passed, ssem, rsem, chip(ring, ahead))
        passed = rows_from(buffer, 4 * (1 - ring) + ahead, 16, 16)
        remote(passed, passed, ssem, rsem, chip(ring, behind))

    def x_half(owner, which):
        return xall.at[:, pl.ds(pl.multiple_of(16 * owner, 16), 16), 256 * which : 256 * which + 256]

    barrier = pltpu.get_barrier_semaphore()

    def greet(to):
        pl.semaphore_signal(barrier, inc=1, device_id=to, device_id_type=MESH)

    @pl.loop(1, 16)
    def _(d):
        greet(((c + d) % 16, s))

    @pl.loop(1, 8)
    def _(d):
        greet((c, (s + 4 * d) % SPACE))

    for d in range(1, 4):
        greet((c, 4 * z + (part + d) % 4))
    greet((c, side))
    greet((2 * k + other, side))
    greet(((2 * k + 15) % 16, side))
    greet(((2 * k + 2) % 16, side))

    own_embed = pltpu.make_async_copy(embed_ref, filters, local.at[0])
    own_embed.start()
    own_mi = pltpu.make_async_copy(mi_ref, mi_all.at[own_rows64], local.at[1])
    own_mi.start()
    own_mo = pltpu.make_async_copy(mo_ref, mo_all.at[own_rows64], local.at[2])
    own_mo.start()

    wide[:, 0:128] = jnp.zeros((32, 128), F32)
    wide[:, 128:768] = t1_ref[...].astype(F32)
    wide[:, 768:1024] = jnp.zeros((32, 256), F32)
    for slot in range(10):
        base = (28 + slot * 80) // 128 * 128
        window = wide[:, base : base + 256]
        shift = 28 + slot * 80 - base
        if shift:
            window = pltpu.roll(window, 256 - shift, axis=1)
        window = window[:, :128]
        for row in range(4):
            aext[row, slot] = window[8 * row : 8 * row + 8]

    pl.semaphore_wait(barrier, 29)

    own_rows = pl.ds(pl.multiple_of(8 * core, 8), 8)
    edge = 3 * core
    below = (k + 2 * core + CHIPS - 1) % CHIPS
    remote(
        aext.at[:, pl.ds(4 * other, 5)], gc.at[:, :, own_rows], halo_send.at[0], halo_recv.at[0], partner
    )
    for to in range(2):
        remote(
            aext.at[edge, pl.ds(4 * to, 5)],
            rv.at[other],
            halo_send.at[1 + to],
            halo_recv.at[1 + other],
            (2 * below + to, s),
        )
        away = right if to == 0 else left
        start = 8 - 8 * to
        remote(
            aext.at[:, start : start + 2],
            rh.at[core],
            halo_send.at[3 + to],
            halo_recv.at[3 + core],
            (2 * k + to, away),
        )
        remote(
            aext.at[edge, start : start + 2],
            rd.at[other],
            halo_send.at[5 + to],
            halo_recv.at[5 + other],
            (2 * below + to, away),
        )
    first_round(mi_ref, mi_all, send.at[1], recv.at[1])

    spot = lax.broadcasted_iota(jnp.int32, (32, 128), 1)
    repeat = (spot % 32 == lax.broadcasted_iota(jnp.int32, (32, 128), 0)).astype(BF16)
    cell = lax.broadcasted_iota(jnp.int32, (20, 128), 1) // 32
    taps[...] = jnp.zeros((384, 128), F32)
    for row in range(3):
        tiled = [jnp.dot(stem_ref[row, i], repeat, preferred_element_type=F32) for i in range(3)]
        for column in range(6):
            value = jnp.zeros((20, 128), F32)
            for i in range(3):
                if 0 <= column - i < 4:
                    value = jnp.where(cell == column - i, tiled[i], value)
            start = 128 * row + 20 * column
            taps[start : start + 20] = value
    stem_bias = jnp.concatenate([sb_ref[...]] * 4, axis=1)
    own_embed.wait()
    for row in range(4):
        for column in range(4):
            pieces = []
            for b in range(2):
                for a in range(2):
                    i, j = 4 * a + row - 1, 4 * b + column - 1
                    pieces.append(filters[i, j] if min(i, j) >= 0 else jnp.zeros((32, 64), BF16))
            start = 32 * (4 * row + column)
            wall[core, start : start + 32] = jnp.concatenate(pieces, axis=1)
    remote(wall.at[core], wall.at[core], send.at[0], recv.at[0], partner)

    gc[:, :, own_rows] = aext[:, pl.ds(4 * core, 5)]
    wait(gc.at[:, :, own_rows], halo_recv.at[0])
    for i in range(2):
        wait(rv.at[i], halo_recv.at[1 + i])
        wait(rh.at[i], halo_recv.at[3 + i])
        wait(rd.at[i], halo_recv.at[5 + i])
    at_left = jnp.logical_and(core == 0, s > 0)
    at_right = jnp.logical_and(core == 1, s < SPACE - 1)
    for half in range(2):
        rows = slice(8 * half, 8 * half + 8)
        for row in range(4):
            for slot, use, column in ((0, at_left, 0), (1, at_left, 1), (4, at_right, 0)):
                gc[row, slot, rows] += jnp.where(use, rh[half, row, column], 0.0)
    beyond = []
    for half, inside in ((0, k > 0), (1, k < CHIPS - 1)):
        slabs = []
        for slot in range(5):
            value = rv[half, slot]
            if slot in (0, 1):
                value = value + jnp.where(at_left, rd[half, slot], 0.0)
            if slot == 4:
                value = value + jnp.where(at_right, rd[half, 0], 0.0)
            value = jnp.where(inside, value, 0.0)
            value = value[7:8] if half == 0 else value[0:1]
            slabs.append(jnp.broadcast_to(value, (16, 128)))
        beyond.append(jnp.concatenate(slabs, axis=0))
    grid = [gc[row].reshape(80, 128) for row in range(4)]
    place = lax.broadcasted_iota(jnp.int32, (80, 128), 0) % 16
    before = jnp.where(place == 0, beyond[0], pltpu.roll(grid[3], 1, axis=0))
    after = jnp.where(place == 15, beyond[1], pltpu.roll(grid[0], 79, axis=0))
    lines = [line.astype(BF16) for line in (before, *grid, after)]
    outside = jnp.logical_and(core == 0, s == 0)
    keep = jnp.logical_or(lax.broadcasted_iota(jnp.int32, (80, 128), 0) >= 16, jnp.logical_not(outside))
    rows16 = pl.ds(pl.multiple_of(16 * k, 16), 16)
    tap = taps[...].astype(BF16)
    for row in range(4):
        patches = jnp.concatenate(lines[row : row + 3], axis=1)
        stem = jnp.dot(patches, tap, preferred_element_type=F32) + stem_bias
        stem = jnp.where(keep, gelu(stem), 0.0)
        xall[:, rows16, 128 * row : 128 * row + 128] = stem.reshape(5, 16, 128).astype(BF16)

    spread(xall.at[:, rows16], xall.at[:, rows16], send.at[2], recv.at[2])

    wait(xall.at[:, :80], recv.at[2])
    forward(x_half, send.at[9], recv.at[9])
    wait(mi_all.at[:192], recv.at[1])
    second_round(mi_all, send.at[10], recv.at[10])

    wait(wall.at[0], recv.at[0])
    wait(xall.at[:, :32], recv.at[9])
    tokens = xall[...].reshape(640, 512)
    low = lax.broadcasted_iota(jnp.int32, (1, 128), 1) < 64
    bias_row = eb_ref[pl.ds(k, 1), :]
    bias_rows = [jnp.where(low, 0.0, pltpu.roll(bias_row, 64, axis=1)), jnp.where(low, 0.0, bias_row)]
    lane = lax.broadcasted_iota(jnp.int32, (64, 128), 1)
    sums = [[0.0, 0.0] for _ in range(4)]
    for half in range(2):
        terms = jnp.dot(tokens, wall[half], preferred_element_type=F32)
        both = terms[128:640, 128:256] + terms[0:512, 0:128] + bias_rows[half]
        for column in range(4):
            turned = both[128 * column : 128 * column + 128].T
            shifted = pltpu.roll(turned[0:64], 1, axis=1)
            value = (turned[64:128] + jnp.where(lane > 0, shifted, 0.0)).astype(BF16)
            eh[core, 64 * half : 64 * half + 64, 128 * column : 128 * column + 128] = value
            wide = value.astype(F32)
            sums[column][0] += jnp.sum(wide, axis=0, keepdims=True)
            sums[column][1] += jnp.sum(wide * wide, axis=0, keepdims=True)
    for column in range(4):
        for kind in range(2):
            st[c, kind : kind + 1, 128 * column : 128 * column + 128] = sums[column][kind]

    @pl.loop(1, 16)
    def _(d):
        remote(st.at[c], st.at[c], send.at[4], recv.at[4], ((c + d) % 16, s))

    remote(eh.at[core], eh.at[core], send.at[5], recv.at[5], partner)

    wait(mi_all.at[:192], recv.at[10])
    third_round(mi_all, send.at[13], recv.at[13])
    gain = jnp.broadcast_to(gn_ref[pl.ds(k, 1), :], (128, 128)).T
    offset = jnp.broadcast_to(nb_ref[pl.ds(k, 1), :], (128, 128)).T
    gain = jnp.concatenate([gain] * 4, axis=1)
    offset = jnp.concatenate([offset] * 4, axis=1)
    wait(st.at[:15], recv.at[4])
    wait(eh.at[0], recv.at[5])
    first_round(mo_ref, mo_all, send.at[3], recv.at[3])
    normed = []
    for half in range(2):
        total = st[half]
        for j in range(1, CHIPS):
            total = total + st[2 * j + half]
        average = total[0:1] * (1.0 / 1024)
        variance = total[1:2] * (1.0 / 1024) - average * average
        scale = lax.rsqrt(variance + 1e-05)
        value = (eh[half].astype(F32) - average) * scale * gain + offset
        normed.append(value.astype(BF16))
    normed = jnp.concatenate(normed, axis=1)

    own_mi.wait()
    wait(mi_all.at[:64], recv.at[13])
    summed = lax.dot_general(normed, mi_all[...], (((1,), (1,)), ((), ())), preferred_element_type=F32)
    summed = summed.astype(BF16)
    for band in range(8):
        hs[band] = summed[16 * band : 16 * band + 16]

    @pl.loop(1, 8)
    def _(d):
        to = (z + d) % 8
        remote(hs.at[to], rs.at[z], send.at[6], recv.at[6], (c, 4 * to + part))

    wait(mo_all.at[:192], recv.at[3])
    second_round(mo_all, send.at[11], recv.at[11])
    rs[z] = hs[z]
    wait(rs.at[:7], recv.at[6])
    total = rs[0].astype(F32)
    for source in range(1, 8):
        total = total + rs[source].astype(F32)
    quarter[part] = total.astype(BF16)
    for d in range(1, 4):
        to = 4 * z + (part + d) % 4
        remote(quarter.at[part], quarter.at[part], send.at[7], recv.at[7], (c, to))
    wait(quarter.at[:3], recv.at[7])
    total = quarter[0].astype(F32)
    for source in range(1, 4):
        total = total + quarter[source].astype(F32)
    rows = mb_ref[...]
    turned = pltpu.roll(rows, 64, axis=1)
    ours = jnp.where(low, jnp.where(core == 0, rows, turned), 0.0)
    theirs = jnp.where(low, 0.0, jnp.where(core == 0, turned, rows))
    hidden_bias = [ours[2 * i : 2 * i + 1] + theirs[2 * i + 1 : 2 * i + 2] for i in range(4)]
    total = total + jnp.concatenate(hidden_bias, axis=1)
    act[z] = gelu(total).astype(BF16)

    @pl.loop(1, 8)
    def _(d):
        remote(act.at[z], act.at[z], send.at[12], recv.at[12], (c, (s + 4 * d) % SPACE))

    wait(mo_all.at[:192], recv.at[11])
    third_round(mo_all, send.at[14], recv.at[14])
    own_mo.wait()
    wait(act.at[:7], recv.at[12])
    wait(mo_all.at[:64], recv.at[14])

    def rows_of(which):
        return act[pl.ds(4 * which, 4)].reshape(64, 512)

    others = rows_of(other)
    for half in range(2):
        part_out = jnp.dot(others, mo_all[:, 512 * half : 512 * half + 512], preferred_element_type=F32)
        po[half] = part_out
        remote(po.at[half], pr.at[half], send.at[8 + 7 * half], recv.at[8 + 7 * half], partner)
    mine = jnp.dot(rows_of(core), mo_all[...], preferred_element_type=F32) + ob_ref[...]
    residual = [eh[half, pl.ds(pl.multiple_of(64 * core, 64), 64), :].astype(F32) for half in range(2)]
    mine = mine + jnp.concatenate(residual, axis=1)
    for half in range(2):
        wait(pr.at[half], recv.at[8 + 7 * half])
        span = slice(512 * half, 512 * half + 512)
        out_ref[:, span] = (mine[:, span] + pr[half]).astype(BF16)

    wait(gc.at[:, :, own_rows], halo_send.at[0])
    for i in range(2):
        wait(rv.at[i], halo_send.at[1 + i])
        wait(rh.at[i], halo_send.at[3 + i])
        wait(rd.at[i], halo_send.at[5 + i])
    wait(wall.at[0], send.at[0])
    wait(mi_all.at[:192], send.at[1])
    wait(xall.at[:, :80], send.at[2])
    wait(mo_all.at[:192], send.at[3])
    wait(st.at[:15], send.at[4])
    wait(eh.at[0], send.at[5])
    wait(rs.at[:7], send.at[6])
    wait(quarter.at[:3], send.at[7])
    wait(po.at[0], send.at[8])
    wait(po.at[1], send.at[15])
    wait(xall.at[:, :32], send.at[9])
    wait(mi_all.at[:192], send.at[10])
    wait(mo_all.at[:192], send.at[11])
    wait(mi_all.at[:64], send.at[13])
    wait(mo_all.at[:64], send.at[14])
    wait(act.at[:7], send.at[12])


def shards(
    fields,
    stem_weight,
    stem_bias,
    embed_weight,
    embed_bias,
    norm_gain,
    norm_bias,
    mix_in,
    mix_in_bias,
    mix_out,
    mix_out_bias,
):
    t1 = fields[0].reshape(20, 8, 4, 32).transpose(2, 1, 3, 0).reshape(32, 640)
    out = pl.pallas_call(
        kernel,
        out_shape=jax.ShapeDtypeStruct((64, 1024), BF16),
        in_specs=[pl.BlockSpec(memory_space=pltpu.VMEM)] * 8 + [pl.BlockSpec(memory_space=pl.ANY)] * 3,
        out_specs=pl.BlockSpec(memory_space=pltpu.VMEM),
        scratch_shapes=[
            pltpu.VMEM((32, 1024), F32),
            pltpu.VMEM((4, 10, 8, 128), F32),
            pltpu.VMEM((384, 128), F32),
            pltpu.VMEM((7, 7, 32, 64), BF16),
            pltpu.VMEM((4, 5, 16, 128), F32),
            pltpu.VMEM((2, 5, 8, 128), F32),
            pltpu.VMEM((2, 4, 2, 8, 128), F32),
            pltpu.VMEM((2, 2, 8, 128), F32),
            pltpu.VMEM((5, 128, 512), BF16),
            pltpu.VMEM((2, 512, 256), BF16),
            pltpu.VMEM((2, 128, 512), BF16),
            pltpu.VMEM((16, 2, 512), F32),
            pltpu.VMEM((512, 1024), BF16),
            pltpu.VMEM((512, 1024), BF16),
            pltpu.VMEM((8, 16, 512), BF16),
            pltpu.VMEM((8, 16, 512), BF16),
            pltpu.VMEM((4, 16, 512), BF16),
            pltpu.VMEM((8, 16, 512), BF16),
            pltpu.VMEM((2, 64, 512), F32),
            pltpu.VMEM((2, 64, 512), F32),
            pltpu.SemaphoreType.DMA((7,)),
            pltpu.SemaphoreType.DMA((7,)),
            pltpu.SemaphoreType.DMA((16,)),
            pltpu.SemaphoreType.DMA((16,)),
            pltpu.SemaphoreType.DMA((3,)),
        ],
        compiler_params=pltpu.CompilerParams(collective_id=0, has_side_effects=True),
    )(
        t1,
        stem_weight,
        stem_bias[None],
        embed_bias.reshape(8, 128),
        norm_gain.reshape(8, 128),
        norm_bias.reshape(8, 128),
        mix_in_bias.reshape(8, 128),
        mix_out_bias[None],
        embed_weight,
        mix_in.T,
        mix_out,
    )
    return out[None]


def solution(mesh):
    placed = (
        P(None, None, "chan", "space"),
        P(),
        P(),
        P(None, None, None, "chan"),
        P(),
        P(),
        P(),
        P("space", "chan"),
        P(),
        P("chan", "space"),
        P("space"),
    )
    return jax.shard_map(
        shards, mesh=mesh, in_specs=placed, out_specs=P(None, "chan", "space"), check_vma=False
    )
```

```python
import functools

import jax
import jax.numpy as jnp
from jax import lax
from jax.experimental import pallas as pl
from jax.experimental.pallas import tpu as pltpu
from jax.sharding import PartitionSpec as P

MESH = pl.DeviceIdType.MESH
CHIPS = 8
SPACE = 32
F32 = jnp.float32
BF16 = jnp.bfloat16


def gelu(x):
    return 0.5 * x * (1.0 + lax.erf(x * 0.7071067811865476))


def kernel(
    t1_ref,
    stem_ref,
    sb_ref,
    eb_ref,
    gn_ref,
    nb_ref,
    mb_ref,
    ob_ref,
    embed_ref,
    mi_ref,
    mo_ref,
    out_ref,
    wide,
    aext,
    taps,
    filters,
    gc,
    rv,
    rh,
    rd,
    xall,
    wall,
    eh,
    st,
    mi_all,
    mo_all,
    hs,
    rs,
    quarter,
    act,
    po,
    pr,
    halo_send,
    halo_recv,
    send,
    recv,
    local,
):
    c, s = lax.axis_index("chan"), lax.axis_index("space")
    k, core = c // 2, c % 2
    other = 1 - core
    partner = (2 * k + other, s)
    z, part = s // 4, s % 4
    right, left = (s + 1) % SPACE, (s + SPACE - 1) % SPACE
    side = jnp.where(core == 0, left, right)

    def remote(src, dst, ssem, rsem, to):
        copy = pltpu.make_async_remote_copy(
            src_ref=src, dst_ref=dst, send_sem=ssem, recv_sem=rsem, device_id=to, device_id_type=MESH
        )
        copy.start()

    def wait(ref, sem):
        pltpu.make_async_copy(ref, ref, sem).wait()

    ring, x = k // 4, k % 4
    ahead, behind = (x + 1) % 4, (x + 3) % 4

    def chip(r, i):
        return (2 * (4 * r + i) + core, s)

    near = [chip(ring, ahead), chip(ring, behind), chip(1 - ring, x), chip(1 - ring, ahead), chip(1 - ring, behind)]

    def spread(src, dst, ssem, rsem):
        for to in near:
            remote(src, dst, ssem, rsem, to)

    def forward(half, ssem, rsem):
        for r in range(2):
            passed = half(4 * r + behind, 0)
            remote(passed, passed, ssem, rsem, chip(ring, ahead))
            passed = half(4 * r + ahead, 1)
            remote(passed, passed, ssem, rsem, chip(ring, behind))

    def rows_from(buffer, owner, start, size):
        return buffer.at[pl.ds(pl.multiple_of(64 * owner + start, 16), size)]

    own_rows64 = pl.ds(pl.multiple_of(64 * k, 64), 64)

    def first_round(mine, buffer, ssem, rsem):
        for to in (chip(ring, ahead), chip(ring, behind), chip(1 - ring, x)):
            remote(mine, buffer.at[own_rows64], ssem, rsem, to)

    def second_round(buffer, ssem, rsem):
        across, back, front = 4 * (1 - ring) + x, 4 * ring + behind, 4 * ring + ahead
        for owner, start, to in (
            (back, 0, chip(ring, ahead)),
            (front, 32, chip(ring, behind)),
            (across, 0, chip(ring, ahead)),
            (across, 0, chip(ring, behind)),
            (back, 32, chip(1 - ring, x)),
            (front, 32, chip(1 - ring, x)),
        ):
            passed = rows_from(buffer, owner, start, 32)
            remote(passed, passed, ssem, rsem, to)

    def third_round(buffer, ssem, rsem):
        passed = rows_from(buffer, 4 * ring + (x + 2) % 4, 32, 32)
        remote(passed, passed, ssem, rsem, chip(1 - ring, x))
        passed = rows_from(buffer, 4 * (1 - ring) + behind, 0, 16)
        remote(passed, passed, ssem, rsem, chip(ring, ahead))
        passed = rows_from(buffer, 4 * (1 - ring) + ahead, 16, 16)
        remote(passed, passed, ssem, rsem, chip(ring, behind))

    def x_half(slots, count, owner, which):
        rows = pl.ds(pl.multiple_of(16 * owner, 16), 16)
        return xall.at[pl.ds(slots, count), rows, 256 * which : 256 * which + 256]

    def fetch(src, dst, index):
        copy = pltpu.make_async_copy(src, dst, local.at[index])
        copy.start()
        return copy

    own_embed = fetch(embed_ref, filters, 0)
    own_mi = fetch(mi_ref, mi_all.at[own_rows64], 1)
    own_mo = fetch(mo_ref, mo_all.at[own_rows64], 2)

    barrier = pltpu.get_barrier_semaphore()

    def greet(to):
        pl.semaphore_signal(barrier, inc=1, device_id=to, device_id_type=MESH)

    @pl.loop(1, 16)
    def _(d):
        greet(((c + d) % 16, s))

    @pl.loop(1, 8)
    def _(d):
        greet((c, (s + 4 * d) % SPACE))

    for d in range(1, 4):
        greet((c, 4 * z + (part + d) % 4))
    greet((c, side))
    greet((2 * k + other, side))
    greet(((2 * k + 15) % 16, side))
    greet(((2 * k + 2) % 16, side))

    wide[:, 0:128] = jnp.zeros((32, 128), F32)
    wide[:, 128:768] = t1_ref[...].astype(F32)
    wide[:, 768:1024] = jnp.zeros((32, 256), F32)
    for slot in range(10):
        base = (28 + slot * 80) // 128 * 128
        window = wide[:, base : base + 256]
        shift = 28 + slot * 80 - base
        if shift:
            window = pltpu.roll(window, 256 - shift, axis=1)
        window = window[:, :128]
        aext[slot] = window.astype(BF16)

    pl.semaphore_wait(barrier, 29)

    edge = pl.ds(pl.multiple_of(16 * core, 16), 16)
    below = (k + 2 * core + CHIPS - 1) % CHIPS
    remote(aext.at[pl.ds(4 * other, 5)], gc.at[:, core], halo_send.at[0], halo_recv.at[0], partner)
    for to in range(2):
        remote(
            aext.at[pl.ds(4 * to, 5), edge],
            rv.at[other],
            halo_send.at[1 + to],
            halo_recv.at[1 + other],
            (2 * below + to, s),
        )
    for to in range(2):
        away = right if to == 0 else left
        side_slots = slice(8 - 8 * to, 10 - 8 * to)
        remote(
            aext.at[side_slots], rh.at[core], halo_send.at[3 + to], halo_recv.at[3 + core], (2 * k + to, away)
        )
        remote(
            aext.at[side_slots, edge],
            rd.at[other],
            halo_send.at[5 + to],
            halo_recv.at[5 + other],
            (2 * below + to, away),
        )
    first_round(mi_ref, mi_all, send.at[1], recv.at[1])

    spot = lax.broadcasted_iota(jnp.int32, (32, 128), 1)
    repeat = (spot % 32 == lax.broadcasted_iota(jnp.int32, (32, 128), 0)).astype(BF16)
    cell = lax.broadcasted_iota(jnp.int32, (20, 128), 1) // 32
    taps[...] = jnp.zeros((384, 128), F32)
    for row in range(3):
        tiled = [jnp.dot(stem_ref[row, i], repeat, preferred_element_type=F32) for i in range(3)]
        for column in range(6):
            value = jnp.zeros((20, 128), F32)
            for i in range(3):
                if 0 <= column - i < 4:
                    value = jnp.where(cell == column - i, tiled[i], value)
            start = 128 * row + 20 * column
            taps[start : start + 20] = value
    stem_bias = jnp.concatenate([sb_ref[...]] * 4, axis=1)
    own_embed.wait()
    for row in range(4):
        for column in range(4):
            pieces = []
            for b in range(2):
                for a in range(2):
                    i, j = 4 * a + row - 1, 4 * b + column - 1
                    pieces.append(filters[i, j] if min(i, j) >= 0 else jnp.zeros((32, 64), BF16))
            start = 32 * (4 * row + column)
            wall[core, start : start + 32] = jnp.concatenate(pieces, axis=1)
    remote(wall.at[core], wall.at[core], send.at[0], recv.at[0], partner)

    gc[:, core] = aext[pl.ds(4 * core, 5)]
    at_left = jnp.logical_and(core == 0, s > 0)
    at_right = jnp.logical_and(core == 1, s < SPACE - 1)
    outside = jnp.logical_and(core == 0, s == 0)
    rows16 = pl.ds(pl.multiple_of(16 * k, 16), 16)
    tap = taps[...].astype(BF16)

    def sides(ref, half, j):
        first = jnp.where(at_left, ref[half, j].astype(F32), 0.0)
        return first + jnp.where(at_right, ref[half, 0].astype(F32), 0.0) if j else first

    def stem_of(slots, count, at_side):
        height = 16 * count
        blocks = [gc[slots + j, half].astype(F32) for j in range(count) for half in range(2)]
        beyond = []
        for half, inside in ((0, k > 0), (1, k < CHIPS - 1)):
            slabs = []
            for j in range(count):
                value = rv[half, slots + j].astype(F32)
                if at_side:
                    value = value + sides(rd, half, j)
                value = jnp.where(inside, value, 0.0)
                value = value[15:16] if half == 0 else value[0:1]
                slabs.append(jnp.broadcast_to(value, (16, 128)))
            beyond.append(jnp.concatenate(slabs, axis=0))
        if at_side:
            blocks = [block + sides(rh, i % 2, i // 2) for i, block in enumerate(blocks)]
        grid = [jnp.concatenate([block[8 * row : 8 * row + 8] for block in blocks], axis=0) for row in range(4)]
        index = lax.broadcasted_iota(jnp.int32, (height, 128), 0)
        before = jnp.where(index % 16 == 0, beyond[0], pltpu.roll(grid[3], 1, axis=0))
        after = jnp.where(index % 16 == 15, beyond[1], pltpu.roll(grid[0], height - 1, axis=0))
        lines = [line.astype(BF16) for line in (before, *grid, after)]
        for row in range(4):
            patches = jnp.concatenate(lines[row : row + 3], axis=1)
            stem = gelu(jnp.dot(patches, tap, preferred_element_type=F32) + stem_bias)
            if at_side:
                stem = jnp.where(jnp.logical_or(index >= 16, jnp.logical_not(outside)), stem, 0.0)
            stem = stem.reshape(count, 16, 128).astype(BF16)
            xall[pl.ds(slots, count), rows16, 128 * row : 128 * row + 128] = stem
        mine = xall.at[pl.ds(slots, count), rows16]
        return mine

    inner, outer = 2 - 2 * core, 3 * core
    wait(gc.at[:, core], halo_recv.at[0])
    for i in range(2):
        wait(rv.at[i], halo_recv.at[1 + i])
    mine = stem_of(inner, 3, False)
    spread(mine, mine, send.at[2], recv.at[2])
    for i in range(2):
        wait(rh.at[i], halo_recv.at[3 + i])
        wait(rd.at[i], halo_recv.at[5 + i])
    mine = stem_of(outer, 2, True)
    spread(mine, mine, send.at[16], recv.at[16])

    wait(xall.at[:3, :80], recv.at[2])
    forward(functools.partial(x_half, inner, 3), send.at[9], recv.at[9])
    wait(xall.at[:2, :80], recv.at[16])
    forward(functools.partial(x_half, outer, 2), send.at[17], recv.at[17])
    wait(mi_all.at[:192], recv.at[1])
    second_round(mi_all, send.at[10], recv.at[10])

    wait(wall.at[0], recv.at[0])
    wait(xall.at[:3, :32], recv.at[9])
    wait(xall.at[:2, :32], recv.at[17])
    tokens = xall[...].reshape(640, 512)
    low = lax.broadcasted_iota(jnp.int32, (1, 128), 1) < 64
    bias_row = eb_ref[pl.ds(k, 1), :]
    bias_rows = [jnp.where(low, 0.0, pltpu.roll(bias_row, 64, axis=1)), jnp.where(low, 0.0, bias_row)]
    lane = lax.broadcasted_iota(jnp.int32, (64, 128), 1)
    sums = [[0.0, 0.0] for _ in range(4)]
    for half in range(2):
        terms = jnp.dot(tokens, wall[half], preferred_element_type=F32)
        both = terms[128:640, 128:256] + terms[0:512, 0:128] + bias_rows[half]
        for column in range(4):
            turned = both[128 * column : 128 * column + 128].T
            shifted = pltpu.roll(turned[0:64], 1, axis=1)
            value = (turned[64:128] + jnp.where(lane > 0, shifted, 0.0)).astype(BF16)
            eh[core, 64 * half : 64 * half + 64, 128 * column : 128 * column + 128] = value
            wide = value.astype(F32)
            sums[column][0] += jnp.sum(wide, axis=0, keepdims=True)
            sums[column][1] += jnp.sum(wide * wide, axis=0, keepdims=True)
    for column in range(4):
        for kind in range(2):
            st[c, kind : kind + 1, 128 * column : 128 * column + 128] = sums[column][kind]

    @pl.loop(1, 16)
    def _(d):
        remote(st.at[c], st.at[c], send.at[4], recv.at[4], ((c + d) % 16, s))

    remote(eh.at[core], eh.at[core], send.at[5], recv.at[5], partner)

    wait(mi_all.at[:192], recv.at[10])
    third_round(mi_all, send.at[13], recv.at[13])
    gain = jnp.broadcast_to(gn_ref[pl.ds(k, 1), :], (128, 128)).T
    offset = jnp.broadcast_to(nb_ref[pl.ds(k, 1), :], (128, 128)).T
    gain = jnp.concatenate([gain] * 4, axis=1)
    offset = jnp.concatenate([offset] * 4, axis=1)
    wait(st.at[:15], recv.at[4])
    wait(eh.at[0], recv.at[5])
    first_round(mo_ref, mo_all, send.at[3], recv.at[3])
    normed = []
    for half in range(2):
        total = st[half]
        for j in range(1, CHIPS):
            total = total + st[2 * j + half]
        average = total[0:1] * (1.0 / 1024)
        variance = total[1:2] * (1.0 / 1024) - average * average
        scale = lax.rsqrt(variance + 1e-05)
        value = (eh[half].astype(F32) - average) * scale * gain + offset
        normed.append(value.astype(BF16))
    normed = jnp.concatenate(normed, axis=1)

    own_mi.wait()
    wait(mi_all.at[:64], recv.at[13])
    summed = lax.dot_general(normed, mi_all[...], (((1,), (1,)), ((), ())), preferred_element_type=F32)
    summed = summed.astype(BF16)
    for band in range(8):
        hs[band] = summed[16 * band : 16 * band + 16]

    @pl.loop(1, 8)
    def _(d):
        to = (z + d) % 8
        remote(hs.at[to], rs.at[z], send.at[6], recv.at[6], (c, 4 * to + part))

    wait(mo_all.at[:192], recv.at[3])
    second_round(mo_all, send.at[11], recv.at[11])
    rs[z] = hs[z]
    wait(rs.at[:7], recv.at[6])
    total = rs[0].astype(F32)
    for source in range(1, 8):
        total = total + rs[source].astype(F32)
    quarter[part] = total.astype(BF16)
    for d in range(1, 4):
        to = 4 * z + (part + d) % 4
        remote(quarter.at[part], quarter.at[part], send.at[7], recv.at[7], (c, to))
    wait(quarter.at[:3], recv.at[7])
    total = quarter[0].astype(F32)
    for source in range(1, 4):
        total = total + quarter[source].astype(F32)
    rows = mb_ref[...]
    turned = pltpu.roll(rows, 64, axis=1)
    ours = jnp.where(low, jnp.where(core == 0, rows, turned), 0.0)
    theirs = jnp.where(low, 0.0, jnp.where(core == 0, turned, rows))
    hidden_bias = [ours[2 * i : 2 * i + 1] + theirs[2 * i + 1 : 2 * i + 2] for i in range(4)]
    total = total + jnp.concatenate(hidden_bias, axis=1)
    act[z] = gelu(total).astype(BF16)

    @pl.loop(1, 8)
    def _(d):
        remote(act.at[z], act.at[z], send.at[12], recv.at[12], (c, (s + 4 * d) % SPACE))

    wait(mo_all.at[:192], recv.at[11])
    third_round(mo_all, send.at[14], recv.at[14])
    own_mo.wait()
    wait(act.at[:7], recv.at[12])
    wait(mo_all.at[:64], recv.at[14])

    def rows_of(which):
        return act[pl.ds(4 * which, 4)].reshape(64, 512)

    others = rows_of(other)
    for half in range(2):
        part_out = jnp.dot(others, mo_all[:, 512 * half : 512 * half + 512], preferred_element_type=F32)
        po[half] = part_out.astype(BF16)
        remote(po.at[half], pr.at[half], send.at[8 + 7 * half], recv.at[8 + 7 * half], partner)
    mine = jnp.dot(rows_of(core), mo_all[...], preferred_element_type=F32) + ob_ref[...]
    residual = [eh[half, pl.ds(pl.multiple_of(64 * core, 64), 64), :].astype(F32) for half in range(2)]
    mine = mine + jnp.concatenate(residual, axis=1)
    for half in range(2):
        wait(pr.at[half], recv.at[8 + 7 * half])
        span = slice(512 * half, 512 * half + 512)
        out_ref[:, span] = (mine[:, span] + pr[half].astype(F32)).astype(BF16)

    wait(gc.at[:, core], halo_send.at[0])
    for i in range(2):
        wait(rv.at[i], halo_send.at[1 + i])
        wait(rh.at[i], halo_send.at[3 + i])
        wait(rd.at[i], halo_send.at[5 + i])
    wait(wall.at[0], send.at[0])
    wait(mi_all.at[:192], send.at[1])
    wait(xall.at[:3, :80], send.at[2])
    wait(xall.at[:2, :80], send.at[16])
    wait(mo_all.at[:192], send.at[3])
    wait(st.at[:15], send.at[4])
    wait(eh.at[0], send.at[5])
    wait(rs.at[:7], send.at[6])
    wait(quarter.at[:3], send.at[7])
    wait(po.at[0], send.at[8])
    wait(po.at[1], send.at[15])
    wait(xall.at[:3, :32], send.at[9])
    wait(xall.at[:2, :32], send.at[17])
    wait(mi_all.at[:192], send.at[10])
    wait(mo_all.at[:192], send.at[11])
    wait(mi_all.at[:64], send.at[13])
    wait(mo_all.at[:64], send.at[14])
    wait(act.at[:7], send.at[12])


def shards(
    fields,
    stem_weight,
    stem_bias,
    embed_weight,
    embed_bias,
    norm_gain,
    norm_bias,
    mix_in,
    mix_in_bias,
    mix_out,
    mix_out_bias,
):
    t1 = fields[0].reshape(20, 8, 4, 32).transpose(2, 1, 3, 0).reshape(32, 640)
    out = pl.pallas_call(
        kernel,
        out_shape=jax.ShapeDtypeStruct((64, 1024), BF16),
        in_specs=[pl.BlockSpec(memory_space=pltpu.VMEM)] * 8 + [pl.BlockSpec(memory_space=pltpu.HBM)] * 3,
        out_specs=pl.BlockSpec(memory_space=pltpu.VMEM),
        scratch_shapes=[
            pltpu.VMEM((32, 1024), F32),
            pltpu.VMEM((10, 32, 128), BF16),
            pltpu.VMEM((384, 128), F32),
            pltpu.VMEM((7, 7, 32, 64), BF16),
            pltpu.VMEM((5, 2, 32, 128), BF16),
            pltpu.VMEM((2, 5, 16, 128), BF16),
            pltpu.VMEM((2, 2, 32, 128), BF16),
            pltpu.VMEM((2, 2, 16, 128), BF16),
            pltpu.VMEM((5, 128, 512), BF16),
            pltpu.VMEM((2, 512, 256), BF16),
            pltpu.VMEM((2, 128, 512), BF16),
            pltpu.VMEM((16, 2, 512), F32),
            pltpu.VMEM((512, 1024), BF16),
            pltpu.VMEM((512, 1024), BF16),
            pltpu.VMEM((8, 16, 512), BF16),
            pltpu.VMEM((8, 16, 512), BF16),
            pltpu.VMEM((4, 16, 512), BF16),
            pltpu.VMEM((8, 16, 512), BF16),
            pltpu.VMEM((2, 64, 512), BF16),
            pltpu.VMEM((2, 64, 512), BF16),
            pltpu.SemaphoreType.DMA((7,)),
            pltpu.SemaphoreType.DMA((7,)),
            pltpu.SemaphoreType.DMA((18,)),
            pltpu.SemaphoreType.DMA((18,)),
            pltpu.SemaphoreType.DMA((3,)),
        ],
        compiler_params=pltpu.CompilerParams(collective_id=0, has_side_effects=True, vmem_limit_bytes=16 * 2**20),
    )(
        t1,
        stem_weight,
        stem_bias[None],
        embed_bias.reshape(8, 128),
        norm_gain.reshape(8, 128),
        norm_bias.reshape(8, 128),
        mix_in_bias.reshape(8, 128),
        mix_out_bias[None],
        embed_weight,
        mix_in.T,
        mix_out,
    )
    return out[None]


def solution(mesh):
    placed = (
        P(None, None, "chan", "space"),
        P(),
        P(),
        P(None, None, None, "chan"),
        P(),
        P(),
        P(),
        P("space", "chan"),
        P(),
        P("chan", "space"),
        P("space"),
    )
    return jax.shard_map(
        shards, mesh=mesh, in_specs=placed, out_specs=P(None, "chan", "space"), check_vma=False
    )
```

```python
import functools

import jax
import jax.numpy as jnp
from jax import lax
from jax.experimental import pallas as pl
from jax.experimental.pallas import tpu as pltpu
from jax.sharding import PartitionSpec as P

MESH = pl.DeviceIdType.MESH
CHIPS = 8
SPACE = 32
F32 = jnp.float32
BF16 = jnp.bfloat16


def gelu(x):
    return 0.5 * x * (1.0 + lax.erf(x * 0.7071067811865476))


def kernel(
    stem_in,
    sb_in,
    eb_in,
    gn_in,
    nb_in,
    mb_in,
    ob_in,
    filters_in,
    fields_ref,
    mi_ref,
    mo_ref,
    out_ref,
    cells,
    filters,
    stem_ref,
    sb_ref,
    eb_ref,
    gn_ref,
    nb_ref,
    mb_ref,
    ob_ref,
    aext,
    taps,
    gc,
    rv,
    rh,
    rd,
    xall,
    wall,
    eh,
    st,
    mi_all,
    mo_all,
    hs,
    rs,
    quarter,
    act,
    po,
    pr,
    halo_send,
    halo_recv,
    send,
    recv,
    local,
):
    c, s = lax.axis_index("chan"), lax.axis_index("space")
    k, core = c // 2, c % 2
    other = 1 - core
    partner = (2 * k + other, s)
    z, part = s // 4, s % 4
    right, left = (s + 1) % SPACE, (s + SPACE - 1) % SPACE
    side = jnp.where(core == 0, left, right)

    def remote(src, dst, ssem, rsem, to):
        copy = pltpu.make_async_remote_copy(
            src_ref=src, dst_ref=dst, send_sem=ssem, recv_sem=rsem, device_id=to, device_id_type=MESH
        )
        copy.start()

    def wait(ref, sem):
        pltpu.make_async_copy(ref, ref, sem).wait()

    ring, x = k // 4, k % 4
    ahead, behind = (x + 1) % 4, (x + 3) % 4

    def chip(r, i):
        return (2 * (4 * r + i) + core, s)

    near = [chip(ring, ahead), chip(ring, behind), chip(1 - ring, x), chip(1 - ring, ahead), chip(1 - ring, behind)]

    def spread(src, dst, ssem, rsem):
        for to in near:
            remote(src, dst, ssem, rsem, to)

    def forward(half, ssem, rsem):
        for r in range(2):
            passed = half(4 * r + behind, 0)
            remote(passed, passed, ssem, rsem, chip(ring, ahead))
            passed = half(4 * r + ahead, 1)
            remote(passed, passed, ssem, rsem, chip(ring, behind))

    def rows_from(buffer, owner, start, size):
        return buffer.at[pl.ds(pl.multiple_of(64 * owner + start, 16), size)]

    own_rows64 = pl.ds(pl.multiple_of(64 * k, 64), 64)

    def first_round(mine, buffer, ssem, rsem):
        for to in (chip(ring, ahead), chip(ring, behind), chip(1 - ring, x)):
            remote(mine, buffer.at[own_rows64], ssem, rsem, to)

    def second_round(buffer, ssem, rsem, along):
        across, back, front = 4 * (1 - ring) + x, 4 * ring + behind, 4 * ring + ahead
        hops = [(back, 0, 32, chip(ring, ahead)), (front, 32, 32, chip(ring, behind))]
        if along:
            hops += [(across, 0, 64, chip(ring, ahead)), (across, 0, 64, chip(ring, behind))]
        else:
            hops += [(across, 0, 32, chip(ring, ahead)), (across, 0, 32, chip(ring, behind))]
            hops += [(back, 32, 32, chip(1 - ring, x)), (front, 32, 32, chip(1 - ring, x))]
        for owner, start, size, to in hops:
            passed = rows_from(buffer, owner, start, size)
            remote(passed, passed, ssem, rsem, to)

    def third_round(buffer, ssem, rsem):
        passed = rows_from(buffer, 4 * ring + (x + 2) % 4, 32, 32)
        remote(passed, passed, ssem, rsem, chip(1 - ring, x))
        passed = rows_from(buffer, 4 * (1 - ring) + behind, 0, 16)
        remote(passed, passed, ssem, rsem, chip(ring, ahead))
        passed = rows_from(buffer, 4 * (1 - ring) + ahead, 16, 16)
        remote(passed, passed, ssem, rsem, chip(ring, behind))

    def x_half(slots, count, owner, which):
        rows = pl.ds(pl.multiple_of(16 * owner, 16), 16)
        return xall.at[pl.ds(slots, count), rows, 256 * which : 256 * which + 256]

    def fetch(src, dst, index):
        copy = pltpu.make_async_copy(src, dst, local.at[index])
        copy.start()
        return copy

    own_fields = fetch(fields_ref, cells, 0)
    barrier = pltpu.get_barrier_semaphore()

    def greet(to):
        pl.semaphore_signal(barrier, inc=1, device_id=to, device_id_type=MESH)

    @pl.loop(1, 16)
    def _(d):
        greet(((c + d) % 16, s))

    @pl.loop(1, 8)
    def _(d):
        greet((c, (s + 4 * d) % SPACE))

    for d in range(1, 4):
        greet((c, 4 * z + (part + d) % 4))
    greet((c, side))
    greet((2 * k + other, side))
    greet(((2 * k + 15) % 16, side))
    greet(((2 * k + 2) % 16, side))

    own_filters = fetch(filters_in, filters, 1)
    own_stem = fetch(stem_in, stem_ref, 2)
    own_mi = fetch(mi_ref, mi_all.at[own_rows64], 3)
    own_mo = fetch(mo_ref, mo_all.at[own_rows64], 4)
    rest = [(sb_in, sb_ref), (eb_in, eb_ref), (gn_in, gn_ref), (nb_in, nb_ref), (mb_in, mb_ref), (ob_in, ob_ref)]
    own_rest = [fetch(src, dst, 5 + i) for i, (src, dst) in enumerate(rest)]

    source = lax.broadcasted_iota(jnp.int32, (640, 256), 0)
    target = lax.broadcasted_iota(jnp.int32, (640, 256), 1)
    target = target % 128 + target // 128 * 80 - (source % 32 + 5) * 20 - source // 32
    order = lax.broadcasted_iota(jnp.int32, (32, 32), 0)
    order = 4 * (order % 8) + order // 8 == lax.broadcasted_iota(jnp.int32, (32, 32), 1)
    own_fields.wait()
    grid = jnp.concatenate([cells[i] for i in range(20)], axis=1)
    grid = jnp.dot(order.astype(BF16), grid, preferred_element_type=F32).astype(BF16)
    for pair in range(5):
        chosen = (target == -160 * pair).astype(BF16)
        window = jnp.dot(grid, chosen, preferred_element_type=F32).astype(BF16)
        aext[2 * pair] = window[:, :128]
        aext[2 * pair + 1] = window[:, 128:]

    pl.semaphore_wait(barrier, 29)

    edge = pl.ds(pl.multiple_of(16 * core, 16), 16)
    below = (k + 2 * core + CHIPS - 1) % CHIPS
    remote(aext.at[pl.ds(4 * other, 5)], gc.at[:, core], halo_send.at[0], halo_recv.at[0], partner)
    for to in range(2):
        remote(
            aext.at[pl.ds(4 * to, 5), edge],
            rv.at[other],
            halo_send.at[1 + to],
            halo_recv.at[1 + other],
            (2 * below + to, s),
        )
    for to in range(2):
        away = right if to == 0 else left
        side_slots = slice(8 - 8 * to, 10 - 8 * to)
        remote(
            aext.at[side_slots], rh.at[core], halo_send.at[3 + to], halo_recv.at[3 + core], (2 * k + to, away)
        )
        remote(
            aext.at[side_slots, edge],
            rd.at[other],
            halo_send.at[5 + to],
            halo_recv.at[5 + other],
            (2 * below + to, away),
        )
    first_round(mi_ref, mi_all, send.at[1], recv.at[1])

    spot = lax.broadcasted_iota(jnp.int32, (32, 128), 1)
    repeat = (spot % 32 == lax.broadcasted_iota(jnp.int32, (32, 128), 0)).astype(BF16)
    cell = lax.broadcasted_iota(jnp.int32, (20, 128), 1) // 32
    own_stem.wait()
    for copy in own_rest:
        copy.wait()
    taps[...] = jnp.zeros((384, 128), F32)
    for row in range(3):
        tiled = [jnp.dot(stem_ref[row, i], repeat, preferred_element_type=F32) for i in range(3)]
        for column in range(6):
            value = jnp.zeros((20, 128), F32)
            for i in range(3):
                if 0 <= column - i < 4:
                    value = jnp.where(cell == column - i, tiled[i], value)
            start = 128 * row + 20 * column
            taps[start : start + 20] = value
    stem_bias = jnp.concatenate([sb_ref[...]] * 4, axis=1)
    own_filters.wait()
    for row in range(4):
        for column in range(4):
            pieces = []
            for b in range(2):
                for a in range(2):
                    i, j = 4 * a + row - 1, 4 * b + column - 1
                    pieces.append(filters[i, j] if min(i, j) >= 0 else jnp.zeros((32, 64), BF16))
            start = 32 * (4 * row + column)
            wall[core, start : start + 32] = jnp.concatenate(pieces, axis=1)
    remote(wall.at[core], wall.at[core], send.at[0], recv.at[0], partner)

    gc[:, core] = aext[pl.ds(4 * core, 5)]
    at_left = jnp.logical_and(core == 0, s > 0)
    at_right = jnp.logical_and(core == 1, s < SPACE - 1)
    outside = jnp.logical_and(core == 0, s == 0)
    rows16 = pl.ds(pl.multiple_of(16 * k, 16), 16)
    tap = taps[...].astype(BF16)

    def sides(ref, half, j):
        first = jnp.where(at_left, ref[half, j].astype(F32), 0.0)
        return first + jnp.where(at_right, ref[half, 0].astype(F32), 0.0) if j else first

    def stem_of(slots, count, at_side):
        height = 16 * count
        blocks = [gc[slots + j, half].astype(F32) for j in range(count) for half in range(2)]
        beyond = []
        for half, inside in ((0, k > 0), (1, k < CHIPS - 1)):
            slabs = []
            for j in range(count):
                value = rv[half, slots + j].astype(F32)
                if at_side:
                    value = value + sides(rd, half, j)
                value = jnp.where(inside, value, 0.0)
                value = value[15:16] if half == 0 else value[0:1]
                slabs.append(jnp.broadcast_to(value, (16, 128)))
            beyond.append(jnp.concatenate(slabs, axis=0))
        if at_side:
            blocks = [block + sides(rh, i % 2, i // 2) for i, block in enumerate(blocks)]
        grid = [jnp.concatenate([block[8 * row : 8 * row + 8] for block in blocks], axis=0) for row in range(4)]
        index = lax.broadcasted_iota(jnp.int32, (height, 128), 0)
        before = jnp.where(index % 16 == 0, beyond[0], pltpu.roll(grid[3], 1, axis=0))
        after = jnp.where(index % 16 == 15, beyond[1], pltpu.roll(grid[0], height - 1, axis=0))
        lines = [line.astype(BF16) for line in (before, *grid, after)]
        for row in range(4):
            patches = jnp.concatenate(lines[row : row + 3], axis=1)
            stem = gelu(jnp.dot(patches, tap, preferred_element_type=F32) + stem_bias)
            if at_side:
                stem = jnp.where(jnp.logical_or(index >= 16, jnp.logical_not(outside)), stem, 0.0)
            stem = stem.reshape(count, 16, 128).astype(BF16)
            xall[pl.ds(slots, count), rows16, 128 * row : 128 * row + 128] = stem
        mine = xall.at[pl.ds(slots, count), rows16]
        return mine

    inner, outer = 2 - 2 * core, 3 * core
    wait(gc.at[:, core], halo_recv.at[0])
    for i in range(2):
        wait(rv.at[i], halo_recv.at[1 + i])
    mine = stem_of(inner, 3, False)
    spread(mine, mine, send.at[2], recv.at[2])
    for i in range(2):
        wait(rh.at[i], halo_recv.at[3 + i])
        wait(rd.at[i], halo_recv.at[5 + i])
    mine = stem_of(outer, 2, True)
    spread(mine, mine, send.at[16], recv.at[16])

    wait(xall.at[:3, :80], recv.at[2])
    forward(functools.partial(x_half, inner, 3), send.at[9], recv.at[9])
    wait(xall.at[:2, :80], recv.at[16])
    forward(functools.partial(x_half, outer, 2), send.at[17], recv.at[17])
    wait(mi_all.at[:192], recv.at[1])
    second_round(mi_all, send.at[10], recv.at[10], False)

    wait(wall.at[0], recv.at[0])
    wait(xall.at[:3, :32], recv.at[9])
    wait(xall.at[:2, :32], recv.at[17])
    tokens = xall[...].reshape(640, 512)
    low = lax.broadcasted_iota(jnp.int32, (1, 128), 1) < 64
    bias_row = eb_ref[pl.ds(k, 1), :]
    bias_rows = [jnp.where(low, 0.0, pltpu.roll(bias_row, 64, axis=1)), jnp.where(low, 0.0, bias_row)]
    lane = lax.broadcasted_iota(jnp.int32, (64, 128), 1)
    sums = [[0.0, 0.0] for _ in range(4)]
    for half in range(2):
        terms = jnp.dot(tokens, wall[half], preferred_element_type=F32)
        both = terms[128:640, 128:256] + terms[0:512, 0:128] + bias_rows[half]
        for column in range(4):
            turned = both[128 * column : 128 * column + 128].T
            shifted = pltpu.roll(turned[0:64], 1, axis=1)
            value = (turned[64:128] + jnp.where(lane > 0, shifted, 0.0)).astype(BF16)
            eh[core, 64 * half : 64 * half + 64, 128 * column : 128 * column + 128] = value
            wide = value.astype(F32)
            sums[column][0] += jnp.sum(wide, axis=0, keepdims=True)
            sums[column][1] += jnp.sum(wide * wide, axis=0, keepdims=True)
    for column in range(4):
        for kind in range(2):
            st[c, kind : kind + 1, 128 * column : 128 * column + 128] = sums[column][kind]

    @pl.loop(1, 16)
    def _(d):
        remote(st.at[c], st.at[c], send.at[4], recv.at[4], ((c + d) % 16, s))

    remote(eh.at[core], eh.at[core], send.at[5], recv.at[5], partner)

    wait(mi_all.at[:192], recv.at[10])
    third_round(mi_all, send.at[13], recv.at[13])
    gain = jnp.broadcast_to(gn_ref[pl.ds(k, 1), :], (128, 128)).T
    offset = jnp.broadcast_to(nb_ref[pl.ds(k, 1), :], (128, 128)).T
    gain = jnp.concatenate([gain] * 4, axis=1)
    offset = jnp.concatenate([offset] * 4, axis=1)
    wait(st.at[:15], recv.at[4])
    wait(eh.at[0], recv.at[5])
    first_round(mo_ref, mo_all, send.at[3], recv.at[3])
    normed = []
    for half in range(2):
        total = st[half]
        for j in range(1, CHIPS):
            total = total + st[2 * j + half]
        average = total[0:1] * (1.0 / 1024)
        variance = total[1:2] * (1.0 / 1024) - average * average
        scale = lax.rsqrt(variance + 1e-05)
        value = (eh[half].astype(F32) - average) * scale * gain + offset
        normed.append(value.astype(BF16))
    normed = jnp.concatenate(normed, axis=1)

    own_mi.wait()
    wait(mi_all.at[:64], recv.at[13])
    summed = lax.dot_general(normed, mi_all[...], (((1,), (1,)), ((), ())), preferred_element_type=F32)
    summed = summed.astype(BF16)
    for band in range(8):
        hs[band] = summed[16 * band : 16 * band + 16]

    @pl.loop(1, 8)
    def _(d):
        to = (z + d) % 8
        remote(hs.at[to], rs.at[z], send.at[6], recv.at[6], (c, 4 * to + part))

    wait(mo_all.at[:192], recv.at[3])
    second_round(mo_all, send.at[11], recv.at[11], True)
    rs[z] = hs[z]
    wait(rs.at[:7], recv.at[6])
    total = rs[0].astype(F32)
    for source in range(1, 8):
        total = total + rs[source].astype(F32)
    quarter[part] = total.astype(BF16)
    for d in range(1, 4):
        to = 4 * z + (part + d) % 4
        remote(quarter.at[part], quarter.at[part], send.at[7], recv.at[7], (c, to))
    wait(quarter.at[:3], recv.at[7])
    total = quarter[0].astype(F32)
    for source in range(1, 4):
        total = total + quarter[source].astype(F32)
    rows = mb_ref[...]
    turned = pltpu.roll(rows, 64, axis=1)
    ours = jnp.where(low, jnp.where(core == 0, rows, turned), 0.0)
    theirs = jnp.where(low, 0.0, jnp.where(core == 0, turned, rows))
    hidden_bias = [ours[2 * i : 2 * i + 1] + theirs[2 * i + 1 : 2 * i + 2] for i in range(4)]
    total = total + jnp.concatenate(hidden_bias, axis=1)
    act[z] = gelu(total).astype(BF16)

    @pl.loop(1, 8)
    def _(d):
        remote(act.at[z], act.at[z], send.at[12], recv.at[12], (c, (s + 4 * d) % SPACE))

    wait(mo_all.at[:192], recv.at[11])
    third_round(mo_all, send.at[14], recv.at[14])
    own_mo.wait()
    wait(act.at[:7], recv.at[12])
    wait(mo_all.at[:64], recv.at[14])

    def rows_of(which):
        return act[pl.ds(4 * which, 4)].reshape(64, 512)

    others = rows_of(other)
    for half in range(2):
        part_out = jnp.dot(others, mo_all[:, 512 * half : 512 * half + 512], preferred_element_type=F32)
        po[half] = part_out.astype(BF16)
        remote(po.at[half], pr.at[half], send.at[8 + 7 * half], recv.at[8 + 7 * half], partner)
    mine = jnp.dot(rows_of(core), mo_all[...], preferred_element_type=F32) + ob_ref[...]
    residual = [eh[half, pl.ds(pl.multiple_of(64 * core, 64), 64), :].astype(F32) for half in range(2)]
    mine = mine + jnp.concatenate(residual, axis=1)
    for half in range(2):
        wait(pr.at[half], recv.at[8 + 7 * half])
        span = slice(512 * half, 512 * half + 512)
        out_ref[:, span] = (mine[:, span] + pr[half].astype(F32)).astype(BF16)

    wait(gc.at[:, core], halo_send.at[0])
    for i in range(2):
        wait(rv.at[i], halo_send.at[1 + i])
        wait(rh.at[i], halo_send.at[3 + i])
        wait(rd.at[i], halo_send.at[5 + i])
    wait(wall.at[0], send.at[0])
    wait(mi_all.at[:192], send.at[1])
    wait(xall.at[:3, :80], send.at[2])
    wait(xall.at[:2, :80], send.at[16])
    wait(mo_all.at[:192], send.at[3])
    wait(st.at[:15], send.at[4])
    wait(eh.at[0], send.at[5])
    wait(rs.at[:7], send.at[6])
    wait(quarter.at[:3], send.at[7])
    wait(po.at[0], send.at[8])
    wait(po.at[1], send.at[15])
    wait(xall.at[:3, :32], send.at[9])
    wait(xall.at[:2, :32], send.at[17])
    wait(mi_all.at[:192], send.at[10])
    wait(mo_all.at[:192], send.at[11])
    wait(mi_all.at[:64], send.at[13])
    wait(mo_all.at[:64], send.at[14])
    wait(act.at[:7], send.at[12])


def shards(
    fields,
    stem_weight,
    stem_bias,
    embed_weight,
    embed_bias,
    norm_gain,
    norm_bias,
    mix_in,
    mix_in_bias,
    mix_out,
    mix_out_bias,
):
    out = pl.pallas_call(
        kernel,
        out_shape=pltpu.VMEM((64, 1024), BF16),
        in_specs=[pl.BlockSpec(memory_space=pl.ANY)] * 11,
        out_specs=pl.BlockSpec(memory_space=pltpu.VMEM),
        scratch_shapes=[
            pltpu.VMEM((20, 32, 32), BF16),
            pltpu.VMEM((7, 7, 32, 64), BF16),
            pltpu.VMEM((3, 3, 20, 32), BF16),
            pltpu.VMEM((1, 32), F32),
            pltpu.VMEM((8, 128), F32),
            pltpu.VMEM((8, 128), F32),
            pltpu.VMEM((8, 128), F32),
            pltpu.VMEM((8, 128), F32),
            pltpu.VMEM((1, 1024), F32),
            pltpu.VMEM((10, 32, 128), BF16),
            pltpu.VMEM((384, 128), F32),
            pltpu.VMEM((5, 2, 32, 128), BF16),
            pltpu.VMEM((2, 5, 16, 128), BF16),
            pltpu.VMEM((2, 2, 32, 128), BF16),
            pltpu.VMEM((2, 2, 16, 128), BF16),
            pltpu.VMEM((5, 128, 512), BF16),
            pltpu.VMEM((2, 512, 256), BF16),
            pltpu.VMEM((2, 128, 512), BF16),
            pltpu.VMEM((16, 2, 512), F32),
            pltpu.VMEM((512, 1024), BF16),
            pltpu.VMEM((512, 1024), BF16),
            pltpu.VMEM((8, 16, 512), BF16),
            pltpu.VMEM((8, 16, 512), BF16),
            pltpu.VMEM((4, 16, 512), BF16),
            pltpu.VMEM((8, 16, 512), BF16),
            pltpu.VMEM((2, 64, 512), BF16),
            pltpu.VMEM((2, 64, 512), BF16),
            pltpu.SemaphoreType.DMA((7,)),
            pltpu.SemaphoreType.DMA((7,)),
            pltpu.SemaphoreType.DMA((18,)),
            pltpu.SemaphoreType.DMA((18,)),
            pltpu.SemaphoreType.DMA((11,)),
        ],
        compiler_params=pltpu.CompilerParams(collective_id=0, has_side_effects=True, vmem_limit_bytes=58 * 2**20),
    )(
        stem_weight,
        stem_bias[None],
        embed_bias.reshape(8, 128),
        norm_gain.reshape(8, 128),
        norm_bias.reshape(8, 128),
        mix_in_bias.reshape(8, 128),
        mix_out_bias[None],
        embed_weight,
        fields[0],
        mix_in.T,
        mix_out,
    )
    return out[None]


def solution(mesh):
    placed = (
        P(None, None, "chan", "space"),
        P(),
        P(),
        P(None, None, None, "chan"),
        P(),
        P(),
        P(),
        P("space", "chan"),
        P(),
        P("chan", "space"),
        P("space"),
    )
    return jax.shard_map(
        shards, mesh=mesh, in_specs=placed, out_specs=P(None, "chan", "space"), check_vma=False
    )
```

```python
import functools

import jax
import jax.numpy as jnp
from jax import lax
from jax.experimental import pallas as pl
from jax.experimental.pallas import tpu as pltpu
from jax.sharding import PartitionSpec as P

MESH = pl.DeviceIdType.MESH
CHIPS = 8
SPACE = 32
F32 = jnp.float32
BF16 = jnp.bfloat16


def gelu(x):
    return 0.5 * x * (1.0 + lax.erf(x * 0.7071067811865476))


def kernel(
    stem_in,
    sb_in,
    eb_in,
    gn_in,
    nb_in,
    mb_in,
    ob_in,
    filters_in,
    fields_ref,
    mi_ref,
    mo_ref,
    out_ref,
    cells,
    filters,
    stem_ref,
    sb_ref,
    eb_ref,
    gn_ref,
    nb_ref,
    mb_ref,
    ob_ref,
    aext,
    taps,
    gc,
    rv,
    rh,
    rd,
    xall,
    wall,
    eh,
    st,
    mi_all,
    mo_all,
    hs,
    rs,
    quarter,
    act,
    po,
    pr,
    halo_send,
    halo_recv,
    send,
    recv,
    local,
    meet,
):
    c, s = lax.axis_index("chan"), lax.axis_index("space")
    k, core = c // 2, c % 2
    other = 1 - core
    partner = (2 * k + other, s)
    z, part = s // 4, s % 4
    right, left = (s + 1) % SPACE, (s + SPACE - 1) % SPACE
    side = jnp.where(core == 0, left, right)

    def remote(src, dst, ssem, rsem, to):
        copy = pltpu.make_async_remote_copy(
            src_ref=src, dst_ref=dst, send_sem=ssem, recv_sem=rsem, device_id=to, device_id_type=MESH
        )
        copy.start()

    def wait(ref, sem):
        pltpu.make_async_copy(ref, ref, sem).wait()

    ring, x = k // 4, k % 4
    ahead, behind = (x + 1) % 4, (x + 3) % 4

    def chip(r, i):
        return (2 * (4 * r + i) + core, s)

    near = [chip(ring, ahead), chip(ring, behind), chip(1 - ring, x), chip(1 - ring, ahead), chip(1 - ring, behind)]

    far = [chip(1 - ring, (x + 2) % 4), chip(ring, (x + 2) % 4)]

    def spread(src, dst, ssem, rsem, everyone=False):
        for to in far + near[::-1] if everyone else near:
            remote(src, dst, ssem, rsem, to)

    def forward(half, ssem, rsem):
        for r in range(2):
            passed = half(4 * r + behind, 0)
            remote(passed, passed, ssem, rsem, chip(ring, ahead))
            passed = half(4 * r + ahead, 1)
            remote(passed, passed, ssem, rsem, chip(ring, behind))

    def rows_from(buffer, owner, start, size):
        return buffer.at[pl.ds(pl.multiple_of(64 * owner + start, 16), size)]

    own_rows64 = pl.ds(pl.multiple_of(64 * k, 64), 64)

    def first_round(mine, buffer, ssem, rsem):
        for to in (chip(ring, ahead), chip(ring, behind), chip(1 - ring, x)):
            remote(mine, buffer.at[own_rows64], ssem, rsem, to)

    def second_round(buffer, ssem, rsem, along):
        across, back, front = 4 * (1 - ring) + x, 4 * ring + behind, 4 * ring + ahead
        hops = [(back, 0, 32, chip(ring, ahead)), (front, 32, 32, chip(ring, behind))]
        if along:
            hops += [(across, 0, 64, chip(ring, ahead)), (across, 0, 64, chip(ring, behind))]
        else:
            hops += [(across, 0, 32, chip(ring, ahead)), (across, 0, 32, chip(ring, behind))]
            hops += [(back, 32, 32, chip(1 - ring, x)), (front, 32, 32, chip(1 - ring, x))]
        for owner, start, size, to in hops:
            passed = rows_from(buffer, owner, start, size)
            remote(passed, passed, ssem, rsem, to)

    def third_round(buffer, ssem, rsem):
        passed = rows_from(buffer, 4 * ring + (x + 2) % 4, 32, 32)
        remote(passed, passed, ssem, rsem, chip(1 - ring, x))
        passed = rows_from(buffer, 4 * (1 - ring) + behind, 0, 16)
        remote(passed, passed, ssem, rsem, chip(ring, ahead))
        passed = rows_from(buffer, 4 * (1 - ring) + ahead, 16, 16)
        remote(passed, passed, ssem, rsem, chip(ring, behind))

    def x_half(slots, count, owner, which):
        rows = pl.ds(pl.multiple_of(16 * owner, 16), 16)
        return xall.at[pl.ds(slots, count), rows, 256 * which : 256 * which + 256]

    def fetch(src, dst, index):
        copy = pltpu.make_async_copy(src, dst, local.at[index])
        copy.start()
        return copy

    own_fields = fetch(fields_ref, cells, 0)
    barrier = pltpu.get_barrier_semaphore()

    def greet(to):
        pl.semaphore_signal(barrier, inc=1, device_id=to, device_id_type=MESH)

    @pl.loop(1, 16)
    def _(d):
        greet(((c + d) % 16, s))

    def over_z(d):
        return (c, (s + 4 * d) % SPACE)

    def over_parts(d):
        return (c, 4 * z + (part + d) % 4)

    for d in (1, 7):
        greet(over_z(d))
    for d in (1, 3):
        greet(over_parts(d))
    greet((c, side))
    greet((2 * k + other, side))
    greet(((2 * k + 15) % 16, side))
    greet(((2 * k + 2) % 16, side))

    own_filters = fetch(filters_in, filters, 1)
    own_stem = fetch(stem_in, stem_ref, 2)
    own_mi = fetch(mi_ref, mi_all.at[own_rows64], 3)
    own_mo = fetch(mo_ref, mo_all.at[own_rows64], 4)
    rest = [(sb_in, sb_ref), (eb_in, eb_ref), (gn_in, gn_ref), (nb_in, nb_ref), (mb_in, mb_ref), (ob_in, ob_ref)]
    own_rest = [fetch(src, dst, 5 + i) for i, (src, dst) in enumerate(rest)]

    source = lax.broadcasted_iota(jnp.int32, (640, 256), 0)
    target = lax.broadcasted_iota(jnp.int32, (640, 256), 1)
    target = target % 128 + target // 128 * 80 - (source % 32 + 5) * 20 - source // 32
    order = lax.broadcasted_iota(jnp.int32, (32, 32), 0)
    order = 4 * (order % 8) + order // 8 == lax.broadcasted_iota(jnp.int32, (32, 32), 1)
    own_fields.wait()
    grid = jnp.concatenate([cells[i] for i in range(20)], axis=1)
    grid = jnp.dot(order.astype(BF16), grid, preferred_element_type=F32).astype(BF16)
    for pair in range(5):
        chosen = (target == -160 * pair).astype(BF16)
        window = jnp.dot(grid, chosen, preferred_element_type=F32).astype(BF16)
        aext[2 * pair] = window[:, :128]
        aext[2 * pair + 1] = window[:, 128:]

    pl.semaphore_wait(barrier, 23)

    def tell(index, to):
        pl.semaphore_signal(meet.at[index], inc=1, device_id=to, device_id_type=MESH)


    edge = pl.ds(pl.multiple_of(16 * core, 16), 16)
    below = (k + 2 * core + CHIPS - 1) % CHIPS
    down_here, up_here = k > 0, k < CHIPS - 1
    vertical = jnp.where(core == 0, down_here, up_here)
    for to in range(2):
        away = right if to == 0 else left
        within = s < SPACE - 1 if to == 0 else s > 0
        side_slots = slice(8 - 8 * to, 10 - 8 * to)

        @pl.when(within)
        def _(to=to, away=away, side_slots=side_slots):
            remote(
                aext.at[side_slots],
                rh.at[core],
                halo_send.at[3 + to],
                halo_recv.at[3 + core],
                (2 * k + to, away),
            )

        @pl.when(jnp.logical_and(within, vertical))
        def _(to=to, away=away, side_slots=side_slots):
            remote(
                aext.at[side_slots, edge],
                rd.at[other],
                halo_send.at[5 + to],
                halo_recv.at[5 + other],
                (2 * below + to, away),
            )

    remote(aext.at[pl.ds(4 * other, 5)], gc.at[:, core], halo_send.at[0], halo_recv.at[0], partner)

    @pl.when(vertical)
    def _():
        for to in range(2):
            remote(
                aext.at[pl.ds(4 * to, 5), edge],
                rv.at[other],
                halo_send.at[1 + to],
                halo_recv.at[1 + other],
                (2 * below + to, s),
            )

    for d in (1, 7):
        tell(0, over_z(d))
    for d in (1, 3):
        tell(1, over_parts(d))
    first_round(mi_ref, mi_all, send.at[1], recv.at[1])

    spot = lax.broadcasted_iota(jnp.int32, (32, 128), 1)
    repeat = (spot % 32 == lax.broadcasted_iota(jnp.int32, (32, 128), 0)).astype(BF16)
    cell = lax.broadcasted_iota(jnp.int32, (20, 128), 1) // 32
    own_stem.wait()
    for copy in own_rest:
        copy.wait()
    taps[...] = jnp.zeros((384, 128), F32)
    for row in range(3):
        tiled = [jnp.dot(stem_ref[row, i], repeat, preferred_element_type=F32) for i in range(3)]
        for column in range(6):
            value = jnp.zeros((20, 128), F32)
            for i in range(3):
                if 0 <= column - i < 4:
                    value = jnp.where(cell == column - i, tiled[i], value)
            start = 128 * row + 20 * column
            taps[start : start + 20] = value
    stem_bias = jnp.concatenate([sb_ref[...]] * 4, axis=1)
    own_filters.wait()
    for row in range(4):
        for column in range(4):
            pieces = []
            for b in range(2):
                for a in range(2):
                    i, j = 4 * a + row - 1, 4 * b + column - 1
                    pieces.append(filters[i, j] if min(i, j) >= 0 else jnp.zeros((32, 64), BF16))
            start = 32 * (4 * row + column)
            wall[core, start : start + 32] = jnp.concatenate(pieces, axis=1)
    remote(wall.at[core], wall.at[core], send.at[0], recv.at[0], partner)

    gc[:, core] = aext[pl.ds(4 * core, 5)]
    at_left = jnp.logical_and(core == 0, s > 0)
    at_right = jnp.logical_and(core == 1, s < SPACE - 1)
    outside = jnp.logical_and(core == 0, s == 0)
    rows16 = pl.ds(pl.multiple_of(16 * k, 16), 16)
    tap = taps[...].astype(BF16)

    def sides(ref, half, j):
        first = jnp.where(at_left, ref[half, j].astype(F32), 0.0)
        return first + jnp.where(at_right, ref[half, 0].astype(F32), 0.0) if j else first

    def stem_of(slots, count, at_side):
        height = 16 * count
        blocks = [gc[slots + j, half].astype(F32) for j in range(count) for half in range(2)]
        beyond = []
        for half, inside in ((0, k > 0), (1, k < CHIPS - 1)):
            slabs = []
            for j in range(count):
                value = rv[half, slots + j].astype(F32)
                if at_side:
                    value = value + sides(rd, half, j)
                value = jnp.where(inside, value, 0.0)
                value = value[15:16] if half == 0 else value[0:1]
                slabs.append(jnp.broadcast_to(value, (16, 128)))
            beyond.append(jnp.concatenate(slabs, axis=0))
        if at_side:
            blocks = [block + sides(rh, i % 2, i // 2) for i, block in enumerate(blocks)]
        grid = [jnp.concatenate([block[8 * row : 8 * row + 8] for block in blocks], axis=0) for row in range(4)]
        index = lax.broadcasted_iota(jnp.int32, (height, 128), 0)
        before = jnp.where(index % 16 == 0, beyond[0], pltpu.roll(grid[3], 1, axis=0))
        after = jnp.where(index % 16 == 15, beyond[1], pltpu.roll(grid[0], height - 1, axis=0))
        lines = [line.astype(BF16) for line in (before, *grid, after)]
        for row in range(4):
            patches = jnp.concatenate(lines[row : row + 3], axis=1)
            stem = gelu(jnp.dot(patches, tap, preferred_element_type=F32) + stem_bias)
            if at_side:
                stem = jnp.where(jnp.logical_or(index >= 16, jnp.logical_not(outside)), stem, 0.0)
            stem = stem.reshape(count, 16, 128).astype(BF16)
            xall[pl.ds(slots, count), rows16, 128 * row : 128 * row + 128] = stem
        mine = xall.at[pl.ds(slots, count), rows16]
        return mine

    inner, outer = 2 - 2 * core, 3 * core
    wait(gc.at[:, core], halo_recv.at[0])
    for i, here in ((0, down_here), (1, up_here)):

        @pl.when(here)
        def _(i=i):
            wait(rv.at[i], halo_recv.at[1 + i])

    mine = stem_of(inner, 3, False)
    spread(mine, mine, send.at[2], recv.at[2])
    beside = jnp.logical_or(at_left, at_right)
    for i, here in ((0, down_here), (1, up_here)):

        @pl.when(beside)
        def _(i=i):
            wait(rh.at[i], halo_recv.at[3 + i])

        @pl.when(jnp.logical_and(beside, here))
        def _(i=i):
            wait(rd.at[i], halo_recv.at[5 + i])

    mine = stem_of(outer, 2, True)
    spread(mine, mine, send.at[16], recv.at[16], True)

    pl.semaphore_wait(meet.at[0], 2)
    pl.semaphore_wait(meet.at[1], 2)
    for d in (2, 6):
        tell(2, over_z(d))
    wait(xall.at[:3, :80], recv.at[2])
    forward(functools.partial(x_half, inner, 3), send.at[9], recv.at[9])
    wait(mi_all.at[:192], recv.at[1])
    second_round(mi_all, send.at[10], recv.at[10], False)

    wait(wall.at[0], recv.at[0])
    wait(xall.at[:3, :32], recv.at[9])
    wait(xall.at[:2, :112], recv.at[16])
    tokens = xall[...].reshape(640, 512)
    low = lax.broadcasted_iota(jnp.int32, (1, 128), 1) < 64
    bias_row = eb_ref[pl.ds(k, 1), :]
    bias_rows = [jnp.where(low, 0.0, pltpu.roll(bias_row, 64, axis=1)), jnp.where(low, 0.0, bias_row)]
    lane = lax.broadcasted_iota(jnp.int32, (64, 128), 1)
    sums = [[0.0, 0.0] for _ in range(4)]
    for half in range(2):
        terms = jnp.dot(tokens, wall[half], preferred_element_type=F32)
        both = terms[128:640, 128:256] + terms[0:512, 0:128] + bias_rows[half]
        for column in range(4):
            turned = both[128 * column : 128 * column + 128].T
            shifted = pltpu.roll(turned[0:64], 1, axis=1)
            value = (turned[64:128] + jnp.where(lane > 0, shifted, 0.0)).astype(BF16)
            eh[core, 64 * half : 64 * half + 64, 128 * column : 128 * column + 128] = value
            wide = value.astype(F32)
            sums[column][0] += jnp.sum(wide, axis=0, keepdims=True)
            sums[column][1] += jnp.sum(wide * wide, axis=0, keepdims=True)
    for column in range(4):
        for kind in range(2):
            st[c, kind : kind + 1, 128 * column : 128 * column + 128] = sums[column][kind]

    @pl.loop(1, 16)
    def _(d):
        remote(st.at[c], st.at[c], send.at[4], recv.at[4], ((c + d) % 16, s))

    remote(eh.at[core], eh.at[core], send.at[5], recv.at[5], partner)

    wait(mi_all.at[:192], recv.at[10])
    third_round(mi_all, send.at[13], recv.at[13])
    gain = jnp.broadcast_to(gn_ref[pl.ds(k, 1), :], (128, 128)).T
    offset = jnp.broadcast_to(nb_ref[pl.ds(k, 1), :], (128, 128)).T
    gain = jnp.concatenate([gain] * 4, axis=1)
    offset = jnp.concatenate([offset] * 4, axis=1)
    wait(st.at[:15], recv.at[4])
    wait(eh.at[0], recv.at[5])
    first_round(mo_ref, mo_all, send.at[3], recv.at[3])
    normed = []
    for half in range(2):
        total = st[half]
        for j in range(1, CHIPS):
            total = total + st[2 * j + half]
        average = total[0:1] * (1.0 / 1024)
        variance = total[1:2] * (1.0 / 1024) - average * average
        scale = lax.rsqrt(variance + 1e-05)
        value = (eh[half].astype(F32) - average) * scale * gain + offset
        normed.append(value.astype(BF16))
    normed = jnp.concatenate(normed, axis=1)

    own_mi.wait()
    wait(mi_all.at[:64], recv.at[13])
    summed = lax.dot_general(normed, mi_all[...], (((1,), (1,)), ((), ())), preferred_element_type=F32)
    summed = summed.astype(BF16)
    for band in range(8):
        hs[band] = summed[16 * band : 16 * band + 16]

    pl.semaphore_wait(meet.at[2], 2)
    for d in (4, 3, 5, 2, 6, 1, 7):
        remote(hs.at[(z + d) % 8], rs.at[z], send.at[6], recv.at[6], over_z(d))

    rs[z] = hs[z]
    wait(rs.at[:7], recv.at[6])
    total = rs[0].astype(F32)
    for source in range(1, 8):
        total = total + rs[source].astype(F32)
    quarter[part] = total.astype(BF16)
    for d in (2, 1, 3):
        remote(quarter.at[part], quarter.at[part], send.at[7], recv.at[7], over_parts(d))
    wait(mo_all.at[:192], recv.at[3])
    second_round(mo_all, send.at[11], recv.at[11], True)
    wait(quarter.at[:3], recv.at[7])
    total = quarter[0].astype(F32)
    for source in range(1, 4):
        total = total + quarter[source].astype(F32)
    rows = mb_ref[...]
    turned = pltpu.roll(rows, 64, axis=1)
    ours = jnp.where(low, jnp.where(core == 0, rows, turned), 0.0)
    theirs = jnp.where(low, 0.0, jnp.where(core == 0, turned, rows))
    hidden_bias = [ours[2 * i : 2 * i + 1] + theirs[2 * i + 1 : 2 * i + 2] for i in range(4)]
    total = total + jnp.concatenate(hidden_bias, axis=1)
    act[z] = gelu(total).astype(BF16)

    for d in (4, 3, 5, 2, 6, 1, 7):
        remote(act.at[z], act.at[z], send.at[12], recv.at[12], over_z(d))

    wait(mo_all.at[:192], recv.at[11])
    third_round(mo_all, send.at[14], recv.at[14])
    own_mo.wait()
    wait(act.at[:7], recv.at[12])
    wait(mo_all.at[:64], recv.at[14])

    def rows_of(which):
        return act[pl.ds(4 * which, 4)].reshape(64, 512)

    others = rows_of(other)
    for half in range(2):
        part_out = jnp.dot(others, mo_all[:, 512 * half : 512 * half + 512], preferred_element_type=F32)
        po[half] = part_out.astype(BF16)
        remote(po.at[half], pr.at[half], send.at[8 + 7 * half], recv.at[8 + 7 * half], partner)
    mine = jnp.dot(rows_of(core), mo_all[...], preferred_element_type=F32) + ob_ref[...]
    residual = [eh[half, pl.ds(pl.multiple_of(64 * core, 64), 64), :].astype(F32) for half in range(2)]
    mine = mine + jnp.concatenate(residual, axis=1)
    for half in range(2):
        wait(pr.at[half], recv.at[8 + 7 * half])
        span = slice(512 * half, 512 * half + 512)
        out_ref[:, span] = (mine[:, span] + pr[half].astype(F32)).astype(BF16)

    wait(gc.at[:, core], halo_send.at[0])
    for to in range(2):
        within = s < SPACE - 1 if to == 0 else s > 0

        @pl.when(vertical)
        def _(to=to):
            wait(rv.at[to], halo_send.at[1 + to])

        @pl.when(within)
        def _(to=to):
            wait(rh.at[to], halo_send.at[3 + to])

        @pl.when(jnp.logical_and(within, vertical))
        def _(to=to):
            wait(rd.at[to], halo_send.at[5 + to])

    wait(wall.at[0], send.at[0])
    wait(mi_all.at[:192], send.at[1])
    wait(xall.at[:3, :80], send.at[2])
    wait(xall.at[:2, :112], send.at[16])
    wait(mo_all.at[:192], send.at[3])
    wait(st.at[:15], send.at[4])
    wait(eh.at[0], send.at[5])
    wait(rs.at[:7], send.at[6])
    wait(quarter.at[:3], send.at[7])
    wait(po.at[0], send.at[8])
    wait(po.at[1], send.at[15])
    wait(xall.at[:3, :32], send.at[9])
    wait(mi_all.at[:192], send.at[10])
    wait(mo_all.at[:192], send.at[11])
    wait(mi_all.at[:64], send.at[13])
    wait(mo_all.at[:64], send.at[14])
    wait(act.at[:7], send.at[12])


def shards(
    fields,
    stem_weight,
    stem_bias,
    embed_weight,
    embed_bias,
    norm_gain,
    norm_bias,
    mix_in,
    mix_in_bias,
    mix_out,
    mix_out_bias,
):
    out = pl.pallas_call(
        kernel,
        out_shape=pltpu.VMEM((64, 1024), BF16),
        in_specs=[pl.BlockSpec(memory_space=pl.ANY)] * 11,
        out_specs=pl.BlockSpec(memory_space=pltpu.VMEM),
        scratch_shapes=[
            pltpu.VMEM((20, 32, 32), BF16),
            pltpu.VMEM((7, 7, 32, 64), BF16),
            pltpu.VMEM((3, 3, 20, 32), BF16),
            pltpu.VMEM((1, 32), F32),
            pltpu.VMEM((8, 128), F32),
            pltpu.VMEM((8, 128), F32),
            pltpu.VMEM((8, 128), F32),
            pltpu.VMEM((8, 128), F32),
            pltpu.VMEM((1, 1024), F32),
            pltpu.VMEM((10, 32, 128), BF16),
            pltpu.VMEM((384, 128), F32),
            pltpu.VMEM((5, 2, 32, 128), BF16),
            pltpu.VMEM((2, 5, 16, 128), BF16),
            pltpu.VMEM((2, 2, 32, 128), BF16),
            pltpu.VMEM((2, 2, 16, 128), BF16),
            pltpu.VMEM((5, 128, 512), BF16),
            pltpu.VMEM((2, 512, 256), BF16),
            pltpu.VMEM((2, 128, 512), BF16),
            pltpu.VMEM((16, 2, 512), F32),
            pltpu.VMEM((512, 1024), BF16),
            pltpu.VMEM((512, 1024), BF16),
            pltpu.VMEM((8, 16, 512), BF16),
            pltpu.VMEM((8, 16, 512), BF16),
            pltpu.VMEM((4, 16, 512), BF16),
            pltpu.VMEM((8, 16, 512), BF16),
            pltpu.VMEM((2, 64, 512), BF16),
            pltpu.VMEM((2, 64, 512), BF16),
            pltpu.SemaphoreType.DMA((7,)),
            pltpu.SemaphoreType.DMA((7,)),
            pltpu.SemaphoreType.DMA((18,)),
            pltpu.SemaphoreType.DMA((18,)),
            pltpu.SemaphoreType.DMA((11,)),
            pltpu.SemaphoreType.REGULAR((3,)),
        ],
        compiler_params=pltpu.CompilerParams(collective_id=0, has_side_effects=True, vmem_limit_bytes=58 * 2**20),
    )(
        stem_weight,
        stem_bias[None],
        embed_bias.reshape(8, 128),
        norm_gain.reshape(8, 128),
        norm_bias.reshape(8, 128),
        mix_in_bias.reshape(8, 128),
        mix_out_bias[None],
        embed_weight,
        fields[0],
        mix_in.T,
        mix_out,
    )
    return out[None]


def solution(mesh):
    placed = (
        P(None, None, "chan", "space"),
        P(),
        P(),
        P(None, None, None, "chan"),
        P(),
        P(),
        P(),
        P("space", "chan"),
        P(),
        P("chan", "space"),
        P("space"),
    )
    return jax.shard_map(
        shards, mesh=mesh, in_specs=placed, out_specs=P(None, "chan", "space"), check_vma=False
    )
```

```python
import functools

import jax
import jax.numpy as jnp
from jax import lax
from jax.experimental import pallas as pl
from jax.experimental.pallas import tpu as pltpu
from jax.sharding import PartitionSpec as P

MESH = pl.DeviceIdType.MESH
CHIPS = 8
SPACE = 32
F32 = jnp.float32
BF16 = jnp.bfloat16


def gelu(x):
    return 0.5 * x * (1.0 + lax.erf(x * 0.7071067811865476))


def kernel(
    stem_in,
    sb_in,
    eb_in,
    gn_in,
    nb_in,
    mb_in,
    ob_in,
    filters_in,
    fields_ref,
    mi_ref,
    mo_ref,
    out_ref,
    cells,
    filters,
    stem_ref,
    sb_ref,
    eb_ref,
    gn_ref,
    nb_ref,
    mb_ref,
    ob_ref,
    aext,
    taps,
    gc,
    rv,
    rh,
    rd,
    xall,
    wall,
    eh,
    st,
    mi_all,
    mo_all,
    hs,
    rs,
    quarter,
    act,
    po,
    pr,
    halo_send,
    halo_recv,
    send,
    recv,
    rs_send,
    rs_recv,
    quarter_send,
    quarter_recv,
    act_send,
    act_recv,
    local,
    meet,
):
    c, s = lax.axis_index("chan"), lax.axis_index("space")
    k, core = c // 2, c % 2
    other = 1 - core
    partner = (2 * k + other, s)
    z, part = s // 4, s % 4
    right, left = (s + 1) % SPACE, (s + SPACE - 1) % SPACE
    side = jnp.where(core == 0, left, right)

    def remote(src, dst, ssem, rsem, to):
        copy = pltpu.make_async_remote_copy(
            src_ref=src, dst_ref=dst, send_sem=ssem, recv_sem=rsem, device_id=to, device_id_type=MESH
        )
        copy.start()

    def wait(ref, sem):
        pltpu.make_async_copy(ref, ref, sem).wait()

    ring, x = k // 4, k % 4
    ahead, behind = (x + 1) % 4, (x + 3) % 4

    def chip(r, i):
        return (2 * (4 * r + i) + core, s)

    near = [chip(ring, ahead), chip(ring, behind), chip(1 - ring, x), chip(1 - ring, ahead), chip(1 - ring, behind)]

    far = [chip(1 - ring, (x + 2) % 4), chip(ring, (x + 2) % 4)]

    def spread(src, dst, ssem, rsem, everyone=False):
        for to in far + near[::-1] if everyone else near:
            remote(src, dst, ssem, rsem, to)

    def forward(half, ssem, rsem):
        for r in range(2):
            passed = half(4 * r + behind, 0)
            remote(passed, passed, ssem, rsem, chip(ring, ahead))
            passed = half(4 * r + ahead, 1)
            remote(passed, passed, ssem, rsem, chip(ring, behind))

    def rows_from(buffer, owner, start, size):
        return buffer.at[pl.ds(pl.multiple_of(64 * owner + start, 16), size)]

    own_rows64 = pl.ds(pl.multiple_of(64 * k, 64), 64)

    def first_round(mine, buffer, ssem, rsem):
        for to in (chip(ring, ahead), chip(ring, behind), chip(1 - ring, x)):
            remote(mine, buffer.at[own_rows64], ssem, rsem, to)

    def second_round(buffer, ssem, rsem, along):
        across, back, front = 4 * (1 - ring) + x, 4 * ring + behind, 4 * ring + ahead
        hops = [(back, 0, 32, chip(ring, ahead)), (front, 32, 32, chip(ring, behind))]
        if along:
            hops += [(across, 0, 64, chip(ring, ahead)), (across, 0, 64, chip(ring, behind))]
        else:
            hops += [(across, 0, 32, chip(ring, ahead)), (across, 0, 32, chip(ring, behind))]
            hops += [(back, 32, 32, chip(1 - ring, x)), (front, 32, 32, chip(1 - ring, x))]
        for owner, start, size, to in hops:
            passed = rows_from(buffer, owner, start, size)
            remote(passed, passed, ssem, rsem, to)

    def third_round(buffer, ssem, rsem):
        passed = rows_from(buffer, 4 * ring + (x + 2) % 4, 32, 32)
        remote(passed, passed, ssem, rsem, chip(1 - ring, x))
        passed = rows_from(buffer, 4 * (1 - ring) + behind, 0, 16)
        remote(passed, passed, ssem, rsem, chip(ring, ahead))
        passed = rows_from(buffer, 4 * (1 - ring) + ahead, 16, 16)
        remote(passed, passed, ssem, rsem, chip(ring, behind))

    def x_half(slots, count, owner, which):
        rows = pl.ds(pl.multiple_of(16 * owner, 16), 16)
        return xall.at[pl.ds(slots, count), rows, 256 * which : 256 * which + 256]

    def fetch(src, dst, index):
        copy = pltpu.make_async_copy(src, dst, local.at[index])
        copy.start()
        return copy

    own_fields = fetch(fields_ref, cells, 0)
    barrier = pltpu.get_barrier_semaphore()

    def greet(to):
        pl.semaphore_signal(barrier, inc=1, device_id=to, device_id_type=MESH)

    def over_z(d):
        return (c, (s + 4 * d) % SPACE)

    def over_parts(d):
        return (c, 4 * z + (part + d) % 4)

    for d in (1, 7):
        greet(over_z(d))
    for d in (1, 3):
        greet(over_parts(d))
    greet((c, side))
    greet((2 * k + other, side))
    above_us, below_us = ((2 * k + 15) % 16, s), ((2 * k + 2) % 16, s)
    for to in (above_us, below_us, partner, *near):
        greet(to)

    own_filters = fetch(filters_in, filters, 1)
    own_stem = fetch(stem_in, stem_ref, 2)
    own_mi = fetch(mi_ref, mi_all.at[own_rows64], 3)
    own_mo = fetch(mo_ref, mo_all.at[own_rows64], 4)
    rest = [(sb_in, sb_ref), (eb_in, eb_ref), (gn_in, gn_ref), (nb_in, nb_ref), (mb_in, mb_ref), (ob_in, ob_ref)]
    own_rest = [fetch(src, dst, 5 + i) for i, (src, dst) in enumerate(rest)]

    source = lax.broadcasted_iota(jnp.int32, (640, 256), 0)
    target = lax.broadcasted_iota(jnp.int32, (640, 256), 1)
    target = target % 128 + target // 128 * 80 - (source % 32 + 5) * 20 - source // 32
    order = lax.broadcasted_iota(jnp.int32, (32, 32), 0)
    order = 4 * (order % 8) + order // 8 == lax.broadcasted_iota(jnp.int32, (32, 32), 1)
    own_fields.wait()
    grid = jnp.concatenate([cells[i] for i in range(20)], axis=1)
    grid = jnp.dot(order.astype(BF16), grid, preferred_element_type=F32).astype(BF16)
    for pair in range(5):
        chosen = (target == -160 * pair).astype(BF16)
        window = jnp.dot(grid, chosen, preferred_element_type=F32).astype(BF16)
        aext[2 * pair] = window[:, :128]
        aext[2 * pair + 1] = window[:, 128:]

    pl.semaphore_wait(barrier, 14)

    def tell(index, to):
        pl.semaphore_signal(meet.at[index], inc=1, device_id=to, device_id_type=MESH)


    edge = pl.ds(pl.multiple_of(16 * core, 16), 16)
    below = (k + 2 * core + CHIPS - 1) % CHIPS
    down_here, up_here = k > 0, k < CHIPS - 1
    vertical = jnp.where(core == 0, down_here, up_here)
    for to in range(2):
        away = right if to == 0 else left
        within = s < SPACE - 1 if to == 0 else s > 0
        side_slots = slice(8 - 8 * to, 10 - 8 * to)

        @pl.when(within)
        def _(to=to, away=away, side_slots=side_slots):
            remote(
                aext.at[side_slots],
                rh.at[core],
                halo_send.at[3 + to],
                halo_recv.at[3 + core],
                (2 * k + to, away),
            )

    remote(aext.at[pl.ds(4 * other, 5)], gc.at[:, core], halo_send.at[0], halo_recv.at[0], partner)

    @pl.when(vertical)
    def _():
        for to in range(2):
            remote(
                aext.at[pl.ds(4 * to, 5), edge],
                rv.at[other],
                halo_send.at[1 + to],
                halo_recv.at[1 + other],
                (2 * below + to, s),
            )

    for to in (above_us, below_us):
        tell(3, to)
    for d in (1, 7):
        tell(0, over_z(d))
    for d in (1, 3):
        tell(1, over_parts(d))
    for to in (chip(ring, ahead), chip(ring, behind)):
        tell(4, to)
    first_round(mi_ref, mi_all, send.at[1], recv.at[1])

    pl.semaphore_wait(meet.at[3], 2)
    for to in range(2):
        away = right if to == 0 else left
        within = s < SPACE - 1 if to == 0 else s > 0
        side_slots = slice(8 - 8 * to, 10 - 8 * to)

        @pl.when(jnp.logical_and(within, vertical))
        def _(to=to, away=away, side_slots=side_slots):
            remote(
                aext.at[side_slots, edge],
                rd.at[other],
                halo_send.at[5 + to],
                halo_recv.at[5 + other],
                (2 * below + to, away),
            )


    spot = lax.broadcasted_iota(jnp.int32, (32, 128), 1)
    repeat = (spot % 32 == lax.broadcasted_iota(jnp.int32, (32, 128), 0)).astype(BF16)
    cell = lax.broadcasted_iota(jnp.int32, (20, 128), 1) // 32
    own_stem.wait()
    for copy in own_rest:
        copy.wait()
    taps[...] = jnp.zeros((384, 128), F32)
    for row in range(3):
        tiled = [jnp.dot(stem_ref[row, i], repeat, preferred_element_type=F32) for i in range(3)]
        for column in range(6):
            value = jnp.zeros((20, 128), F32)
            for i in range(3):
                if 0 <= column - i < 4:
                    value = jnp.where(cell == column - i, tiled[i], value)
            start = 128 * row + 20 * column
            taps[start : start + 20] = value
    stem_bias = jnp.concatenate([sb_ref[...]] * 4, axis=1)
    own_filters.wait()
    for row in range(4):
        for column in range(4):
            pieces = []
            for b in range(2):
                for a in range(2):
                    i, j = 4 * a + row - 1, 4 * b + column - 1
                    pieces.append(filters[i, j] if min(i, j) >= 0 else jnp.zeros((32, 64), BF16))
            start = 32 * (4 * row + column)
            wall[core, start : start + 32] = jnp.concatenate(pieces, axis=1)
    remote(wall.at[core], wall.at[core], send.at[0], recv.at[0], partner)

    gc[:, core] = aext[pl.ds(4 * core, 5)]
    at_left = jnp.logical_and(core == 0, s > 0)
    at_right = jnp.logical_and(core == 1, s < SPACE - 1)
    outside = jnp.logical_and(core == 0, s == 0)
    rows16 = pl.ds(pl.multiple_of(16 * k, 16), 16)
    tap = taps[...].astype(BF16)

    def sides(ref, half, j):
        first = jnp.where(at_left, ref[half, j].astype(F32), 0.0)
        return first + jnp.where(at_right, ref[half, 0].astype(F32), 0.0) if j else first

    def stem_of(slots, count, at_side):
        height = 16 * count
        blocks = [gc[slots + j, half].astype(F32) for j in range(count) for half in range(2)]
        beyond = []
        for half, inside in ((0, k > 0), (1, k < CHIPS - 1)):
            slabs = []
            for j in range(count):
                value = rv[half, slots + j].astype(F32)
                if at_side:
                    value = value + sides(rd, half, j)
                value = jnp.where(inside, value, 0.0)
                value = value[15:16] if half == 0 else value[0:1]
                slabs.append(jnp.broadcast_to(value, (16, 128)))
            beyond.append(jnp.concatenate(slabs, axis=0))
        if at_side:
            blocks = [block + sides(rh, i % 2, i // 2) for i, block in enumerate(blocks)]
        grid = [jnp.concatenate([block[8 * row : 8 * row + 8] for block in blocks], axis=0) for row in range(4)]
        index = lax.broadcasted_iota(jnp.int32, (height, 128), 0)
        before = jnp.where(index % 16 == 0, beyond[0], pltpu.roll(grid[3], 1, axis=0))
        after = jnp.where(index % 16 == 15, beyond[1], pltpu.roll(grid[0], height - 1, axis=0))
        lines = [line.astype(BF16) for line in (before, *grid, after)]
        for row in range(4):
            patches = jnp.concatenate(lines[row : row + 3], axis=1)
            stem = gelu(jnp.dot(patches, tap, preferred_element_type=F32) + stem_bias)
            if at_side:
                stem = jnp.where(jnp.logical_or(index >= 16, jnp.logical_not(outside)), stem, 0.0)
            stem = stem.reshape(count, 16, 128).astype(BF16)
            xall[pl.ds(slots, count), rows16, 128 * row : 128 * row + 128] = stem
        mine = xall.at[pl.ds(slots, count), rows16]
        return mine

    inner, outer = 2 - 2 * core, 3 * core
    wait(gc.at[:, core], halo_recv.at[0])
    for i, here in ((0, down_here), (1, up_here)):

        @pl.when(here)
        def _(i=i):
            wait(rv.at[i], halo_recv.at[1 + i])

    mine = stem_of(inner, 3, False)
    spread(mine, mine, send.at[2], recv.at[2])
    beside = jnp.logical_or(at_left, at_right)
    for i, here in ((0, down_here), (1, up_here)):

        @pl.when(beside)
        def _(i=i):
            wait(rh.at[i], halo_recv.at[3 + i])

        @pl.when(jnp.logical_and(beside, here))
        def _(i=i):
            wait(rd.at[i], halo_recv.at[5 + i])

    pl.semaphore_wait(meet.at[4], 2)
    mine = stem_of(outer, 2, True)
    spread(mine, mine, send.at[16], recv.at[16], True)

    pl.semaphore_wait(meet.at[0], 2)
    pl.semaphore_wait(meet.at[1], 2)
    for d in (2, 6):
        tell(2, over_z(d))
    wait(xall.at[:3, :80], recv.at[2])
    forward(functools.partial(x_half, inner, 3), send.at[9], recv.at[9])
    wait(mi_all.at[:192], recv.at[1])
    second_round(mi_all, send.at[10], recv.at[10], False)

    wait(wall.at[0], recv.at[0])
    wait(xall.at[:3, :32], recv.at[9])
    wait(xall.at[:2, :112], recv.at[16])
    tokens = xall[...].reshape(640, 512)
    low = lax.broadcasted_iota(jnp.int32, (1, 128), 1) < 64
    bias_row = eb_ref[pl.ds(k, 1), :]
    bias_rows = [jnp.where(low, 0.0, pltpu.roll(bias_row, 64, axis=1)), jnp.where(low, 0.0, bias_row)]
    lane = lax.broadcasted_iota(jnp.int32, (64, 128), 1)
    sums = [[0.0, 0.0] for _ in range(4)]
    for half in range(2):
        terms = jnp.dot(tokens, wall[half], preferred_element_type=F32)
        both = terms[128:640, 128:256] + terms[0:512, 0:128] + bias_rows[half]
        for column in range(4):
            turned = both[128 * column : 128 * column + 128].T
            shifted = pltpu.roll(turned[0:64], 1, axis=1)
            value = (turned[64:128] + jnp.where(lane > 0, shifted, 0.0)).astype(BF16)
            eh[core, 64 * half : 64 * half + 64, 128 * column : 128 * column + 128] = value
            wide = value.astype(F32)
            sums[column][0] += jnp.sum(wide, axis=0, keepdims=True)
            sums[column][1] += jnp.sum(wide * wide, axis=0, keepdims=True)
    for column in range(4):
        for kind in range(2):
            st[c, kind : kind + 1, 128 * column : 128 * column + 128] = sums[column][kind]

    for r, step in ((1, 2), (0, 2), (1, 1), (1, 3), (0, 1), (0, 3), (1, 0), (0, 0)):
        for which in (other, core):
            if r or step or which is other:
                to = 2 * (4 * (1 - ring if r else ring) + (x + step) % 4) + which
                remote(st.at[c], st.at[c], send.at[4], recv.at[4], (to, s))

    remote(eh.at[core], eh.at[core], send.at[5], recv.at[5], partner)

    wait(mi_all.at[:192], recv.at[10])
    third_round(mi_all, send.at[13], recv.at[13])
    gain = jnp.broadcast_to(gn_ref[pl.ds(k, 1), :], (128, 128)).T
    offset = jnp.broadcast_to(nb_ref[pl.ds(k, 1), :], (128, 128)).T
    gain = jnp.concatenate([gain] * 4, axis=1)
    offset = jnp.concatenate([offset] * 4, axis=1)
    wait(st.at[:15], recv.at[4])
    wait(eh.at[0], recv.at[5])
    first_round(mo_ref, mo_all, send.at[3], recv.at[3])
    normed = []
    for half in range(2):
        total = st[half]
        for j in range(1, CHIPS):
            total = total + st[2 * j + half]
        average = total[0:1] * (1.0 / 1024)
        variance = total[1:2] * (1.0 / 1024) - average * average
        scale = lax.rsqrt(variance + 1e-05)
        value = (eh[half].astype(F32) - average) * scale * gain + offset
        normed.append(value.astype(BF16))
    normed = jnp.concatenate(normed, axis=1)

    own_mi.wait()
    wait(mi_all.at[:64], recv.at[13])
    pl.semaphore_wait(meet.at[2], 2)
    for half in range(2):
        units = slice(256 * half, 256 * half + 256)
        summed = lax.dot_general(normed, mi_all[units], (((1,), (1,)), ((), ())), preferred_element_type=F32)
        summed = summed.astype(BF16)
        for band in range(8):
            hs[half, band] = summed[16 * band : 16 * band + 16]
        for d in (4, 3, 5, 2, 6, 1, 7):
            remote(hs.at[half, (z + d) % 8], rs.at[half, z], rs_send.at[half], rs_recv.at[half], over_z(d))

    for half in range(2):
        rs[half, z] = hs[half, z]
        wait(rs.at[half, :7], rs_recv.at[half])
        total = rs[half, 0].astype(F32)
        for source in range(1, 8):
            total = total + rs[half, source].astype(F32)
        quarter[half, part] = total.astype(BF16)
        mine = quarter.at[half, part]
        for d in (2, 1, 3):
            remote(mine, mine, quarter_send.at[half], quarter_recv.at[half], over_parts(d))
        if half == 0:
            wait(mo_all.at[:192], recv.at[3])
            second_round(mo_all, send.at[11], recv.at[11], True)
    rows = mb_ref[...]
    turned = pltpu.roll(rows, 64, axis=1)
    ours = jnp.where(low, jnp.where(core == 0, rows, turned), 0.0)
    theirs = jnp.where(low, 0.0, jnp.where(core == 0, turned, rows))
    hidden_bias = [ours[2 * i : 2 * i + 1] + theirs[2 * i + 1 : 2 * i + 2] for i in range(4)]
    for half in range(2):
        wait(quarter.at[half, :3], quarter_recv.at[half])
        total = quarter[half, 0].astype(F32)
        for source in range(1, 4):
            total = total + quarter[half, source].astype(F32)
        total = total + jnp.concatenate(hidden_bias[2 * half : 2 * half + 2], axis=1)
        act[half, z] = gelu(total).astype(BF16)
        for d in (4, 3, 5, 2, 6, 1, 7):
            remote(act.at[half, z], act.at[half, z], act_send.at[half], act_recv.at[half], over_z(d))

    wait(mo_all.at[:192], recv.at[11])
    third_round(mo_all, send.at[14], recv.at[14])
    own_mo.wait()

    def rows_of(which, half):
        return act[half, pl.ds(4 * which, 4)].reshape(64, 256)

    def product(which, half):
        units = slice(256 * half, 256 * half + 256)
        return jnp.dot(rows_of(which, half), mo_all[units], preferred_element_type=F32)

    wait(act.at[0, :7], act_recv.at[0])
    wait(mo_all.at[:64], recv.at[14])
    early = product(other, 0)
    mine = product(core, 0) + ob_ref[...]
    wait(act.at[1, :7], act_recv.at[1])
    for half in range(2):
        span = slice(512 * half, 512 * half + 512)
        late = jnp.dot(rows_of(other, 1), mo_all[256:512, span], preferred_element_type=F32)
        po[half] = (early[:, span] + late).astype(BF16)
        remote(po.at[half], pr.at[half], send.at[8 + 7 * half], recv.at[8 + 7 * half], partner)
    mine = mine + product(core, 1)
    residual = [eh[half, pl.ds(pl.multiple_of(64 * core, 64), 64), :].astype(F32) for half in range(2)]
    mine = mine + jnp.concatenate(residual, axis=1)
    for half in range(2):
        wait(pr.at[half], recv.at[8 + 7 * half])
        span = slice(512 * half, 512 * half + 512)
        out_ref[:, span] = (mine[:, span] + pr[half].astype(F32)).astype(BF16)

    wait(gc.at[:, core], halo_send.at[0])
    for to in range(2):
        within = s < SPACE - 1 if to == 0 else s > 0

        @pl.when(vertical)
        def _(to=to):
            wait(rv.at[to], halo_send.at[1 + to])

        @pl.when(within)
        def _(to=to):
            wait(rh.at[to], halo_send.at[3 + to])

        @pl.when(jnp.logical_and(within, vertical))
        def _(to=to):
            wait(rd.at[to], halo_send.at[5 + to])

    wait(wall.at[0], send.at[0])
    wait(mi_all.at[:192], send.at[1])
    wait(xall.at[:3, :80], send.at[2])
    wait(xall.at[:2, :112], send.at[16])
    wait(mo_all.at[:192], send.at[3])
    wait(st.at[:15], send.at[4])
    wait(eh.at[0], send.at[5])
    for half in range(2):
        wait(rs.at[half, :7], rs_send.at[half])
        wait(quarter.at[half, :3], quarter_send.at[half])
        wait(act.at[half, :7], act_send.at[half])
    wait(po.at[0], send.at[8])
    wait(po.at[1], send.at[15])
    wait(xall.at[:3, :32], send.at[9])
    wait(mi_all.at[:192], send.at[10])
    wait(mo_all.at[:192], send.at[11])
    wait(mi_all.at[:64], send.at[13])
    wait(mo_all.at[:64], send.at[14])


def shards(
    fields,
    stem_weight,
    stem_bias,
    embed_weight,
    embed_bias,
    norm_gain,
    norm_bias,
    mix_in,
    mix_in_bias,
    mix_out,
    mix_out_bias,
):
    out = pl.pallas_call(
        kernel,
        out_shape=pltpu.VMEM((64, 1024), BF16),
        in_specs=[pl.BlockSpec(memory_space=pl.ANY)] * 11,
        out_specs=pl.BlockSpec(memory_space=pltpu.VMEM),
        scratch_shapes=[
            pltpu.VMEM((20, 32, 32), BF16),
            pltpu.VMEM((7, 7, 32, 64), BF16),
            pltpu.VMEM((3, 3, 20, 32), BF16),
            pltpu.VMEM((1, 32), F32),
            pltpu.VMEM((8, 128), F32),
            pltpu.VMEM((8, 128), F32),
            pltpu.VMEM((8, 128), F32),
            pltpu.VMEM((8, 128), F32),
            pltpu.VMEM((1, 1024), F32),
            pltpu.VMEM((10, 32, 128), BF16),
            pltpu.VMEM((384, 128), F32),
            pltpu.VMEM((5, 2, 32, 128), BF16),
            pltpu.VMEM((2, 5, 16, 128), BF16),
            pltpu.VMEM((2, 2, 32, 128), BF16),
            pltpu.VMEM((2, 2, 16, 128), BF16),
            pltpu.VMEM((5, 128, 512), BF16),
            pltpu.VMEM((2, 512, 256), BF16),
            pltpu.VMEM((2, 128, 512), BF16),
            pltpu.VMEM((16, 2, 512), F32),
            pltpu.VMEM((512, 1024), BF16),
            pltpu.VMEM((512, 1024), BF16),
            pltpu.VMEM((2, 8, 16, 256), BF16),
            pltpu.VMEM((2, 8, 16, 256), BF16),
            pltpu.VMEM((2, 4, 16, 256), BF16),
            pltpu.VMEM((2, 8, 16, 256), BF16),
            pltpu.VMEM((2, 64, 512), BF16),
            pltpu.VMEM((2, 64, 512), BF16),
            pltpu.SemaphoreType.DMA((7,)),
            pltpu.SemaphoreType.DMA((7,)),
            pltpu.SemaphoreType.DMA((18,)),
            pltpu.SemaphoreType.DMA((18,)),
            *[pltpu.SemaphoreType.DMA((2,))] * 6,
            pltpu.SemaphoreType.DMA((11,)),
            pltpu.SemaphoreType.REGULAR((5,)),
        ],
        compiler_params=pltpu.CompilerParams(collective_id=0, has_side_effects=True, vmem_limit_bytes=58 * 2**20),
    )(
        stem_weight,
        stem_bias[None],
        embed_bias.reshape(8, 128),
        norm_gain.reshape(8, 128),
        norm_bias.reshape(8, 128),
        mix_in_bias.reshape(8, 128),
        mix_out_bias[None],
        embed_weight,
        fields[0],
        mix_in.T,
        mix_out,
    )
    return out[None]


def solution(mesh):
    placed = (
        P(None, None, "chan", "space"),
        P(),
        P(),
        P(None, None, None, "chan"),
        P(),
        P(),
        P(),
        P("space", "chan"),
        P(),
        P("chan", "space"),
        P("space"),
    )
    return jax.shard_map(
        shards, mesh=mesh, in_specs=placed, out_specs=P(None, "chan", "space"), check_vma=False
    )
```

```python
import functools

import jax
import jax.numpy as jnp
from jax import lax
from jax.experimental import pallas as pl
from jax.experimental.pallas import tpu as pltpu
from jax.sharding import PartitionSpec as P

MESH = pl.DeviceIdType.MESH
CHIPS = 8
SPACE = 32
F32 = jnp.float32
BF16 = jnp.bfloat16


def gelu(x):
    return 0.5 * x * (1.0 + lax.erf(x * 0.7071067811865476))


def kernel(
    stem_in,
    sb_in,
    eb_in,
    gn_in,
    nb_in,
    mb_in,
    ob_in,
    filters_in,
    fields_ref,
    mi_ref,
    mo_ref,
    out_ref,
    cells,
    filters,
    stem_ref,
    sb_ref,
    eb_ref,
    gn_ref,
    nb_ref,
    mb_ref,
    ob_ref,
    aext,
    taps,
    gc,
    rv,
    rh,
    rd,
    xall,
    wall,
    eh,
    st,
    mi_all,
    mo_all,
    hs,
    rs,
    quarter,
    act,
    po,
    pr,
    halo_send,
    halo_recv,
    send,
    recv,
    rs_send,
    rs_recv,
    quarter_send,
    quarter_recv,
    act_send,
    act_recv,
    local,
    meet,
):
    c, s = lax.axis_index("chan"), lax.axis_index("space")
    k, core = c // 2, c % 2
    other = 1 - core
    partner = (2 * k + other, s)
    z, part = s // 4, s % 4
    right, left = (s + 1) % SPACE, (s + SPACE - 1) % SPACE
    side = jnp.where(core == 0, left, right)

    def remote(src, dst, ssem, rsem, to):
        copy = pltpu.make_async_remote_copy(
            src_ref=src, dst_ref=dst, send_sem=ssem, recv_sem=rsem, device_id=to, device_id_type=MESH
        )
        copy.start()

    def wait(ref, sem):
        pltpu.make_async_copy(ref, ref, sem).wait()

    ring, x = k // 4, k % 4
    ahead, behind = (x + 1) % 4, (x + 3) % 4

    def chip(r, i):
        return (2 * (4 * r + i) + core, s)

    near = [chip(ring, ahead), chip(ring, behind), chip(1 - ring, x), chip(1 - ring, ahead), chip(1 - ring, behind)]

    far = [chip(1 - ring, (x + 2) % 4), chip(ring, (x + 2) % 4)]

    def spread(src, dst, ssem, rsem):
        for to in far + near[::-1]:
            remote(src, dst, ssem, rsem, to)

    def forward(half, r, ssem, rsem):
        passed = half(4 * r + behind, 0)
        remote(passed, passed, ssem, rsem, chip(ring, ahead))
        passed = half(4 * r + ahead, 1)
        remote(passed, passed, ssem, rsem, chip(ring, behind))

    def rows_from(buffer, owner, start, size):
        return buffer.at[pl.ds(pl.multiple_of(64 * owner + start, 16), size)]

    own_rows64 = pl.ds(pl.multiple_of(64 * k, 64), 64)

    def first_round(mine, buffer, ssem, rsem):
        for to in (chip(ring, ahead), chip(ring, behind), chip(1 - ring, x)):
            remote(mine, buffer.at[own_rows64], ssem, rsem, to)

    def second_round(buffer, ssem, rsem, along):
        across, back, front = 4 * (1 - ring) + x, 4 * ring + behind, 4 * ring + ahead
        hops = [(back, 0, 32, chip(ring, ahead)), (front, 32, 32, chip(ring, behind))]
        if along:
            hops += [(across, 0, 64, chip(ring, ahead)), (across, 0, 64, chip(ring, behind))]
        else:
            hops += [(across, 0, 32, chip(ring, ahead)), (across, 0, 32, chip(ring, behind))]
            hops += [(back, 32, 32, chip(1 - ring, x)), (front, 32, 32, chip(1 - ring, x))]
        for owner, start, size, to in hops:
            passed = rows_from(buffer, owner, start, size)
            remote(passed, passed, ssem, rsem, to)

    def third_round(buffer, ssem, rsem):
        passed = rows_from(buffer, 4 * ring + (x + 2) % 4, 32, 32)
        remote(passed, passed, ssem, rsem, chip(1 - ring, x))
        passed = rows_from(buffer, 4 * (1 - ring) + behind, 0, 16)
        remote(passed, passed, ssem, rsem, chip(ring, ahead))
        passed = rows_from(buffer, 4 * (1 - ring) + ahead, 16, 16)
        remote(passed, passed, ssem, rsem, chip(ring, behind))

    def x_half(slots, count, owner, which):
        rows = pl.ds(pl.multiple_of(16 * owner, 16), 16)
        return xall.at[pl.ds(slots, count), rows, 256 * which : 256 * which + 256]

    def fetch(src, dst, index):
        copy = pltpu.make_async_copy(src, dst, local.at[index])
        copy.start()
        return copy

    own_fields = fetch(fields_ref, cells, 0)
    barrier = pltpu.get_barrier_semaphore()

    def greet(to):
        pl.semaphore_signal(barrier, inc=1, device_id=to, device_id_type=MESH)

    def over_z(d):
        return (c, (s + 4 * d) % SPACE)

    def over_parts(d):
        return (c, 4 * z + (part + d) % 4)

    def line_z(d, act_on):
        @pl.when(z >= d)
        def _():
            act_on((c, s - 4 * d))

        @pl.when(z + d < 8)
        def _():
            act_on((c, s + 4 * d))

    def on_line(d):
        return (z >= d).astype(jnp.int32) + (z + d < 8).astype(jnp.int32)

    line_z(1, greet)
    for d in (1, 3):
        greet(over_parts(d))

    @pl.when(jnp.where(core == 0, s > 0, s < SPACE - 1))
    def _():
        greet((c, side))
        greet((2 * k + other, side))

    above_us, below_us = ((2 * k + 15) % 16, s), ((2 * k + 2) % 16, s)
    for to in (above_us, below_us, partner, *near):
        greet(to)

    own_filters = fetch(filters_in, filters, 1)
    own_stem = fetch(stem_in, stem_ref, 2)
    own_mi = fetch(mi_ref, mi_all.at[own_rows64], 3)
    own_mo = fetch(mo_ref, mo_all.at[own_rows64], 4)
    rest = [(sb_in, sb_ref), (eb_in, eb_ref), (gn_in, gn_ref), (nb_in, nb_ref), (mb_in, mb_ref), (ob_in, ob_ref)]
    own_rest = [fetch(src, dst, 5 + i) for i, (src, dst) in enumerate(rest)]

    source = lax.broadcasted_iota(jnp.int32, (640, 256), 0)
    target = lax.broadcasted_iota(jnp.int32, (640, 256), 1)
    target = target % 128 + target // 128 * 80 - (source % 32 + 5) * 20 - source // 32
    order = lax.broadcasted_iota(jnp.int32, (32, 32), 0)
    order = 4 * (order % 8) + order // 8 == lax.broadcasted_iota(jnp.int32, (32, 32), 1)
    own_fields.wait()
    grid = jnp.concatenate([cells[i] for i in range(20)], axis=1)
    grid = jnp.dot(order.astype(BF16), grid, preferred_element_type=F32).astype(BF16)
    for pair in range(5):
        chosen = (target == -160 * pair).astype(BF16)
        window = jnp.dot(grid, chosen, preferred_element_type=F32).astype(BF16)
        aext[2 * pair] = window[:, :128]
        aext[2 * pair + 1] = window[:, 128:]

    beside_us = (s > 0).astype(jnp.int32) + (s < SPACE - 1).astype(jnp.int32)
    pl.semaphore_wait(barrier, 10 + on_line(1) + beside_us)

    def tell(index, to):
        pl.semaphore_signal(meet.at[index], inc=1, device_id=to, device_id_type=MESH)


    edge = pl.ds(pl.multiple_of(16 * core, 16), 16)
    below = (k + 2 * core + CHIPS - 1) % CHIPS
    down_here, up_here = k > 0, k < CHIPS - 1
    vertical = jnp.where(core == 0, down_here, up_here)
    for to in range(2):
        away = right if to == 0 else left
        within = s < SPACE - 1 if to == 0 else s > 0
        side_slots = slice(8 - 8 * to, 10 - 8 * to)

        @pl.when(within)
        def _(to=to, away=away, side_slots=side_slots):
            remote(
                aext.at[side_slots],
                rh.at[core],
                halo_send.at[3 + to],
                halo_recv.at[3 + core],
                (2 * k + to, away),
            )

    remote(aext.at[pl.ds(4 * other, 5)], gc.at[:, core], halo_send.at[0], halo_recv.at[0], partner)

    @pl.when(vertical)
    def _():
        for to in range(2):
            remote(
                aext.at[pl.ds(4 * to, 5), edge],
                rv.at[other],
                halo_send.at[1 + to],
                halo_recv.at[1 + other],
                (2 * below + to, s),
            )

    for to in (above_us, below_us):
        tell(3, to)
    line_z(1, functools.partial(tell, 0))
    for d in (1, 3):
        tell(1, over_parts(d))
    for to in (chip(ring, ahead), chip(ring, behind)):
        tell(4, to)
    first_round(mi_ref, mi_all, send.at[1], recv.at[1])

    pl.semaphore_wait(meet.at[3], 2)
    for to in range(2):
        away = right if to == 0 else left
        within = s < SPACE - 1 if to == 0 else s > 0
        side_slots = slice(8 - 8 * to, 10 - 8 * to)

        @pl.when(jnp.logical_and(within, vertical))
        def _(to=to, away=away, side_slots=side_slots):
            remote(
                aext.at[side_slots, edge],
                rd.at[other],
                halo_send.at[5 + to],
                halo_recv.at[5 + other],
                (2 * below + to, away),
            )


    spot = lax.broadcasted_iota(jnp.int32, (32, 128), 1)
    repeat = (spot % 32 == lax.broadcasted_iota(jnp.int32, (32, 128), 0)).astype(BF16)
    cell = lax.broadcasted_iota(jnp.int32, (20, 128), 1) // 32
    own_stem.wait()
    for copy in own_rest:
        copy.wait()
    taps[...] = jnp.zeros((384, 128), F32)
    for row in range(3):
        tiled = [jnp.dot(stem_ref[row, i], repeat, preferred_element_type=F32) for i in range(3)]
        for column in range(6):
            value = jnp.zeros((20, 128), F32)
            for i in range(3):
                if 0 <= column - i < 4:
                    value = jnp.where(cell == column - i, tiled[i], value)
            start = 128 * row + 20 * column
            taps[start : start + 20] = value
    stem_bias = jnp.concatenate([sb_ref[...]] * 4, axis=1)
    own_filters.wait()
    for row in range(4):
        for column in range(4):
            pieces = []
            for b in range(2):
                for a in range(2):
                    i, j = 4 * a + row - 1, 4 * b + column - 1
                    pieces.append(filters[i, j] if min(i, j) >= 0 else jnp.zeros((32, 64), BF16))
            start = 32 * (4 * row + column)
            wall[core, start : start + 32] = jnp.concatenate(pieces, axis=1)
    remote(wall.at[core], wall.at[core], send.at[0], recv.at[0], partner)

    gc[:, core] = aext[pl.ds(4 * core, 5)]
    at_left = jnp.logical_and(core == 0, s > 0)
    at_right = jnp.logical_and(core == 1, s < SPACE - 1)
    outside = jnp.logical_and(core == 0, s == 0)
    rows16 = pl.ds(pl.multiple_of(16 * k, 16), 16)
    tap = taps[...].astype(BF16)

    def sides(ref, half, j):
        first = jnp.where(at_left, ref[half, j].astype(F32), 0.0)
        return first + jnp.where(at_right, ref[half, 0].astype(F32), 0.0) if j else first

    def stem_of(slots, count, at_side):
        height = 16 * count
        blocks = [gc[slots + j, half].astype(F32) for j in range(count) for half in range(2)]
        beyond = []
        for half, inside in ((0, k > 0), (1, k < CHIPS - 1)):
            slabs = []
            for j in range(count):
                value = rv[half, slots + j].astype(F32)
                if at_side:
                    value = value + sides(rd, half, j)
                value = jnp.where(inside, value, 0.0)
                value = value[15:16] if half == 0 else value[0:1]
                slabs.append(jnp.broadcast_to(value, (16, 128)))
            beyond.append(jnp.concatenate(slabs, axis=0))
        if at_side:
            blocks = [block + sides(rh, i % 2, i // 2) for i, block in enumerate(blocks)]
        grid = [jnp.concatenate([block[8 * row : 8 * row + 8] for block in blocks], axis=0) for row in range(4)]
        index = lax.broadcasted_iota(jnp.int32, (height, 128), 0)
        before = jnp.where(index % 16 == 0, beyond[0], pltpu.roll(grid[3], 1, axis=0))
        after = jnp.where(index % 16 == 15, beyond[1], pltpu.roll(grid[0], height - 1, axis=0))
        lines = [line.astype(BF16) for line in (before, *grid, after)]
        for row in range(4):
            patches = jnp.concatenate(lines[row : row + 3], axis=1)
            stem = gelu(jnp.dot(patches, tap, preferred_element_type=F32) + stem_bias)
            if at_side:
                stem = jnp.where(jnp.logical_or(index >= 16, jnp.logical_not(outside)), stem, 0.0)
            stem = stem.reshape(count, 16, 128).astype(BF16)
            xall[pl.ds(slots, count), rows16, 128 * row : 128 * row + 128] = stem
        mine = xall.at[pl.ds(slots, count), rows16]
        return mine

    inner, outer = 2 - 2 * core, 3 * core
    wait(gc.at[:, core], halo_recv.at[0])
    for i, here in ((0, down_here), (1, up_here)):

        @pl.when(here)
        def _(i=i):
            wait(rv.at[i], halo_recv.at[1 + i])

    mine = stem_of(inner, 3, False)
    for i, to in enumerate(near):
        remote(mine, mine, send.at[2], recv.at[2 if i < 2 else 12], to)

    beside = jnp.logical_or(at_left, at_right)
    for i, here in ((0, down_here), (1, up_here)):

        @pl.when(beside)
        def _(i=i):
            wait(rh.at[i], halo_recv.at[3 + i])

        @pl.when(jnp.logical_and(beside, here))
        def _(i=i):
            wait(rd.at[i], halo_recv.at[5 + i])

    pl.semaphore_wait(meet.at[4], 2)
    mine = stem_of(outer, 2, True)
    spread(mine, mine, send.at[16], recv.at[16])

    pl.semaphore_wait(meet.at[0], on_line(1))
    pl.semaphore_wait(meet.at[1], 2)
    line_z(2, functools.partial(tell, 2))
    wait(xall.at[:3, :32], recv.at[2])
    forward(functools.partial(x_half, inner, 3), ring, send.at[9], recv.at[9])
    wait(xall.at[:3, :48], recv.at[12])
    forward(functools.partial(x_half, inner, 3), 1 - ring, send.at[9], recv.at[9])
    pl.semaphore_wait(meet.at[2], on_line(2))
    line_z(4, functools.partial(tell, 5))
    wait(mi_all.at[:192], recv.at[1])
    second_round(mi_all, send.at[10], recv.at[10], False)

    wait(wall.at[0], recv.at[0])
    wait(xall.at[:3, :32], recv.at[9])
    wait(xall.at[:2, :112], recv.at[16])
    tokens = xall[...].reshape(640, 512)
    low = lax.broadcasted_iota(jnp.int32, (1, 128), 1) < 64
    bias_row = eb_ref[pl.ds(k, 1), :]
    bias_rows = [jnp.where(low, 0.0, pltpu.roll(bias_row, 64, axis=1)), jnp.where(low, 0.0, bias_row)]
    lane = lax.broadcasted_iota(jnp.int32, (64, 128), 1)
    sums = [[0.0, 0.0] for _ in range(4)]
    for half in range(2):
        terms = jnp.dot(tokens, wall[half], preferred_element_type=F32)
        both = terms[128:640, 128:256] + terms[0:512, 0:128] + bias_rows[half]
        for column in range(4):
            turned = both[128 * column : 128 * column + 128].T
            shifted = pltpu.roll(turned[0:64], 1, axis=1)
            value = (turned[64:128] + jnp.where(lane > 0, shifted, 0.0)).astype(BF16)
            eh[core, 64 * half : 64 * half + 64, 128 * column : 128 * column + 128] = value
            wide = value.astype(F32)
            sums[column][0] += jnp.sum(wide, axis=0, keepdims=True)
            sums[column][1] += jnp.sum(wide * wide, axis=0, keepdims=True)
    for column in range(4):
        for kind in range(2):
            st[c, kind : kind + 1, 128 * column : 128 * column + 128] = sums[column][kind]

    for r, step in ((1, 2), (0, 2), (1, 1), (1, 3), (0, 1), (0, 3), (1, 0), (0, 0)):
        for which in (other, core):
            if r or step or which is other:
                to = 2 * (4 * (1 - ring if r else ring) + (x + step) % 4) + which
                remote(st.at[c], st.at[c], send.at[4], recv.at[4], (to, s))

    remote(eh.at[core], eh.at[core], send.at[5], recv.at[5], partner)

    wait(mi_all.at[:192], recv.at[10])
    third_round(mi_all, send.at[13], recv.at[13])
    gain = jnp.broadcast_to(gn_ref[pl.ds(k, 1), :], (128, 128)).T
    offset = jnp.broadcast_to(nb_ref[pl.ds(k, 1), :], (128, 128)).T
    gain = jnp.concatenate([gain] * 4, axis=1)
    offset = jnp.concatenate([offset] * 4, axis=1)
    wait(st.at[:15], recv.at[4])
    wait(eh.at[0], recv.at[5])
    first_round(mo_ref, mo_all, send.at[3], recv.at[3])
    normed = []
    for half in range(2):
        total = st[half]
        for j in range(1, CHIPS):
            total = total + st[2 * j + half]
        average = total[0:1] * (1.0 / 1024)
        variance = total[1:2] * (1.0 / 1024) - average * average
        scale = lax.rsqrt(variance + 1e-05)
        value = (eh[half].astype(F32) - average) * scale * gain + offset
        normed.append(value.astype(BF16))
    normed = jnp.concatenate(normed, axis=1)

    own_mi.wait()
    wait(mi_all.at[:64], recv.at[13])
    pl.semaphore_wait(meet.at[5], 1)
    for half in range(2):
        units = slice(256 * half, 256 * half + 256)
        summed = lax.dot_general(normed, mi_all[units], (((1,), (1,)), ((), ())), preferred_element_type=F32)
        summed = summed.astype(BF16)
        for band in range(8):
            hs[half, band] = summed[16 * band : 16 * band + 16]
        for d in (4, 3, 5, 2, 6, 1, 7):
            remote(hs.at[half, (z + d) % 8], rs.at[half, z], rs_send.at[half], rs_recv.at[half], over_z(d))

    for half in range(2):
        rs[half, z] = hs[half, z]
        wait(rs.at[half, :7], rs_recv.at[half])
        total = rs[half, 0].astype(F32)
        for source in range(1, 8):
            total = total + rs[half, source].astype(F32)
        quarter[half, part] = total.astype(BF16)
        mine = quarter.at[half, part]
        for d in (2, 1, 3):
            remote(mine, mine, quarter_send.at[half], quarter_recv.at[half], over_parts(d))
        if half == 0:
            wait(mo_all.at[:192], recv.at[3])
            second_round(mo_all, send.at[11], recv.at[11], True)
    rows = mb_ref[...]
    turned = pltpu.roll(rows, 64, axis=1)
    ours = jnp.where(low, jnp.where(core == 0, rows, turned), 0.0)
    theirs = jnp.where(low, 0.0, jnp.where(core == 0, turned, rows))
    hidden_bias = [ours[2 * i : 2 * i + 1] + theirs[2 * i + 1 : 2 * i + 2] for i in range(4)]
    for half in range(2):
        wait(quarter.at[half, :3], quarter_recv.at[half])
        total = quarter[half, 0].astype(F32)
        for source in range(1, 4):
            total = total + quarter[half, source].astype(F32)
        total = total + jnp.concatenate(hidden_bias[2 * half : 2 * half + 2], axis=1)
        act[half, z] = gelu(total).astype(BF16)
        for d in (4, 3, 5, 2, 6, 1, 7):
            remote(act.at[half, z], act.at[half, z], act_send.at[half], act_recv.at[half], over_z(d))

    wait(mo_all.at[:192], recv.at[11])
    third_round(mo_all, send.at[14], recv.at[14])
    own_mo.wait()

    def rows_of(which, half):
        return act[half, pl.ds(4 * which, 4)].reshape(64, 256)

    def product(which, half):
        units = slice(256 * half, 256 * half + 256)
        return jnp.dot(rows_of(which, half), mo_all[units], preferred_element_type=F32)

    wait(act.at[0, :7], act_recv.at[0])
    wait(mo_all.at[:64], recv.at[14])
    early = product(other, 0)
    mine = product(core, 0) + ob_ref[...]
    wait(act.at[1, :7], act_recv.at[1])
    for half in range(2):
        span = slice(512 * half, 512 * half + 512)
        late = jnp.dot(rows_of(other, 1), mo_all[256:512, span], preferred_element_type=F32)
        po[half] = (early[:, span] + late).astype(BF16)
        remote(po.at[half], pr.at[half], send.at[8 + 7 * half], recv.at[8 + 7 * half], partner)
    mine = mine + product(core, 1)
    residual = [eh[half, pl.ds(pl.multiple_of(64 * core, 64), 64), :].astype(F32) for half in range(2)]
    mine = mine + jnp.concatenate(residual, axis=1)
    for half in range(2):
        wait(pr.at[half], recv.at[8 + 7 * half])
        span = slice(512 * half, 512 * half + 512)
        out_ref[:, span] = (mine[:, span] + pr[half].astype(F32)).astype(BF16)

    wait(gc.at[:, core], halo_send.at[0])
    for to in range(2):
        within = s < SPACE - 1 if to == 0 else s > 0

        @pl.when(vertical)
        def _(to=to):
            wait(rv.at[to], halo_send.at[1 + to])

        @pl.when(within)
        def _(to=to):
            wait(rh.at[to], halo_send.at[3 + to])

        @pl.when(jnp.logical_and(within, vertical))
        def _(to=to):
            wait(rd.at[to], halo_send.at[5 + to])

    wait(wall.at[0], send.at[0])
    wait(mi_all.at[:192], send.at[1])
    wait(xall.at[:3, :80], send.at[2])
    wait(xall.at[:2, :112], send.at[16])
    wait(mo_all.at[:192], send.at[3])
    wait(st.at[:15], send.at[4])
    wait(eh.at[0], send.at[5])
    for half in range(2):
        wait(rs.at[half, :7], rs_send.at[half])
        wait(quarter.at[half, :3], quarter_send.at[half])
        wait(act.at[half, :7], act_send.at[half])
    wait(po.at[0], send.at[8])
    wait(po.at[1], send.at[15])
    wait(xall.at[:3, :32], send.at[9])
    wait(mi_all.at[:192], send.at[10])
    wait(mo_all.at[:192], send.at[11])
    wait(mi_all.at[:64], send.at[13])
    wait(mo_all.at[:64], send.at[14])


def shards(
    fields,
    stem_weight,
    stem_bias,
    embed_weight,
    embed_bias,
    norm_gain,
    norm_bias,
    mix_in,
    mix_in_bias,
    mix_out,
    mix_out_bias,
):
    out = pl.pallas_call(
        kernel,
        out_shape=pltpu.VMEM((64, 1024), BF16),
        in_specs=[pl.BlockSpec(memory_space=pl.ANY)] * 11,
        out_specs=pl.BlockSpec(memory_space=pltpu.VMEM),
        scratch_shapes=[
            pltpu.VMEM((20, 32, 32), BF16),
            pltpu.VMEM((7, 7, 32, 64), BF16),
            pltpu.VMEM((3, 3, 20, 32), BF16),
            pltpu.VMEM((1, 32), F32),
            pltpu.VMEM((8, 128), F32),
            pltpu.VMEM((8, 128), F32),
            pltpu.VMEM((8, 128), F32),
            pltpu.VMEM((8, 128), F32),
            pltpu.VMEM((1, 1024), F32),
            pltpu.VMEM((10, 32, 128), BF16),
            pltpu.VMEM((384, 128), F32),
            pltpu.VMEM((5, 2, 32, 128), BF16),
            pltpu.VMEM((2, 5, 16, 128), BF16),
            pltpu.VMEM((2, 2, 32, 128), BF16),
            pltpu.VMEM((2, 2, 16, 128), BF16),
            pltpu.VMEM((5, 128, 512), BF16),
            pltpu.VMEM((2, 512, 256), BF16),
            pltpu.VMEM((2, 128, 512), BF16),
            pltpu.VMEM((16, 2, 512), F32),
            pltpu.VMEM((512, 1024), BF16),
            pltpu.VMEM((512, 1024), BF16),
            pltpu.VMEM((2, 8, 16, 256), BF16),
            pltpu.VMEM((2, 8, 16, 256), BF16),
            pltpu.VMEM((2, 4, 16, 256), BF16),
            pltpu.VMEM((2, 8, 16, 256), BF16),
            pltpu.VMEM((2, 64, 512), BF16),
            pltpu.VMEM((2, 64, 512), BF16),
            pltpu.SemaphoreType.DMA((7,)),
            pltpu.SemaphoreType.DMA((7,)),
            pltpu.SemaphoreType.DMA((18,)),
            pltpu.SemaphoreType.DMA((18,)),
            *[pltpu.SemaphoreType.DMA((2,))] * 6,
            pltpu.SemaphoreType.DMA((11,)),
            pltpu.SemaphoreType.REGULAR((6,)),
        ],
        compiler_params=pltpu.CompilerParams(collective_id=0, has_side_effects=True, vmem_limit_bytes=58 * 2**20),
    )(
        stem_weight,
        stem_bias[None],
        embed_bias.reshape(8, 128),
        norm_gain.reshape(8, 128),
        norm_bias.reshape(8, 128),
        mix_in_bias.reshape(8, 128),
        mix_out_bias[None],
        embed_weight,
        fields[0],
        mix_in.T,
        mix_out,
    )
    return out[None]


def solution(mesh):
    placed = (
        P(None, None, "chan", "space"),
        P(),
        P(),
        P(None, None, None, "chan"),
        P(),
        P(),
        P(),
        P("space", "chan"),
        P(),
        P("chan", "space"),
        P("space"),
    )
    return jax.shard_map(
        shards, mesh=mesh, in_specs=placed, out_specs=P(None, "chan", "space"), check_vma=False
    )
```

```python
import functools

import jax
import jax.numpy as jnp
from jax import lax
from jax.experimental import pallas as pl
from jax.experimental.pallas import tpu as pltpu
from jax.sharding import PartitionSpec as P

MESH = pl.DeviceIdType.MESH
CHIPS = 8
SPACE = 32
F32 = jnp.float32
BF16 = jnp.bfloat16


def gelu(x):
    return 0.5 * x * (1.0 + lax.erf(x * 0.7071067811865476))


def kernel(
    stem_in,
    sb_in,
    eb_in,
    gn_in,
    nb_in,
    mb_in,
    ob_in,
    filters_in,
    fields_ref,
    mi_ref,
    mo_ref,
    out_ref,
    cells,
    filters,
    stem_ref,
    sb_ref,
    eb_ref,
    gn_ref,
    nb_ref,
    mb_ref,
    ob_ref,
    aext,
    taps,
    gc,
    rv,
    rh,
    rd,
    xall,
    wall,
    eh,
    st,
    mi_all,
    mo_all,
    hs,
    rs,
    quarter,
    act,
    po,
    pr,
    halo_send,
    halo_recv,
    send,
    recv,
    rs_send,
    rs_recv,
    quarter_send,
    quarter_recv,
    act_send,
    act_recv,
    local,
    meet,
):
    c, s = lax.axis_index("chan"), lax.axis_index("space")
    k, core = c // 2, c % 2
    other = 1 - core
    partner = (2 * k + other, s)
    z, part = s // 4, s % 4
    right, left = (s + 1) % SPACE, (s + SPACE - 1) % SPACE
    side = jnp.where(core == 0, left, right)

    def remote(src, dst, ssem, rsem, to):
        copy = pltpu.make_async_remote_copy(
            src_ref=src, dst_ref=dst, send_sem=ssem, recv_sem=rsem, device_id=to, device_id_type=MESH
        )
        copy.start()

    def wait(ref, sem):
        pltpu.make_async_copy(ref, ref, sem).wait()

    ring, x = k // 4, k % 4
    ahead, behind = (x + 1) % 4, (x + 3) % 4

    def chip(r, i):
        return (2 * (4 * r + i) + core, s)

    near = [chip(ring, ahead), chip(ring, behind), chip(1 - ring, x), chip(1 - ring, ahead), chip(1 - ring, behind)]

    far = [chip(1 - ring, (x + 2) % 4), chip(ring, (x + 2) % 4)]

    def spread(src, dst, ssem, rsem):
        for to in far + near[::-1]:
            remote(src, dst, ssem, rsem, to)

    def forward(half, r, ssem, rsem):
        passed = half(4 * r + behind, 0)
        remote(passed, passed, ssem, rsem, chip(ring, ahead))
        passed = half(4 * r + ahead, 1)
        remote(passed, passed, ssem, rsem, chip(ring, behind))

    def rows_from(buffer, owner, start, size):
        return buffer.at[pl.ds(pl.multiple_of(64 * owner + start, 16), size)]

    own_rows64 = pl.ds(pl.multiple_of(64 * k, 64), 64)

    def first_round(mine, buffer, ssem, rsem):
        for to in (chip(ring, ahead), chip(ring, behind), chip(1 - ring, x)):
            remote(mine, buffer.at[own_rows64], ssem, rsem, to)

    def second_round(buffer, ssem, rsem, along):
        across, back, front = 4 * (1 - ring) + x, 4 * ring + behind, 4 * ring + ahead
        hops = [(back, 0, 32, chip(ring, ahead)), (front, 32, 32, chip(ring, behind))]
        if along:
            hops += [(across, 0, 64, chip(ring, ahead)), (across, 0, 64, chip(ring, behind))]
        else:
            hops += [(across, 0, 32, chip(ring, ahead)), (across, 0, 32, chip(ring, behind))]
            hops += [(back, 32, 32, chip(1 - ring, x)), (front, 32, 32, chip(1 - ring, x))]
        for owner, start, size, to in hops:
            passed = rows_from(buffer, owner, start, size)
            remote(passed, passed, ssem, rsem, to)

    def third_round(buffer, ssem, rsem):
        passed = rows_from(buffer, 4 * ring + (x + 2) % 4, 32, 32)
        remote(passed, passed, ssem, rsem, chip(1 - ring, x))
        passed = rows_from(buffer, 4 * (1 - ring) + behind, 0, 16)
        remote(passed, passed, ssem, rsem, chip(ring, ahead))
        passed = rows_from(buffer, 4 * (1 - ring) + ahead, 16, 16)
        remote(passed, passed, ssem, rsem, chip(ring, behind))

    def x_half(slots, count, owner, which):
        rows = pl.ds(pl.multiple_of(16 * owner, 16), 16)
        return xall.at[pl.ds(slots, count), rows, 256 * which : 256 * which + 256]

    def fetch(src, dst, index):
        copy = pltpu.make_async_copy(src, dst, local.at[index])
        copy.start()
        return copy

    own_fields = fetch(fields_ref, cells, 0)
    barrier = pltpu.get_barrier_semaphore()

    def greet(to):
        pl.semaphore_signal(barrier, inc=1, device_id=to, device_id_type=MESH)

    def over_z(d):
        return (c, (s + 4 * d) % SPACE)

    def over_parts(d):
        return (c, 4 * z + (part + d) % 4)

    def line_z(d, act_on):
        @pl.when(z >= d)
        def _():
            act_on((c, s - 4 * d))

        @pl.when(z + d < 8)
        def _():
            act_on((c, s + 4 * d))

    def on_line(d):
        return (z >= d).astype(jnp.int32) + (z + d < 8).astype(jnp.int32)

    line_z(1, greet)
    for d in (1, 3):
        greet(over_parts(d))

    @pl.when(jnp.where(core == 0, s > 0, s < SPACE - 1))
    def _():
        greet((c, side))
        greet((2 * k + other, side))

    above_us, below_us = ((2 * k + 15) % 16, s), ((2 * k + 2) % 16, s)
    for to in (above_us, below_us, partner, *near):
        greet(to)

    own_filters = fetch(filters_in, filters, 1)
    own_stem = fetch(stem_in, stem_ref, 2)
    own_mi = fetch(mi_ref, mi_all.at[own_rows64], 3)
    own_mo = fetch(mo_ref, mo_all.at[own_rows64], 4)
    rest = [(sb_in, sb_ref), (eb_in, eb_ref), (gn_in, gn_ref), (nb_in, nb_ref), (mb_in, mb_ref), (ob_in, ob_ref)]
    own_rest = [fetch(src, dst, 5 + i) for i, (src, dst) in enumerate(rest)]

    source = lax.broadcasted_iota(jnp.int32, (640, 256), 0)
    target = lax.broadcasted_iota(jnp.int32, (640, 256), 1)
    target = target % 128 + target // 128 * 80 - (source % 32 + 5) * 20 - source // 32
    order = lax.broadcasted_iota(jnp.int32, (32, 32), 0)
    order = 4 * (order % 8) + order // 8 == lax.broadcasted_iota(jnp.int32, (32, 32), 1)
    own_fields.wait()
    grid = jnp.concatenate([cells[i] for i in range(20)], axis=1)
    grid = jnp.dot(order.astype(BF16), grid, preferred_element_type=F32).astype(BF16)
    for pair in range(5):
        chosen = (target == -160 * pair).astype(BF16)
        window = jnp.dot(grid, chosen, preferred_element_type=F32).astype(BF16)
        aext[2 * pair] = window[:, :128]
        aext[2 * pair + 1] = window[:, 128:]

    beside_us = (s > 0).astype(jnp.int32) + (s < SPACE - 1).astype(jnp.int32)
    pl.semaphore_wait(barrier, 10 + on_line(1) + beside_us)

    def tell(index, to):
        pl.semaphore_signal(meet.at[index], inc=1, device_id=to, device_id_type=MESH)


    edge = pl.ds(pl.multiple_of(16 * core, 16), 16)
    below = (k + 2 * core + CHIPS - 1) % CHIPS
    down_here, up_here = k > 0, k < CHIPS - 1
    vertical = jnp.where(core == 0, down_here, up_here)
    for to in range(2):
        away = right if to == 0 else left
        within = s < SPACE - 1 if to == 0 else s > 0
        side_slots = slice(8 - 8 * to, 10 - 8 * to)

        @pl.when(within)
        def _(to=to, away=away, side_slots=side_slots):
            remote(
                aext.at[side_slots],
                rh.at[core],
                halo_send.at[3 + to],
                halo_recv.at[3 + core],
                (2 * k + to, away),
            )

    remote(aext.at[pl.ds(4 * other, 5)], gc.at[:, core], halo_send.at[0], halo_recv.at[0], partner)

    @pl.when(vertical)
    def _():
        for to in range(2):
            remote(
                aext.at[pl.ds(4 * to, 5), edge],
                rv.at[other],
                halo_send.at[1 + to],
                halo_recv.at[1 + other],
                (2 * below + to, s),
            )

    for to in (above_us, below_us):
        tell(3, to)
    line_z(1, functools.partial(tell, 0))
    for d in (1, 3):
        tell(1, over_parts(d))
    for to in (chip(ring, ahead), chip(ring, behind)):
        tell(4, to)
    first_round(mi_ref, mi_all, send.at[1], recv.at[1])

    pl.semaphore_wait(meet.at[3], 2)
    for to in range(2):
        away = right if to == 0 else left
        within = s < SPACE - 1 if to == 0 else s > 0
        side_slots = slice(8 - 8 * to, 10 - 8 * to)

        @pl.when(jnp.logical_and(within, vertical))
        def _(to=to, away=away, side_slots=side_slots):
            remote(
                aext.at[side_slots, edge],
                rd.at[other],
                halo_send.at[5 + to],
                halo_recv.at[5 + other],
                (2 * below + to, away),
            )


    spot = lax.broadcasted_iota(jnp.int32, (32, 128), 1)
    repeat = (spot % 32 == lax.broadcasted_iota(jnp.int32, (32, 128), 0)).astype(BF16)
    cell = lax.broadcasted_iota(jnp.int32, (20, 128), 1) // 32
    own_stem.wait()
    for copy in own_rest:
        copy.wait()
    taps[...] = jnp.zeros((384, 128), F32)
    for row in range(3):
        tiled = [jnp.dot(stem_ref[row, i], repeat, preferred_element_type=F32) for i in range(3)]
        for column in range(6):
            value = jnp.zeros((20, 128), F32)
            for i in range(3):
                if 0 <= column - i < 4:
                    value = jnp.where(cell == column - i, tiled[i], value)
            start = 128 * row + 20 * column
            taps[start : start + 20] = value
    stem_bias = jnp.concatenate([sb_ref[...]] * 4, axis=1)
    own_filters.wait()
    for row in range(4):
        for column in range(4):
            pieces = []
            for b in range(2):
                for a in range(2):
                    i, j = 4 * a + row - 1, 4 * b + column - 1
                    pieces.append(filters[i, j] if min(i, j) >= 0 else jnp.zeros((32, 64), BF16))
            start = 32 * (4 * row + column)
            wall[core, start : start + 32] = jnp.concatenate(pieces, axis=1)
    remote(wall.at[core], wall.at[core], send.at[0], recv.at[0], partner)

    gc[:, core] = aext[pl.ds(4 * core, 5)]
    at_left = jnp.logical_and(core == 0, s > 0)
    at_right = jnp.logical_and(core == 1, s < SPACE - 1)
    outside = jnp.logical_and(core == 0, s == 0)
    rows16 = pl.ds(pl.multiple_of(16 * k, 16), 16)
    tap = taps[...].astype(BF16)

    def sides(ref, half, j):
        first = jnp.where(at_left, ref[half, j].astype(F32), 0.0)
        return first + jnp.where(at_right, ref[half, 0].astype(F32), 0.0) if j else first

    def stem_of(slots, count, at_side):
        height = 16 * count
        blocks = [gc[slots + j, half].astype(F32) for j in range(count) for half in range(2)]
        beyond = []
        for half, inside in ((0, k > 0), (1, k < CHIPS - 1)):
            slabs = []
            for j in range(count):
                value = rv[half, slots + j].astype(F32)
                if at_side:
                    value = value + sides(rd, half, j)
                value = jnp.where(inside, value, 0.0)
                value = value[15:16] if half == 0 else value[0:1]
                slabs.append(jnp.broadcast_to(value, (16, 128)))
            beyond.append(jnp.concatenate(slabs, axis=0))
        if at_side:
            blocks = [block + sides(rh, i % 2, i // 2) for i, block in enumerate(blocks)]
        grid = [jnp.concatenate([block[8 * row : 8 * row + 8] for block in blocks], axis=0) for row in range(4)]
        index = lax.broadcasted_iota(jnp.int32, (height, 128), 0)
        before = jnp.where(index % 16 == 0, beyond[0], pltpu.roll(grid[3], 1, axis=0))
        after = jnp.where(index % 16 == 15, beyond[1], pltpu.roll(grid[0], height - 1, axis=0))
        lines = [line.astype(BF16) for line in (before, *grid, after)]
        for row in range(4):
            patches = jnp.concatenate(lines[row : row + 3], axis=1)
            stem = gelu(jnp.dot(patches, tap, preferred_element_type=F32) + stem_bias)
            if at_side:
                stem = jnp.where(jnp.logical_or(index >= 16, jnp.logical_not(outside)), stem, 0.0)
            stem = stem.reshape(count, 16, 128).astype(BF16)
            xall[pl.ds(slots, count), rows16, 128 * row : 128 * row + 128] = stem
        mine = xall.at[pl.ds(slots, count), rows16]
        return mine

    inner, outer = 2 - 2 * core, 3 * core
    wait(gc.at[:, core], halo_recv.at[0])
    for i, here in ((0, down_here), (1, up_here)):

        @pl.when(here)
        def _(i=i):
            wait(rv.at[i], halo_recv.at[1 + i])

    mine = stem_of(inner, 3, False)
    for i, to in enumerate(near):
        remote(mine, mine, send.at[2], recv.at[2 if i < 2 else 12], to)

    beside = jnp.logical_or(at_left, at_right)
    for i, here in ((0, down_here), (1, up_here)):

        @pl.when(beside)
        def _(i=i):
            wait(rh.at[i], halo_recv.at[3 + i])

        @pl.when(jnp.logical_and(beside, here))
        def _(i=i):
            wait(rd.at[i], halo_recv.at[5 + i])

    pl.semaphore_wait(meet.at[4], 2)
    mine = stem_of(outer, 2, True)
    spread(mine, mine, send.at[16], recv.at[16])

    pl.semaphore_wait(meet.at[0], on_line(1))
    pl.semaphore_wait(meet.at[1], 2)
    line_z(2, functools.partial(tell, 2))
    wait(xall.at[:3, :32], recv.at[2])
    forward(functools.partial(x_half, inner, 3), ring, send.at[9], recv.at[9])
    wait(xall.at[:3, :48], recv.at[12])
    forward(functools.partial(x_half, inner, 3), 1 - ring, send.at[9], recv.at[9])
    pl.semaphore_wait(meet.at[2], on_line(2))
    line_z(4, functools.partial(tell, 5))
    wait(mi_all.at[:192], recv.at[1])
    second_round(mi_all, send.at[10], recv.at[10], False)

    wait(wall.at[0], recv.at[0])
    wait(xall.at[:3, :32], recv.at[9])
    wait(xall.at[:2, :112], recv.at[16])
    tokens = xall[...].reshape(640, 512)
    low = lax.broadcasted_iota(jnp.int32, (1, 128), 1) < 64
    bias_row = eb_ref[pl.ds(k, 1), :]
    bias_rows = [jnp.where(low, 0.0, pltpu.roll(bias_row, 64, axis=1)), jnp.where(low, 0.0, bias_row)]
    lane = lax.broadcasted_iota(jnp.int32, (64, 128), 1)
    sums = [[0.0, 0.0] for _ in range(4)]
    for half in range(2):
        terms = jnp.dot(tokens, wall[half], preferred_element_type=F32)
        both = terms[128:640, 128:256] + terms[0:512, 0:128] + bias_rows[half]
        for column in range(4):
            turned = both[128 * column : 128 * column + 128].T
            shifted = pltpu.roll(turned[0:64], 1, axis=1)
            value = (turned[64:128] + jnp.where(lane > 0, shifted, 0.0)).astype(BF16)
            eh[core, 64 * half : 64 * half + 64, 128 * column : 128 * column + 128] = value
            wide = value.astype(F32)
            sums[column][0] += jnp.sum(wide, axis=0, keepdims=True)
            sums[column][1] += jnp.sum(wide * wide, axis=0, keepdims=True)
    for column in range(4):
        for kind in range(2):
            st[c, kind : kind + 1, 128 * column : 128 * column + 128] = sums[column][kind]

    for r, step in ((1, 2), (0, 2), (1, 1), (1, 3), (0, 1), (0, 3), (1, 0), (0, 0)):
        for which in (other, core):
            if r or step or which is other:
                to = 2 * (4 * (1 - ring if r else ring) + (x + step) % 4) + which
                remote(st.at[c], st.at[c], send.at[4], recv.at[4], (to, s))

    remote(eh.at[core], eh.at[core], send.at[5], recv.at[5], partner)

    wait(mi_all.at[:192], recv.at[10])
    third_round(mi_all, send.at[13], recv.at[13])
    gain = jnp.broadcast_to(gn_ref[pl.ds(k, 1), :], (128, 128)).T
    offset = jnp.broadcast_to(nb_ref[pl.ds(k, 1), :], (128, 128)).T
    gain = jnp.concatenate([gain] * 4, axis=1)
    offset = jnp.concatenate([offset] * 4, axis=1)
    wait(st.at[:15], recv.at[4])
    wait(eh.at[0], recv.at[5])
    first_round(mo_ref, mo_all, send.at[3], recv.at[3])
    normed = []
    for half in range(2):
        total = st[half]
        for j in range(1, CHIPS):
            total = total + st[2 * j + half]
        average = total[0:1] * (1.0 / 1024)
        variance = total[1:2] * (1.0 / 1024) - average * average
        scale = lax.rsqrt(variance + 1e-05)
        value = (eh[half].astype(F32) - average) * scale * gain + offset
        normed.append(value.astype(BF16))
    normed = jnp.concatenate(normed, axis=1)

    own_mi.wait()
    pl.semaphore_wait(meet.at[5], 1)
    halves = (ring, 1 - ring)
    for half in halves:
        if half is not ring:
            wait(mi_all.at[:64], recv.at[13])
        units = pl.ds(pl.multiple_of(256 * half, 256), 256)
        summed = lax.dot_general(normed, mi_all[units], (((1,), (1,)), ((), ())), preferred_element_type=F32)
        summed = summed.astype(BF16)
        for band in range(8):
            hs[half, band] = summed[16 * band : 16 * band + 16]
        for d in (4, 3, 5, 2, 6, 1, 7):
            remote(hs.at[half, (z + d) % 8], rs.at[half, z], rs_send.at[half], rs_recv.at[half], over_z(d))

    for half in halves:
        rs[half, z] = hs[half, z]
        wait(rs.at[half, :7], rs_recv.at[half])
        total = rs[half, 0].astype(F32)
        for source in range(1, 8):
            total = total + rs[half, source].astype(F32)
        quarter[half, part] = total.astype(BF16)
        mine = quarter.at[half, part]
        for d in (2, 1, 3):
            remote(mine, mine, quarter_send.at[half], quarter_recv.at[half], over_parts(d))
        if half is ring:
            wait(mo_all.at[:192], recv.at[3])
            second_round(mo_all, send.at[11], recv.at[11], True)
    rows = mb_ref[...]
    turned = pltpu.roll(rows, 64, axis=1)
    ours = jnp.where(low, jnp.where(core == 0, rows, turned), 0.0)
    theirs = jnp.where(low, 0.0, jnp.where(core == 0, turned, rows))
    hidden_bias = [ours[2 * i : 2 * i + 1] + theirs[2 * i + 1 : 2 * i + 2] for i in range(4)]
    biases = [jnp.concatenate(hidden_bias[2 * i : 2 * i + 2], axis=1) for i in range(2)]
    for half in halves:
        wait(quarter.at[half, :3], quarter_recv.at[half])
        total = quarter[half, 0].astype(F32)
        for source in range(1, 4):
            total = total + quarter[half, source].astype(F32)
        total = total + jnp.where(half == 0, biases[0], biases[1])
        act[half, z] = gelu(total).astype(BF16)
        for d in (4, 3, 5, 2, 6, 1, 7):
            remote(act.at[half, z], act.at[half, z], act_send.at[half], act_recv.at[half], over_z(d))

    wait(mo_all.at[:192], recv.at[11])
    third_round(mo_all, send.at[14], recv.at[14])
    own_mo.wait()

    def rows_of(which, half):
        return act[half, pl.ds(4 * which, 4)].reshape(64, 256)

    def product(which, half):
        units = pl.ds(pl.multiple_of(256 * half, 256), 256)
        return jnp.dot(rows_of(which, half), mo_all[units], preferred_element_type=F32)

    wait(act.at[ring, :7], act_recv.at[ring])
    early = product(other, ring)
    mine = product(core, ring) + ob_ref[...]
    wait(mo_all.at[:64], recv.at[14])
    wait(act.at[1 - ring, :7], act_recv.at[1 - ring])
    last = pl.ds(pl.multiple_of(256 * (1 - ring), 256), 256)
    for half in range(2):
        span = slice(512 * half, 512 * half + 512)
        late = jnp.dot(rows_of(other, 1 - ring), mo_all[last, span], preferred_element_type=F32)
        po[half] = (early[:, span] + late).astype(BF16)
        remote(po.at[half], pr.at[half], send.at[8 + 7 * half], recv.at[8 + 7 * half], partner)
    mine = mine + product(core, 1 - ring)
    residual = [eh[half, pl.ds(pl.multiple_of(64 * core, 64), 64), :].astype(F32) for half in range(2)]
    mine = mine + jnp.concatenate(residual, axis=1)
    for half in range(2):
        wait(pr.at[half], recv.at[8 + 7 * half])
        span = slice(512 * half, 512 * half + 512)
        out_ref[:, span] = (mine[:, span] + pr[half].astype(F32)).astype(BF16)

    wait(gc.at[:, core], halo_send.at[0])
    for to in range(2):
        within = s < SPACE - 1 if to == 0 else s > 0

        @pl.when(vertical)
        def _(to=to):
            wait(rv.at[to], halo_send.at[1 + to])

        @pl.when(within)
        def _(to=to):
            wait(rh.at[to], halo_send.at[3 + to])

        @pl.when(jnp.logical_and(within, vertical))
        def _(to=to):
            wait(rd.at[to], halo_send.at[5 + to])

    wait(wall.at[0], send.at[0])
    wait(mi_all.at[:192], send.at[1])
    wait(xall.at[:3, :80], send.at[2])
    wait(xall.at[:2, :112], send.at[16])
    wait(mo_all.at[:192], send.at[3])
    wait(st.at[:15], send.at[4])
    wait(eh.at[0], send.at[5])
    for half in range(2):
        wait(rs.at[half, :7], rs_send.at[half])
        wait(quarter.at[half, :3], quarter_send.at[half])
        wait(act.at[half, :7], act_send.at[half])
    wait(po.at[0], send.at[8])
    wait(po.at[1], send.at[15])
    wait(xall.at[:3, :32], send.at[9])
    wait(mi_all.at[:192], send.at[10])
    wait(mo_all.at[:192], send.at[11])
    wait(mi_all.at[:64], send.at[13])
    wait(mo_all.at[:64], send.at[14])


def shards(
    fields,
    stem_weight,
    stem_bias,
    embed_weight,
    embed_bias,
    norm_gain,
    norm_bias,
    mix_in,
    mix_in_bias,
    mix_out,
    mix_out_bias,
):
    out = pl.pallas_call(
        kernel,
        out_shape=pltpu.VMEM((64, 1024), BF16),
        in_specs=[pl.BlockSpec(memory_space=pl.ANY)] * 11,
        out_specs=pl.BlockSpec(memory_space=pltpu.VMEM),
        scratch_shapes=[
            pltpu.VMEM((20, 32, 32), BF16),
            pltpu.VMEM((7, 7, 32, 64), BF16),
            pltpu.VMEM((3, 3, 20, 32), BF16),
            pltpu.VMEM((1, 32), F32),
            pltpu.VMEM((8, 128), F32),
            pltpu.VMEM((8, 128), F32),
            pltpu.VMEM((8, 128), F32),
            pltpu.VMEM((8, 128), F32),
            pltpu.VMEM((1, 1024), F32),
            pltpu.VMEM((10, 32, 128), BF16),
            pltpu.VMEM((384, 128), F32),
            pltpu.VMEM((5, 2, 32, 128), BF16),
            pltpu.VMEM((2, 5, 16, 128), BF16),
            pltpu.VMEM((2, 2, 32, 128), BF16),
            pltpu.VMEM((2, 2, 16, 128), BF16),
            pltpu.VMEM((5, 128, 512), BF16),
            pltpu.VMEM((2, 512, 256), BF16),
            pltpu.VMEM((2, 128, 512), BF16),
            pltpu.VMEM((16, 2, 512), F32),
            pltpu.VMEM((512, 1024), BF16),
            pltpu.VMEM((512, 1024), BF16),
            pltpu.VMEM((2, 8, 16, 256), BF16),
            pltpu.VMEM((2, 8, 16, 256), BF16),
            pltpu.VMEM((2, 4, 16, 256), BF16),
            pltpu.VMEM((2, 8, 16, 256), BF16),
            pltpu.VMEM((2, 64, 512), BF16),
            pltpu.VMEM((2, 64, 512), BF16),
            pltpu.SemaphoreType.DMA((7,)),
            pltpu.SemaphoreType.DMA((7,)),
            pltpu.SemaphoreType.DMA((18,)),
            pltpu.SemaphoreType.DMA((18,)),
            *[pltpu.SemaphoreType.DMA((2,))] * 6,
            pltpu.SemaphoreType.DMA((11,)),
            pltpu.SemaphoreType.REGULAR((6,)),
        ],
        compiler_params=pltpu.CompilerParams(collective_id=0, has_side_effects=True, vmem_limit_bytes=58 * 2**20),
    )(
        stem_weight,
        stem_bias[None],
        embed_bias.reshape(8, 128),
        norm_gain.reshape(8, 128),
        norm_bias.reshape(8, 128),
        mix_in_bias.reshape(8, 128),
        mix_out_bias[None],
        embed_weight,
        fields[0],
        mix_in.T,
        mix_out,
    )
    return out[None]


def solution(mesh):
    placed = (
        P(None, None, "chan", "space"),
        P(),
        P(),
        P(None, None, None, "chan"),
        P(),
        P(),
        P(),
        P("space", "chan"),
        P(),
        P("chan", "space"),
        P("space"),
    )
    return jax.shard_map(
        shards, mesh=mesh, in_specs=placed, out_specs=P(None, "chan", "space"), check_vma=False
    )
```
